32 devices in a mesh: groups: 2 (over y), ctx: 4 (over z), fsdp: 2 (over x), dp: 2 (over core).
Axes of the slice: x: 2, y: 2, z: 4, core: 2. Of those that a mesh axis runs over, the one named last changes fastest.
Arguments:
- query_in: bfloat16 [8, 512, 1024], P(('groups', 'fsdp', 'dp'), 'ctx'), parts along dimension 0, may hold values from -11 to 11
- key_in: bfloat16 [8, 512, 1024], P(('groups', 'fsdp', 'dp'), 'ctx'), parts along dimension 0, may hold values from -11 to 11
- value_in: bfloat16 [8, 512, 1024], P(('groups', 'fsdp', 'dp'), 'ctx'), parts along dimension 0, may hold values from -6 to 6
- utt_lengths: int32 [8], P(('groups', 'fsdp', 'dp')), parts along dimension 0, may hold values from 128 to 512, as said below
- frames_in: bfloat16 [8, 512, 1536], P(('groups', 'fsdp', 'dp'), 'ctx'), parts along dimension 0, may hold values from -6 to 6
- out_weight: bfloat16 [1024, 1536], P(None, 'fsdp'), may hold values from -1.5 to 1.5
- conv_kernel: float32 [31, 1536], P(None, 'fsdp'), may hold values from -1 to 1
- conv_bias: float32 [1536], P('fsdp'), may hold values from -3 to 3
- ln_gain: float32 [1536], P('fsdp'), may hold values from 0.1 to 1.9
- cotangent: bfloat16 [8, 512, 1536], P(('groups', 'fsdp', 'dp'), 'ctx'), parts along dimension 0, may hold values from -6 to 6
Outputs:
- block_out: bfloat16 [8, 512, 1536], P(('groups', 'fsdp', 'dp'), 'ctx'), parts along dimension 0
- hidden_grad: bfloat16 [8, 512, 1536], P(('groups', 'fsdp', 'dp'), 'ctx'), parts along dimension 0
- grad_kernel: float32 [62, 1536], P('groups', 'fsdp'), parts along dimension 0
- grad_bias: float32 [3072], P(('groups', 'fsdp')), parts along dimension 0
- grad_gain: float32 [3072], P(('groups', 'fsdp')), parts along dimension 0
The draws below stay inside these ranges and needn't reach their ends.
There are 2 independent parts, one for each index of `groups`. The reference program is written for one: setup_inputs(seed, part) draws one part's arguments, and reference() takes and returns one part's arrays. A program takes and returns all parts, laid end to end along the dimension named above; an argument that names none is the same for every part. Nothing has to cross between parts.
Inputs may be any that keep to these rules, and one draw needn't show every extreme that they name: `utt_lengths`: in every group one utterance is full, of 512 valid frames.
All inputs are finite; a program needn't handle non-finite values.
Results may differ from the reference program's by a relative error of at most 0.019.
Values may be sent and summed in bfloat16 or wider, within the bound.
No kernel may reach another device: no remote copies, remote signals or barrier semaphores. Data moves between devices by JAX's collectives and lax.ppermute only.
A program may use at most 64 MiB of HBM per device.

```python
import math
import jax
import jax.numpy as jnp
from jax import lax

D = 1536
HEADS = 16
HD = 64
TAPS = 31
HW = 1024
FRAMES = 512
UTTS = 4


def paired_draw(base_key):
    folded = jax.random.fold_in(base_key, 4177)
    key_one, key_two = jax.random.split(folded, 2)
    full_shape = (UTTS, FRAMES, HEADS, HD)
    query_vals = jnp.clip(jax.random.normal(key_one, full_shape, jnp.float32), -4.0, 4.0)
    key_vals = jnp.clip(jax.random.normal(key_two, full_shape, jnp.float32), -4.0, 4.0)
    query_vals = query_vals.reshape(UTTS, FRAMES, HEADS * HD).astype(jnp.bfloat16)
    key_vals = key_vals.reshape(UTTS, FRAMES, HEADS * HD).astype(jnp.bfloat16)
    return (query_vals, key_vals)


def draw_query_in(key, part):
    return paired_draw(key)[0]


def draw_key_in(key, part):
    return paired_draw(key)[1]


def draw_utt_lengths(key, part):
    key_one, key_two = jax.random.split(jax.random.fold_in(key, 31))
    counts_drawn = jax.random.randint(key_one, (UTTS,), FRAMES // 4, FRAMES + 1)
    full_index = jax.random.randint(key_two, (), 0, UTTS)
    return jnp.where(jnp.arange(UTTS) == full_index, FRAMES, counts_drawn).astype(jnp.int32)


def strengthened(result, rng, source, target, parts, factor):
    def block_of(dim):
        return (jnp.arange(result.shape[dim]) // (result.shape[dim] // parts)).reshape((-1,) + (1,) * (result.ndim - 1 - dim))

    one_side = jax.random.permutation(rng, parts)[block_of(target)]
    other_side = (block_of(target) + parts // 2) % parts
    return jnp.where((block_of(source) == one_side) | (block_of(source) == other_side), factor * result, result)


def block_scale(stream_key, dims, cuts, smallest, high):
    level = 1.0
    for axis_at, blocks in cuts:
        steps = jax.random.uniform(jax.random.fold_in(jax.random.fold_in(stream_key, 6), axis_at), (blocks,), jnp.float32, smallest / len(cuts), high / len(cuts))
        level = level * jnp.repeat(jnp.exp(steps), dims[axis_at] // blocks).reshape((-1,) + (1,) * (len(dims) - 1 - axis_at))
    return level


def normal_values(stream_key, shape, spread, limit, shards=(), dtype=jnp.bfloat16):
    entries = jax.random.normal(stream_key, shape, jnp.float32) * spread
    if len(shards) > 0:
        entries = block_scale(stream_key, shape, shards, -0.22, 0.18) * entries
    return jnp.clip(entries, min=-limit, max=limit).astype(dtype)


def heavy_noise(stream_key, extent, deviation, limit, cuts, heavy, kind=jnp.bfloat16):
    array = deviation * jax.random.normal(stream_key, extent, jnp.float32)
    if cuts:
        array = array * block_scale(stream_key, extent, cuts, -0.22, 0.18)
    return jnp.clip(strengthened(array, jax.random.fold_in(stream_key, 3), *heavy), -limit, limit).astype(kind)


def setup_inputs(seed: int = 0, part: int = 0) -> dict:
    streams_of = jax.random.split(jax.random.key(seed), 11)
    part_splits = jax.random.split(jax.random.fold_in(streams_of[10], part), 11)
    return {
        "query_in": draw_query_in(jax.random.fold_in(jax.random.fold_in(streams_of[10], part), 71), part),
        "key_in": draw_key_in(jax.random.fold_in(jax.random.fold_in(streams_of[10], part), 71), part),
        "value_in": normal_values(part_splits[2], (UTTS, FRAMES, HW), 1.0, 6.0, ((0, 4), (1, 4))),
        "utt_lengths": draw_utt_lengths(jax.random.fold_in(jax.random.fold_in(streams_of[10], part), 71), part),
        "frames_in": normal_values(part_splits[4], (UTTS, FRAMES, D), 1.0, 6.0, ((0, 4), (1, 4))),
        "out_weight": normal_values(streams_of[5], (HW, D), (HW // 64) ** -0.5, 1.5, ((1, 2),)),
        "conv_kernel": normal_values(streams_of[6], (TAPS, D), TAPS ** -0.5, 1.0, ((1, 2),), jnp.float32),
        "conv_bias": normal_values(streams_of[7], (D,), 0.5, 3.0, ((0, 2),), jnp.float32),
        "ln_gain": jnp.clip(1.0 + 0.18 * jax.random.normal(streams_of[8], (D,), jnp.float32), 0.1, 1.9),
        "cotangent": heavy_noise(part_splits[9], (UTTS, FRAMES, D), 1.0, 6.0, ((0, 4), (1, 4)), (0, 2, 4, 2.0)),
    }


NEG_FILL = -1e+30

def attend_full(query_rows, key_rows, value_rows, valid_len):
    frame_count = query_rows.shape[0]
    head_count = query_rows.shape[1] // HD
    query_heads = query_rows.reshape(frame_count, head_count, HD)
    key_heads = key_rows.reshape(frame_count, head_count, HD)
    value_heads = value_rows.reshape(frame_count, head_count, HD)
    usable = jnp.arange(frame_count) < valid_len
    block_len = math.gcd(frame_count, 512)
    blocks = query_heads.reshape(frame_count // block_len, block_len, head_count, HD)

    def one_block(query_block):
        scores = jnp.einsum('qhd,khd->qhk', query_block, key_heads, preferred_element_type=jnp.float32) * (1.0 / math.sqrt(HD))
        scores = jnp.where(usable, scores, NEG_FILL)
        row_max = lax.optimization_barrier(jnp.max(scores, axis=-1, keepdims=True))
        weights = jnp.where(usable, jnp.exp(scores - row_max), 0.0)
        totals = lax.optimization_barrier(jnp.sum(weights, axis=-1))
        summed = jnp.einsum('qhk,khd->qhd', weights.astype(jnp.bfloat16), value_heads, preferred_element_type=jnp.float32)
        return (summed / totals[..., None]).astype(jnp.bfloat16)
    return lax.map(one_block, blocks).reshape(frame_count, head_count * HD)

def normalize(block):
    as_float = block.astype(jnp.float32)
    average = lax.optimization_barrier(jnp.mean(as_float, axis=-1, keepdims=True))
    centered = as_float - average
    variance = lax.optimization_barrier(jnp.mean(centered * centered, axis=-1, keepdims=True))
    inv_scale = lax.rsqrt(variance + 1e-05)
    return (centered * inv_scale, inv_scale)

def reference(query_in, key_in, value_in, utt_lengths, frames_in, out_weight, conv_kernel, conv_bias, ln_gain, cotangent):
    half_taps = TAPS // 2

    def per_utt(bundle):
        return attend_full(bundle[0], bundle[1], bundle[2], bundle[3])
    attended = lax.map(per_utt, (query_in, key_in, value_in, utt_lengths))
    projected = jnp.dot(attended.reshape(UTTS * FRAMES, HW), out_weight, preferred_element_type=jnp.float32).reshape(UTTS, FRAMES, D)
    hidden = (frames_in.astype(jnp.float32) + projected).astype(jnp.bfloat16)
    live_mask = (jnp.arange(FRAMES)[None, :] < utt_lengths[:, None]).astype(jnp.float32)[..., None]
    normed, inv_scale = normalize(hidden)
    conv_in = live_mask * normed * ln_gain
    padded = jnp.pad(conv_in, ((0, 0), (half_taps, half_taps), (0, 0)))
    pre_act = conv_bias + jnp.zeros_like(conv_in)
    for tap_index in range(TAPS):
        pre_act = pre_act + conv_kernel[tap_index] * padded[:, tap_index:tap_index + FRAMES]
    gate_val = jax.nn.sigmoid(pre_act)
    block_out = (hidden.astype(jnp.float32) + live_mask * pre_act * gate_val).astype(jnp.bfloat16)
    grad_in = cotangent.astype(jnp.float32)
    grad_pre = grad_in * live_mask * gate_val * (1.0 + pre_act * (1.0 - gate_val))
    grad_padded = jnp.pad(grad_pre, ((0, 0), (half_taps, half_taps), (0, 0)))
    grad_conv = jnp.zeros_like(conv_in)
    kernel_rows = []
    for tap_index in range(TAPS):
        back = 2 * half_taps - tap_index
        grad_conv = grad_conv + conv_kernel[tap_index] * grad_padded[:, back:back + FRAMES]
        kernel_rows.append(lax.optimization_barrier(jnp.sum(grad_pre * padded[:, tap_index:tap_index + FRAMES], axis=(0, 1))))
    grad_conv = live_mask * grad_conv
    grad_hat = grad_conv * ln_gain
    first_mean = lax.optimization_barrier(jnp.mean(grad_hat, axis=-1, keepdims=True))
    second_mean = lax.optimization_barrier(jnp.mean(grad_hat * normed, axis=-1, keepdims=True))
    hidden_grad = (grad_in + (grad_hat - first_mean - normed * second_mean) * inv_scale).astype(jnp.bfloat16)
    factor = 1.0 / math.sqrt(UTTS * FRAMES)
    grad_kernel = jnp.stack(kernel_rows) * factor
    grad_bias = lax.optimization_barrier(jnp.sum(grad_pre, axis=(0, 1))) * factor
    grad_gain = lax.optimization_barrier(jnp.sum(grad_conv * normed, axis=(0, 1))) * factor
    return (block_out, hidden_grad, grad_kernel, grad_bias, grad_gain)
```

```python
import functools
import math

import jax
import jax.numpy as jnp
from jax import lax
from jax.experimental import pallas as pl
from jax.experimental.pallas import tpu as pltpu
from jax.sharding import PartitionSpec as P

HD = 64
TAPS = 31
HALF = TAPS // 2
LANES = 128
WIDE = 32
NEAR = 16
PARAM_ROWS = 40

NEG_FILL = -1e30


def extended(block, sides, width):
    for axis, dim in sides:
        count = lax.axis_size(axis)
        forward = [(i, i + 1) for i in range(count - 1)]
        backward = [(target, source) for source, target in forward]
        low = lax.ppermute(
            lax.slice_in_dim(block, block.shape[dim] - width, None, axis=dim), axis, forward
        )
        high = lax.ppermute(lax.slice_in_dim(block, 0, width, axis=dim), axis, backward)
        block = jnp.concatenate([low, block, high], axis=dim)
    return block


def absorb_block(state, query_heads, key_heads, value_heads, key_start, valid_len):
    run_max, run_sum, summed = state
    scores = jnp.einsum(
        "qhd,khd->qhk", query_heads, key_heads, preferred_element_type=jnp.float32
    ) * (1.0 / math.sqrt(HD))
    usable = key_start + jnp.arange(key_heads.shape[0]) < valid_len
    scores = jnp.where(usable, scores, NEG_FILL)
    new_max = jnp.maximum(run_max, jnp.max(scores, axis=-1))
    rescale = jnp.exp(run_max - new_max)
    weights = jnp.where(usable, jnp.exp(scores - new_max[..., None]), 0.0)
    run_sum = run_sum * rescale + jnp.sum(weights, axis=-1)
    summed = summed * rescale[..., None] + jnp.einsum(
        "qhk,khd->qhd",
        weights.astype(jnp.bfloat16),
        value_heads,
        preferred_element_type=jnp.float32,
    )
    return (new_max, run_sum, summed)


def normalize(block):
    as_float = block.astype(jnp.float32)
    average = jnp.mean(as_float, axis=-1, keepdims=True)
    centered = as_float - average
    variance = jnp.mean(centered * centered, axis=-1, keepdims=True)
    inv_scale = lax.rsqrt(variance + 1e-05)
    return (centered * inv_scale, inv_scale)


def convolve(conv_in, kernel_all, bias_all, out_rows):
    pre_act = bias_all + jnp.zeros((out_rows, conv_in.shape[1]), jnp.float32)
    for tap_index in range(TAPS):
        pre_act = pre_act + kernel_all[tap_index] * conv_in[tap_index : tap_index + out_rows]
    return pre_act


def live_of(positions, valid_len):
    return ((positions >= 0) & (positions < valid_len)).astype(jnp.float32)[:, None]


def general_shards(
    query_in,
    key_in,
    value_in,
    utt_lengths,
    frames_in,
    out_weight,
    conv_kernel,
    conv_bias,
    ln_gain,
    cotangent,
):
    row_count = query_in.shape[1]
    feat_width = query_in.shape[2]
    head_count = feat_width // HD
    valid_len = utt_lengths[0]
    ctx_count = lax.axis_size("ctx")
    row_offset = lax.axis_index("ctx") * row_count
    half_taps = TAPS // 2
    query_heads = query_in[0].reshape(row_count, head_count, HD)
    start_state = (
        jnp.full((row_count, head_count), NEG_FILL, jnp.float32),
        jnp.zeros((row_count, head_count), jnp.float32),
        jnp.zeros((row_count, head_count, HD), jnp.float32),
    )
    state = start_state
    first_row = jnp.int32(0)
    key_part = lax.all_gather(key_in, "ctx", axis=1, tiled=True)
    value_part = lax.all_gather(value_in, "ctx", axis=1, tiled=True)
    piece_rows = key_part.shape[1]
    block_len = math.gcd(piece_rows, 512)
    for block_start in range(0, piece_rows, block_len):
        key_heads = key_part[0, block_start : block_start + block_len].reshape(
            block_len, head_count, HD
        )
        value_heads = value_part[0, block_start : block_start + block_len].reshape(
            block_len, head_count, HD
        )
        state = absorb_block(
            state, query_heads, key_heads, value_heads, first_row + block_start, valid_len
        )
    run_max, run_sum, summed = state
    attended = (summed / run_sum[..., None]).reshape(row_count, feat_width).astype(jnp.bfloat16)
    projected = jnp.dot(
        attended,
        lax.all_gather(out_weight, "fsdp", axis=1, tiled=True),
        preferred_element_type=jnp.float32,
    )
    hidden = (frames_in[0].astype(jnp.float32) + projected).astype(jnp.bfloat16)
    kernel_all, bias_all, gain_all = (
        lax.all_gather(conv_kernel, "fsdp", axis=1, tiled=True),
        lax.all_gather(conv_bias, "fsdp", axis=0, tiled=True),
        lax.all_gather(ln_gain, "fsdp", axis=0, tiled=True),
    )
    grad_in = cotangent[0].astype(jnp.float32)
    live_mask = live_of(row_offset + jnp.arange(row_count), valid_len)
    widened = extended(hidden, (("ctx", 0),), half_taps)
    normed_ext, inv_ext = normalize(widened)
    conv_in = (
        live_of(row_offset - half_taps + jnp.arange(row_count + 2 * half_taps), valid_len)
        * normed_ext
        * gain_all
    )
    pre_act = convolve(conv_in, kernel_all, bias_all, row_count)
    gate_val = jax.nn.sigmoid(pre_act)
    grad_pre = grad_in * live_mask * gate_val * (1.0 + pre_act * (1.0 - gate_val))
    grad_wide = extended(grad_pre.astype(jnp.bfloat16), (("ctx", 0),), half_taps).astype(
        grad_pre.dtype
    )
    normed = normed_ext[half_taps : half_taps + row_count]
    inv_scale = inv_ext[half_taps : half_taps + row_count]
    block_out = (hidden.astype(jnp.float32) + live_mask * pre_act * gate_val).astype(jnp.bfloat16)
    grad_conv = jnp.zeros((row_count, grad_pre.shape[1]), jnp.float32)
    kernel_rows = []
    for tap_index in range(TAPS):
        back = 2 * half_taps - tap_index
        grad_conv = grad_conv + kernel_all[tap_index] * grad_wide[back : back + row_count]
        kernel_rows.append(jnp.sum(grad_pre * conv_in[tap_index : tap_index + row_count], axis=0))
    grad_conv = live_mask * grad_conv
    grad_hat = grad_conv * gain_all
    first_mean = jnp.mean(grad_hat, axis=-1, keepdims=True)
    second_mean = jnp.mean(grad_hat * normed, axis=-1, keepdims=True)
    hidden_grad = (grad_in + (grad_hat - first_mean - normed * second_mean) * inv_scale).astype(
        jnp.bfloat16
    )
    factor = 1.0 / math.sqrt(lax.axis_size("fsdp") * lax.axis_size("dp") * row_count * ctx_count)
    kernel_term = jnp.stack(kernel_rows) * factor
    bias_term = (jnp.sum(grad_pre, axis=0) * factor)[None]
    gain_term = (jnp.sum(grad_conv * normed, axis=0) * factor)[None]
    shares = (
        lax.psum_scatter(
            kernel_term.astype(jnp.bfloat16), "fsdp", scatter_dimension=1, tiled=True
        ).astype(jnp.float32),
        lax.psum_scatter(
            bias_term.astype(jnp.bfloat16), "fsdp", scatter_dimension=1, tiled=True
        ).astype(jnp.float32),
        lax.psum_scatter(
            gain_term.astype(jnp.bfloat16), "fsdp", scatter_dimension=1, tiled=True
        ).astype(jnp.float32),
    )
    totals = lax.psum((shares[0], shares[1], shares[2]), ("ctx", "dp"))
    return (block_out[None], hidden_grad[None], totals[0], totals[1][0], totals[2][0])


def fits_fast(mesh, blocks):
    query_in, frames_in, out_weight = blocks[0], blocks[4], blocks[5]
    ctx_count = mesh.shape["ctx"]
    rows, width = query_in.shape[1], query_in.shape[2]
    return (
        query_in.shape[0] == 1
        and mesh.shape["fsdp"] == 2
        and mesh.shape["dp"] == 2
        and ctx_count > 1
        and width % (ctx_count * LANES) == 0
        and rows % LANES == 0
        and frames_in.shape[2] == 2 * out_weight.shape[1]
        and out_weight.shape[1] % LANES == 0
        and (ctx_count * rows) <= 1024
    )


def cyclic(count, step):
    return [(i, (i + step) % count) for i in range(count)]


def attend_kernel(count, rows, info_ref, *refs):
    parts, outs = refs[:count], refs[count : 2 * count]
    query_all, key_all, value_all, attended = refs[2 * count :]
    place, valid_len = info_ref[0], info_ref[3]
    frames, width = query_all.shape
    for step in range(count):
        owner = lax.rem(place + count - step, count)
        span = pl.ds(pl.multiple_of(owner * rows, rows), rows)
        query_all[span, :] = parts[step][0]
        key_all[span, :] = parts[step][1]
        value_all[span, :] = parts[step][2]
    attended[0:WIDE, :] = jnp.zeros((WIDE, width), attended.dtype)
    attended[WIDE + frames : 2 * WIDE + frames, :] = jnp.zeros((WIDE, width), attended.dtype)
    usable = lax.broadcasted_iota(jnp.int32, (1, frames), 1) < valid_len
    lane = lax.broadcasted_iota(jnp.int32, (1, LANES), 1)
    for pair in range(width // LANES):
        cols = slice(pair * LANES, (pair + 1) * LANES)
        keys, values = key_all[:, cols], value_all[:, cols]
        own = [
            (jnp.where(mine, keys, 0).astype(keys.dtype), jnp.where(mine, values, 0).astype(values.dtype))
            for mine in (lane < HD, lane >= HD)
        ]
        for start in range(0, frames, rows):
            queries = query_all[start : start + rows, cols]
            total = jnp.zeros((rows, LANES), jnp.float32)
            for key_head, value_head in own:
                scores = lax.dot_general(
                    queries, key_head, (((1,), (1,)), ((), ())), preferred_element_type=jnp.float32
                ) * (1.0 / math.sqrt(HD))
                scores = jnp.where(usable, scores, NEG_FILL)
                weights = jnp.exp(scores - jnp.max(scores, axis=1, keepdims=True))
                sums = jnp.sum(weights, axis=1, keepdims=True)
                total += (
                    jnp.dot(
                        weights.astype(jnp.bfloat16), value_head, preferred_element_type=jnp.float32
                    )
                    / sums
                )
            attended[WIDE + start : WIDE + start + rows, cols] = total.astype(attended.dtype)
    for step in range(count):
        owner = lax.rem(place + count - step, count)
        outs[step][...] = attended[pl.ds(pl.multiple_of(owner * rows, rows), rows + 2 * WIDE), :]


def by_residue(first, last):
    return [[o for o in range(first, last + 1) if o % 8 == r] for r in range(8)]


def module_kernel(count, *refs):
    info_ref, *replies = refs[: 1 + count]
    (
        frames_ref, cotan_ref, below_ref, above_ref, w_own, w_near, w_far, par_own, par_other,
        block_out, hidden_grad, sums_own, sums_other,
        attended, params, normed, wide_grad, grad_hat, sums, partial, mean_one, mean_two,
    ) = refs[1 + count :]
    place, side, core, valid_len = info_ref[0], info_ref[1], info_ref[2], info_ref[3]
    rows, features = frames_ref.shape
    half = features // 2
    tiles, half_tiles = features // LANES, half // LANES
    ext, near = rows + 2 * WIDE, rows + 2 * NEAR
    depth = replies[0].shape[1]
    per_part = w_near.shape[0] // depth

    def live(first, length):
        position = place * rows + first + lax.broadcasted_iota(jnp.int32, (length, 1), 0)
        return ((position >= 0) & (position < valid_len)).astype(jnp.float32)

    for step in range(count):
        attended[lax.rem(place + step, count)] = replies[step][...]
    for tile in range(half_tiles):
        cols = slice(tile * LANES, (tile + 1) * LANES)
        for source, base in ((par_own, side * half_tiles), (par_other, (1 - side) * half_tiles)):
            values = source[:, cols]
            gain = values[TAPS + 1 : TAPS + 2]
            row = lax.broadcasted_iota(jnp.int32, (PARAM_ROWS, 1), 0)
            params[base + tile] = jnp.where(row < TAPS, values * gain, values)

    for tile in range(half_tiles):
        cols = slice(tile * LANES, (tile + 1) * LANES)
        for mine in (True, False):
            at = (side if mine else 1 - side) * half_tiles + tile
            span = pl.ds(pl.multiple_of(at * LANES, LANES), LANES)
            product = jnp.zeros((ext, LANES), jnp.float32)
            for part in range(count):
                if mine:
                    index, weight = part, w_own[part * depth : (part + 1) * depth, cols]
                else:
                    inner = part % per_part
                    source = w_near if part < per_part else w_far
                    index = (core if part < per_part else 1 - core) * per_part + inner
                    weight = source[inner * depth : (inner + 1) * depth, cols]
                product += jnp.dot(attended[index], weight, preferred_element_type=jnp.float32)
            residual = jnp.concatenate(
                [below_ref[0:WIDE, span], frames_ref[:, span], above_ref[0:WIDE, span]], axis=0
            )
            hidden = (residual.astype(jnp.float32) + product).astype(jnp.bfloat16)
            block_out[:, span] = hidden[WIDE : WIDE + rows]
            normed[at, 0:ext] = hidden.astype(jnp.float32)

    total = normed[0, 0:ext]
    for tile in range(1, tiles):
        total += normed[tile, 0:ext]
    average = jnp.sum(total, axis=1, keepdims=True) * (1.0 / features)
    total = jnp.zeros((ext, LANES), jnp.float32)
    for tile in range(tiles):
        centered = normed[tile, 0:ext] - average
        total += centered * centered
    variance = jnp.sum(total, axis=1, keepdims=True) * (1.0 / features)
    inv_scale = lax.rsqrt(variance + 1e-05)
    scale = inv_scale * live(-WIDE, ext)
    for tile in range(tiles):
        normed[tile, 0:ext] = (normed[tile, 0:ext] - average) * scale

    live_near = live(-NEAR, near)
    live_rows = live(0, rows)
    mean_one[...] = jnp.zeros_like(mean_one)
    mean_two[...] = jnp.zeros_like(mean_two)

    def one_tile(tile, carry):
        span = pl.ds(pl.multiple_of(tile * LANES, LANES), LANES)
        pre_act = jnp.broadcast_to(params[tile, TAPS : TAPS + 1], (near, LANES))
        for rest, offsets in enumerate(by_residue(1, TAPS)):
            shifted = normed[tile, rest : rest + near + 24]
            for offset in offsets:
                at = offset - rest
                pre_act += params[tile, offset - 1 : offset] * shifted[at : at + near]
        gate = jax.nn.sigmoid(pre_act)
        here = slice(NEAR, NEAR + rows)
        block_out[:, span] = (
            block_out[:, span].astype(jnp.float32) + live_rows * (pre_act * gate)[here]
        ).astype(block_out.dtype)
        cotan = jnp.concatenate(
            [below_ref[WIDE:, span], cotan_ref[:, span], above_ref[WIDE:, span]], axis=0
        ).astype(jnp.float32)
        grad_pre = cotan * live_near * gate * (1.0 + pre_act * (1.0 - gate))
        wide_grad[0:near] = grad_pre
        own_grad = grad_pre[here]
        first = WIDE - HALF
        for rest, offsets in enumerate(by_residue(first, first + TAPS - 1)):
            low = offsets[0]
            shifted = normed[tile, low : low + rows + 24]
            for offset in offsets:
                at = offset - low
                partial[offset - first] = jnp.sum(
                    (own_grad * shifted[at : at + rows]).reshape(rows // 8, 8, LANES), axis=0
                )
        partial[TAPS] = jnp.sum(own_grad.reshape(rows // 8, 8, LANES), axis=0)
        sums[tile] = jnp.sum(partial[...], axis=1)
        grad = jnp.zeros((rows, LANES), jnp.float32)
        for rest, offsets in enumerate(by_residue(1, TAPS)):
            shifted = wide_grad[rest : rest + rows + 24]
            for offset in offsets:
                at = offset - rest
                tap = TAPS - offset
                grad += params[tile, tap : tap + 1] * shifted[at : at + rows]
        grad = live_rows * grad
        grad_hat[tile] = grad
        mean_one[...] += grad
        mean_two[...] += grad * normed[tile, WIDE : WIDE + rows]
        return carry

    lax.fori_loop(0, tiles, one_tile, 0)
    first_mean = jnp.sum(mean_one[...], axis=1, keepdims=True) * (1.0 / features)
    second_mean = jnp.sum(mean_two[...], axis=1, keepdims=True) * (1.0 / features)
    inv_rows = inv_scale[WIDE : WIDE + rows]
    for tile in range(tiles):
        cols = slice(tile * LANES, (tile + 1) * LANES)
        inner = grad_hat[tile] - first_mean - normed[tile, WIDE : WIDE + rows] * second_mean
        hidden_grad[:, cols] = (
            cotan_ref[:, cols].astype(jnp.float32) + inner * inv_rows
        ).astype(hidden_grad.dtype)
    for tile in range(half_tiles):
        cols = slice(tile * LANES, (tile + 1) * LANES)
        sums_own[:, cols] = sums[side * half_tiles + tile]
        sums_other[:, cols] = sums[(1 - side) * half_tiles + tile].astype(sums_other.dtype)


def fast_shards(
    query_in,
    key_in,
    value_in,
    utt_lengths,
    frames_in,
    out_weight,
    conv_kernel,
    conv_bias,
    ln_gain,
    cotangent,
):
    count = lax.axis_size("ctx")
    rows, width = query_in.shape[1], query_in.shape[2]
    features, half = frames_in.shape[2], out_weight.shape[1]
    place, side, core = lax.axis_index("ctx"), lax.axis_index("fsdp"), lax.axis_index("dp")
    info = jnp.stack([place, side, core, utt_lengths[0]]).astype(jnp.int32)
    share = width // count
    vmem = pl.BlockSpec(memory_space=pltpu.VMEM)
    smem = pl.BlockSpec(memory_space=pltpu.SMEM)
    swap = [(0, 1), (1, 0)]

    stacked = jnp.concatenate([query_in, key_in, value_in], axis=0)
    pieces = [
        lax.dynamic_slice_in_dim(stacked, lax.rem(place + step, count) * share, share, axis=2)
        for step in range(count)
    ]
    out_weight_later, conv_kernel_later, _ = lax.optimization_barrier(
        (out_weight, conv_kernel, pieces)
    )
    parts = [
        piece if step == 0 else lax.ppermute(piece, "ctx", cyclic(count, step))
        for step, piece in enumerate(pieces)
    ]

    depth = width // 2
    w_near = lax.ppermute(
        lax.dynamic_slice_in_dim(out_weight_later, core * depth, depth, axis=0), "fsdp", swap
    )
    par_own = jnp.concatenate(
        [
            conv_kernel_later,
            conv_bias[None],
            ln_gain[None],
            jnp.zeros((PARAM_ROWS - TAPS - 2, half), jnp.float32),
        ],
        axis=0,
    )
    par_other = lax.ppermute(par_own, "fsdp", swap)
    parts, w_near, frames_later, cotangent_later = lax.optimization_barrier(
        (parts, w_near, frames_in, cotangent)
    )
    w_far = lax.ppermute(w_near, "dp", swap)

    frames, cotan = frames_in[0], cotangent[0]
    upward = jnp.concatenate(
        [frames_later[0, rows - WIDE :], cotangent_later[0, rows - NEAR :]], axis=0
    )
    downward = jnp.concatenate([frames_later[0, :WIDE], cotangent_later[0, :NEAR]], axis=0)
    below = lax.ppermute(upward, "ctx", [(i, i + 1) for i in range(count - 1)])
    above = lax.ppermute(downward, "ctx", [(i + 1, i) for i in range(count - 1)])

    replies = pl.pallas_call(
        functools.partial(attend_kernel, count, rows),
        name="attend",
        out_shape=[jax.ShapeDtypeStruct((rows + 2 * WIDE, share), jnp.bfloat16)] * count,
        in_specs=[smem] + [vmem] * count,
        out_specs=[vmem] * count,
        scratch_shapes=[pltpu.VMEM((count * rows, share), jnp.bfloat16)] * 3
        + [pltpu.VMEM((count * rows + 2 * WIDE, share), jnp.bfloat16)],
        compiler_params=pltpu.CompilerParams(vmem_limit_bytes=40 << 20),
        cost_estimate=pl.CostEstimate(
            flops=4 * share * (count * rows) ** 2,
            bytes_accessed=2 * 4 * count * rows * share,
            transcendentals=(share // HD) * (count * rows) ** 2,
        ),
    )(info, *parts)
    replies = [
        reply if step == 0 else lax.ppermute(reply, "ctx", cyclic(count, -step))
        for step, reply in enumerate(replies)
    ]

    ext, near = rows + 2 * WIDE, rows + 2 * NEAR
    tiles = features // LANES
    block_out, hidden_grad, sums_own, sums_other = pl.pallas_call(
        functools.partial(module_kernel, count),
        name="conv_module",
        out_shape=[
            jax.ShapeDtypeStruct((rows, features), jnp.bfloat16),
            jax.ShapeDtypeStruct((rows, features), jnp.bfloat16),
            jax.ShapeDtypeStruct((TAPS + 1, half), jnp.float32),
            jax.ShapeDtypeStruct((TAPS + 1, half), jnp.bfloat16),
        ],
        in_specs=[smem] + [vmem] * (count + 9),
        out_specs=[vmem] * 4,
        scratch_shapes=[
            pltpu.VMEM((count, ext, share), jnp.bfloat16),
            pltpu.VMEM((tiles, PARAM_ROWS, LANES), jnp.float32),
            pltpu.VMEM((tiles, ext + 8, LANES), jnp.float32),
            pltpu.VMEM((near + 8, LANES), jnp.float32),
            pltpu.VMEM((tiles, rows, LANES), jnp.float32),
            pltpu.VMEM((tiles, TAPS + 1, LANES), jnp.float32),
            pltpu.VMEM((TAPS + 1, 8, LANES), jnp.float32),
            pltpu.VMEM((rows, LANES), jnp.float32),
            pltpu.VMEM((rows, LANES), jnp.float32),
        ],
        compiler_params=pltpu.CompilerParams(vmem_limit_bytes=40 << 20),
        cost_estimate=pl.CostEstimate(
            flops=2 * ext * width * features + 6 * TAPS * rows * features,
            bytes_accessed=2 * width * features + 12 * rows * features,
            transcendentals=near * features,
        ),
    )(info, *replies, frames, cotan, below, above, out_weight, w_near, w_far, par_own, par_other)

    found = sums_own + lax.ppermute(sums_other, "fsdp", swap).astype(jnp.float32)
    found = found + lax.ppermute(found, "dp", swap)
    found = found.astype(jnp.bfloat16)
    arrived = [found] + [lax.ppermute(found, "ctx", cyclic(count, step)) for step in range(1, count)]
    found = sum(
        lax.select_n(lax.rem(place + count - block, count), *arrived).astype(jnp.float32)
        for block in range(count)
    )
    factor = 1.0 / math.sqrt(lax.axis_size("fsdp") * lax.axis_size("dp") * rows * count)
    found = found * factor
    grad_kernel = found[:TAPS] * ln_gain
    grad_gain = jnp.sum(found[:TAPS] * conv_kernel, axis=0)
    return (block_out[None], hidden_grad[None], grad_kernel, found[TAPS], grad_gain)


def solution(mesh):
    in_specs = (
        P(("groups", "fsdp", "dp"), "ctx", None),
        P(("groups", "fsdp", "dp"), "ctx", None),
        P(("groups", "fsdp", "dp"), "ctx", None),
        P(("groups", "fsdp", "dp")),
        P(("groups", "fsdp", "dp"), "ctx", None),
        P(None, "fsdp"),
        P(None, "fsdp"),
        P("fsdp"),
        P("fsdp"),
        P(("groups", "fsdp", "dp"), "ctx", None),
    )
    out_specs = (
        P(("groups", "fsdp", "dp"), "ctx", None),
        P(("groups", "fsdp", "dp"), "ctx", None),
        P("groups", "fsdp"),
        P(("groups", "fsdp")),
        P(("groups", "fsdp")),
    )

    def shards(*blocks):
        run = fast_shards if fits_fast(mesh, blocks) else general_shards
        return run(*blocks)

    return jax.shard_map(shards, mesh=mesh, in_specs=in_specs, out_specs=out_specs, check_vma=False)
```

```python
import functools
import math

import jax
import jax.numpy as jnp
from jax import lax
from jax.experimental import pallas as pl
from jax.experimental.pallas import tpu as pltpu
from jax.sharding import PartitionSpec as P

HD = 64
TAPS = 31
HALF = TAPS // 2
LANES = 128
WIDE = 32
NEAR = 16
PARAM_ROWS = 40
SHARE = 256
QUERY_ROWS = 128
CHUNKS = SHARE // LANES

NEG_FILL = -1e30


def extended(block, sides, width):
    for axis, dim in sides:
        count = lax.axis_size(axis)
        forward = [(i, i + 1) for i in range(count - 1)]
        backward = [(target, source) for source, target in forward]
        low = lax.ppermute(
            lax.slice_in_dim(block, block.shape[dim] - width, None, axis=dim), axis, forward
        )
        high = lax.ppermute(lax.slice_in_dim(block, 0, width, axis=dim), axis, backward)
        block = jnp.concatenate([low, block, high], axis=dim)
    return block


def absorb_block(state, query_heads, key_heads, value_heads, key_start, valid_len):
    run_max, run_sum, summed = state
    scores = jnp.einsum(
        "qhd,khd->qhk", query_heads, key_heads, preferred_element_type=jnp.float32
    ) * (1.0 / math.sqrt(HD))
    usable = key_start + jnp.arange(key_heads.shape[0]) < valid_len
    scores = jnp.where(usable, scores, NEG_FILL)
    new_max = jnp.maximum(run_max, jnp.max(scores, axis=-1))
    rescale = jnp.exp(run_max - new_max)
    weights = jnp.where(usable, jnp.exp(scores - new_max[..., None]), 0.0)
    run_sum = run_sum * rescale + jnp.sum(weights, axis=-1)
    summed = summed * rescale[..., None] + jnp.einsum(
        "qhk,khd->qhd",
        weights.astype(jnp.bfloat16),
        value_heads,
        preferred_element_type=jnp.float32,
    )
    return (new_max, run_sum, summed)


def normalize(block):
    as_float = block.astype(jnp.float32)
    average = jnp.mean(as_float, axis=-1, keepdims=True)
    centered = as_float - average
    variance = jnp.mean(centered * centered, axis=-1, keepdims=True)
    inv_scale = lax.rsqrt(variance + 1e-05)
    return (centered * inv_scale, inv_scale)


def convolve(conv_in, kernel_all, bias_all, out_rows):
    pre_act = bias_all + jnp.zeros((out_rows, conv_in.shape[1]), jnp.float32)
    for tap_index in range(TAPS):
        pre_act = pre_act + kernel_all[tap_index] * conv_in[tap_index : tap_index + out_rows]
    return pre_act


def live_of(positions, valid_len):
    return ((positions >= 0) & (positions < valid_len)).astype(jnp.float32)[:, None]


def general_shards(
    query_in,
    key_in,
    value_in,
    utt_lengths,
    frames_in,
    out_weight,
    conv_kernel,
    conv_bias,
    ln_gain,
    cotangent,
):
    row_count = query_in.shape[1]
    feat_width = query_in.shape[2]
    head_count = feat_width // HD
    valid_len = utt_lengths[0]
    ctx_count = lax.axis_size("ctx")
    row_offset = lax.axis_index("ctx") * row_count
    half_taps = TAPS // 2
    query_heads = query_in[0].reshape(row_count, head_count, HD)
    start_state = (
        jnp.full((row_count, head_count), NEG_FILL, jnp.float32),
        jnp.zeros((row_count, head_count), jnp.float32),
        jnp.zeros((row_count, head_count, HD), jnp.float32),
    )
    state = start_state
    first_row = jnp.int32(0)
    key_part = lax.all_gather(key_in, "ctx", axis=1, tiled=True)
    value_part = lax.all_gather(value_in, "ctx", axis=1, tiled=True)
    piece_rows = key_part.shape[1]
    block_len = math.gcd(piece_rows, 512)
    for block_start in range(0, piece_rows, block_len):
        key_heads = key_part[0, block_start : block_start + block_len].reshape(
            block_len, head_count, HD
        )
        value_heads = value_part[0, block_start : block_start + block_len].reshape(
            block_len, head_count, HD
        )
        state = absorb_block(
            state, query_heads, key_heads, value_heads, first_row + block_start, valid_len
        )
    run_max, run_sum, summed = state
    attended = (summed / run_sum[..., None]).reshape(row_count, feat_width).astype(jnp.bfloat16)
    projected = jnp.dot(
        attended,
        lax.all_gather(out_weight, "fsdp", axis=1, tiled=True),
        preferred_element_type=jnp.float32,
    )
    hidden = (frames_in[0].astype(jnp.float32) + projected).astype(jnp.bfloat16)
    kernel_all, bias_all, gain_all = (
        lax.all_gather(conv_kernel, "fsdp", axis=1, tiled=True),
        lax.all_gather(conv_bias, "fsdp", axis=0, tiled=True),
        lax.all_gather(ln_gain, "fsdp", axis=0, tiled=True),
    )
    grad_in = cotangent[0].astype(jnp.float32)
    live_mask = live_of(row_offset + jnp.arange(row_count), valid_len)
    widened = extended(hidden, (("ctx", 0),), half_taps)
    normed_ext, inv_ext = normalize(widened)
    conv_in = (
        live_of(row_offset - half_taps + jnp.arange(row_count + 2 * half_taps), valid_len)
        * normed_ext
        * gain_all
    )
    pre_act = convolve(conv_in, kernel_all, bias_all, row_count)
    gate_val = jax.nn.sigmoid(pre_act)
    grad_pre = grad_in * live_mask * gate_val * (1.0 + pre_act * (1.0 - gate_val))
    grad_wide = extended(grad_pre.astype(jnp.bfloat16), (("ctx", 0),), half_taps).astype(
        grad_pre.dtype
    )
    normed = normed_ext[half_taps : half_taps + row_count]
    inv_scale = inv_ext[half_taps : half_taps + row_count]
    block_out = (hidden.astype(jnp.float32) + live_mask * pre_act * gate_val).astype(jnp.bfloat16)
    grad_conv = jnp.zeros((row_count, grad_pre.shape[1]), jnp.float32)
    kernel_rows = []
    for tap_index in range(TAPS):
        back = 2 * half_taps - tap_index
        grad_conv = grad_conv + kernel_all[tap_index] * grad_wide[back : back + row_count]
        kernel_rows.append(jnp.sum(grad_pre * conv_in[tap_index : tap_index + row_count], axis=0))
    grad_conv = live_mask * grad_conv
    grad_hat = grad_conv * gain_all
    first_mean = jnp.mean(grad_hat, axis=-1, keepdims=True)
    second_mean = jnp.mean(grad_hat * normed, axis=-1, keepdims=True)
    hidden_grad = (grad_in + (grad_hat - first_mean - normed * second_mean) * inv_scale).astype(
        jnp.bfloat16
    )
    factor = 1.0 / math.sqrt(lax.axis_size("fsdp") * lax.axis_size("dp") * row_count * ctx_count)
    kernel_term = jnp.stack(kernel_rows) * factor
    bias_term = (jnp.sum(grad_pre, axis=0) * factor)[None]
    gain_term = (jnp.sum(grad_conv * normed, axis=0) * factor)[None]
    shares = (
        lax.psum_scatter(
            kernel_term.astype(jnp.bfloat16), "fsdp", scatter_dimension=1, tiled=True
        ).astype(jnp.float32),
        lax.psum_scatter(
            bias_term.astype(jnp.bfloat16), "fsdp", scatter_dimension=1, tiled=True
        ).astype(jnp.float32),
        lax.psum_scatter(
            gain_term.astype(jnp.bfloat16), "fsdp", scatter_dimension=1, tiled=True
        ).astype(jnp.float32),
    )
    totals = lax.psum((shares[0], shares[1], shares[2]), ("ctx", "dp"))
    return (block_out[None], hidden_grad[None], totals[0], totals[1][0], totals[2][0])


def fits_fast(mesh, blocks):
    query_in, frames_in, out_weight = blocks[0], blocks[4], blocks[5]
    ctx_count = mesh.shape["ctx"]
    rows, width = query_in.shape[1], query_in.shape[2]
    return (
        query_in.shape[0] == 1
        and mesh.shape["fsdp"] == 2
        and mesh.shape["dp"] == 2
        and ctx_count == 4
        and width == ctx_count * SHARE
        and rows == LANES
        and frames_in.shape[2] == 2 * out_weight.shape[1]
        and out_weight.shape[1] % SHARE == 0
    )


def facing(count, step):
    return [(i, i ^ step) for i in range(count)]


def pack_kernel(*refs):
    (
        query_ref, key_ref, value_ref, frames_ref, cotan_ref, weight_ref, taps_ref, bias_ref, gain_ref,
        *outs,
    ) = refs[: 9 + 3 * CHUNKS + 2]
    whole, edges, taps, bias, gain, in_sems = refs[-6:]
    *outs, edge, weight_out = outs
    place, core = lax.axis_index("ctx"), lax.axis_index("dp")
    rows = query_ref.shape[1]
    depth = weight_out.shape[0] - 2 * PARAM_ROWS
    arriving = []

    def fetch(source, target):
        arriving.append(pltpu.make_async_copy(source, target, in_sems.at[len(arriving)]))
        arriving[-1].start()

    per_input = rows // NEAR // 2
    for which, source in enumerate((query_ref, key_ref, value_ref)):
        for part in range(per_input):
            span = slice(part * 2 * NEAR, (part + 1) * 2 * NEAR)
            fetch(source.at[0, span, :], whole.at[which, span, :])
    odd = lax.rem(place, 2)
    for side in range(2):
        high = odd if side else 1 - odd
        wide = pl.multiple_of(high * (rows - WIDE), WIDE)
        near = pl.multiple_of(high * (rows - NEAR), NEAR)
        fetch(frames_ref.at[0, pl.ds(wide, WIDE), :], edges.at[side, 0:WIDE, :])
        fetch(cotan_ref.at[0, pl.ds(near, NEAR), :], edges.at[side, WIDE : WIDE + NEAR, :])
    for part in range(0, depth, 64):
        first = pl.multiple_of(core * depth + part, 64)
        fetch(weight_ref.at[pl.ds(first, 64), :], weight_out.at[part : part + 64, :])
    for source, target in ((taps_ref, taps), (bias_ref, bias), (gain_ref, gain)):
        fetch(source, target)
    for which in range(3):
        for part in range(per_input):
            arriving[which * per_input + part].wait()
        at = slice(which * rows, (which + 1) * rows)
        for index, out in enumerate(outs):
            first = (place ^ (index % 3 + 1)) * SHARE + index // 3 * LANES
            out[at, :] = whole[which, :, pl.ds(pl.multiple_of(first, LANES), LANES)]
    seen = 3 * per_input
    for copy in arriving[seen : seen + 4]:
        copy.wait()
    for block in range(edges.shape[2] // LANES):
        base = 3 * rows + block * (WIDE + NEAR)
        outs[0][base : base + WIDE + NEAR, :] = edges[0, :, block * LANES : (block + 1) * LANES]
    edge[...] = edges[1]
    for copy in arriving[-3:]:
        copy.wait()
    params = parameters(taps, bias, gain)
    rounded = params.astype(jnp.bfloat16)
    weight_out[depth : depth + PARAM_ROWS, :] = rounded
    weight_out[depth + PARAM_ROWS :, :] = (params - rounded.astype(jnp.float32)).astype(jnp.bfloat16)
    for copy in arriving[seen + 4 : -3]:
        copy.wait()


def parameters(taps_ref, bias_ref, gain_ref):
    half = taps_ref.shape[1]
    return jnp.concatenate(
        [
            taps_ref[...],
            bias_ref[...].reshape(1, half),
            gain_ref[...].reshape(1, half),
            jnp.zeros((PARAM_ROWS - TAPS - 2, half), jnp.float32),
        ],
        axis=0,
    )


def attend_kernel(chunk, length_ref, query_ref, key_ref, value_ref, *refs):
    parts, outs = refs[:3], refs[3:7]
    query_all, key_all, value_all, attended, sems = refs[7:]
    place, valid_len = lax.axis_index("ctx"), length_ref[0]
    frames, width = query_all.shape
    rows = frames // 4
    targets = (query_all, key_all, value_all)
    mine = pl.ds(pl.multiple_of(place * rows, rows), rows)
    heads = pl.ds(pl.multiple_of(place * SHARE + chunk * LANES, LANES), LANES)
    copies = [
        pltpu.make_async_copy(source.at[0, :, heads], target.at[mine, :], sems.at[which])
        for which, (source, target) in enumerate(zip((query_ref, key_ref, value_ref), targets))
    ]
    for copy in copies:
        copy.start()
    for step, part in enumerate(parts, 1):
        span = pl.ds(pl.multiple_of((place ^ step) * rows, rows), rows)
        for which, target in enumerate(targets):
            target[span, :] = part[which * rows : (which + 1) * rows, :]
    for copy in copies:
        copy.wait()
    attended[0:WIDE, :] = jnp.zeros((WIDE, width), attended.dtype)
    attended[WIDE + frames : 2 * WIDE + frames, :] = jnp.zeros((WIDE, width), attended.dtype)
    usable = lax.broadcasted_iota(jnp.int32, (1, frames), 1) < valid_len
    lane = lax.broadcasted_iota(jnp.int32, (1, LANES), 1)
    for pair in range(width // LANES):
        cols = slice(pair * LANES, (pair + 1) * LANES)
        keys, values = key_all[:, cols], value_all[:, cols]
        heads = [
            (jnp.where(mine, keys, 0).astype(keys.dtype), jnp.where(mine, values, 0).astype(values.dtype))
            for mine in (lane < HD, lane >= HD)
        ]
        for start in range(0, frames, QUERY_ROWS):
            queries = query_all[start : start + QUERY_ROWS, cols]
            total = jnp.zeros((QUERY_ROWS, LANES), jnp.float32)
            for key_head, value_head in heads:
                scores = lax.dot_general(
                    queries, key_head, (((1,), (1,)), ((), ())), preferred_element_type=jnp.float32
                ) * (1.0 / math.sqrt(HD))
                scores = jnp.where(usable, scores, NEG_FILL)
                weights = jnp.exp(scores - jnp.max(scores, axis=1, keepdims=True))
                sums = jnp.sum(weights, axis=1, keepdims=True)
                total += (
                    jnp.dot(
                        weights.astype(jnp.bfloat16), value_head, preferred_element_type=jnp.float32
                    )
                    / sums
                )
            attended[WIDE + start : WIDE + start + QUERY_ROWS, cols] = total.astype(attended.dtype)
    for step in range(4):
        owner = place ^ step
        outs[step][...] = attended[pl.ds(pl.multiple_of(owner * rows, rows), rows + 2 * WIDE), :]


def by_residue(first, last):
    return [[o for o in range(first, last + 1) if o % 8 == r] for r in range(8)]


def module_kernel(*refs):
    count = 4
    length_ref, *replies = refs[: 1 + count * CHUNKS]
    (
        frames_ref, cotan_ref, beside_ref, edge_ref, w_own, w_near, w_far, taps_ref, bias_ref, gain_ref,
        block_hbm, normed, wide_grad, params, inv_rows, sums_own, sums_other, par_mine,
        edges, attended, sums, partial, block_out, out_sems,
    ) = refs[1 + count * CHUNKS :]
    place, side, core = lax.axis_index("ctx"), lax.axis_index("fsdp"), lax.axis_index("dp")
    valid_len = length_ref[0]
    rows, features = frames_ref.shape
    half = features // 2
    tiles, half_tiles = features // LANES, half // LANES
    ext, near = rows + 2 * WIDE, rows + 2 * NEAR
    depth = SHARE
    weight_rows = w_near.shape[0] - 2 * PARAM_ROWS
    per_part = weight_rows // depth

    even = 1 - lax.rem(place, 2)
    for block in range(features // LANES):
        base = 3 * rows + block * (WIDE + NEAR)
        edges[even, :, block * LANES : (block + 1) * LANES] = beside_ref[base : base + WIDE + NEAR, :]
    edges[1 - even] = edge_ref[...]

    def live(first, length):
        position = place * rows + first + lax.broadcasted_iota(jnp.int32, (length, 1), 0)
        return ((position >= 0) & (position < valid_len)).astype(jnp.float32)

    for step in range(count):
        for chunk in range(CHUNKS):
            cols = slice(chunk * LANES, (chunk + 1) * LANES)
            attended[place ^ step, :, cols] = replies[chunk * count + step][...]
    par_own = parameters(taps_ref, bias_ref, gain_ref)
    par_mine[...] = par_own
    par_other = w_near[weight_rows : weight_rows + PARAM_ROWS, :].astype(jnp.float32)
    par_other += w_near[weight_rows + PARAM_ROWS :, :].astype(jnp.float32)
    for tile in range(half_tiles):
        cols = slice(tile * LANES, (tile + 1) * LANES)
        for source, base in ((par_own, side * half_tiles), (par_other, (1 - side) * half_tiles)):
            values = source[:, cols]
            gain = values[TAPS + 1 : TAPS + 2]
            row = lax.broadcasted_iota(jnp.int32, (PARAM_ROWS, 1), 0)
            params[base + tile] = jnp.where(row < TAPS, values * gain, values)

    for tile in range(half_tiles):
        cols = slice(tile * LANES, (tile + 1) * LANES)
        for mine in (True, False):
            at = (side if mine else 1 - side) * half_tiles + tile
            span = pl.ds(pl.multiple_of(at * LANES, LANES), LANES)
            product = jnp.zeros((ext, LANES), jnp.float32)
            for part in range(count):
                if mine:
                    index, weight = part, w_own[part * depth : (part + 1) * depth, cols]
                else:
                    inner = part % per_part
                    source = w_near if part < per_part else w_far
                    index = (core if part < per_part else 1 - core) * per_part + inner
                    weight = source[inner * depth : (inner + 1) * depth, cols]
                product += jnp.dot(attended[index], weight, preferred_element_type=jnp.float32)
            residual = jnp.concatenate(
                [edges[0, 0:WIDE, span], frames_ref[:, span], edges[1, 0:WIDE, span]], axis=0
            )
            hidden = (residual.astype(jnp.float32) + product).astype(jnp.bfloat16)
            block_out[:, span] = hidden[WIDE : WIDE + rows]
            normed[at, 0:ext] = hidden.astype(jnp.float32)

    total = normed[0, 0:ext]
    for tile in range(1, tiles):
        total += normed[tile, 0:ext]
    average = jnp.sum(total, axis=1, keepdims=True) * (1.0 / features)
    total = jnp.zeros((ext, LANES), jnp.float32)
    for tile in range(tiles):
        centered = normed[tile, 0:ext] - average
        total += centered * centered
    variance = jnp.sum(total, axis=1, keepdims=True) * (1.0 / features)
    inv_scale = lax.rsqrt(variance + 1e-05)
    scale = inv_scale * live(-WIDE, ext)
    for tile in range(tiles):
        normed[tile, 0:ext] = (normed[tile, 0:ext] - average) * scale

    live_near = live(-NEAR, near)
    live_rows = live(0, rows)
    inv_rows[...] = jnp.broadcast_to(inv_scale[WIDE : WIDE + rows], inv_rows.shape)

    def one_tile(tile, carry):
        span = pl.ds(pl.multiple_of(tile * LANES, LANES), LANES)
        pre_act = jnp.broadcast_to(params[tile, TAPS : TAPS + 1], (near, LANES))
        for rest, offsets in enumerate(by_residue(1, TAPS)):
            shifted = normed[tile, rest : rest + near + 24]
            for offset in offsets:
                at = offset - rest
                pre_act += params[tile, offset - 1 : offset] * shifted[at : at + near]
        gate = jax.nn.sigmoid(pre_act)
        here = slice(NEAR, NEAR + rows)
        block_out[:, span] = (
            block_out[:, span].astype(jnp.float32) + live_rows * (pre_act * gate)[here]
        ).astype(block_out.dtype)
        pltpu.make_async_copy(
            block_out.at[:, span], block_hbm.at[:, span], out_sems.at[tile]
        ).start()
        cotan = jnp.concatenate(
            [edges[0, WIDE:, span], cotan_ref[:, span], edges[1, WIDE:, span]], axis=0
        ).astype(jnp.float32)
        grad_pre = cotan * live_near * gate * (1.0 + pre_act * (1.0 - gate))
        wide_grad[tile, 0:near] = grad_pre
        own_grad = grad_pre[here]
        first = WIDE - HALF
        for rest, offsets in enumerate(by_residue(first, first + TAPS - 1)):
            low = offsets[0]
            shifted = normed[tile, low : low + rows + 24]
            for offset in offsets:
                at = offset - low
                partial[offset - first] = jnp.sum(
                    (own_grad * shifted[at : at + rows]).reshape(rows // 8, 8, LANES), axis=0
                )
        partial[TAPS] = jnp.sum(own_grad.reshape(rows // 8, 8, LANES), axis=0)
        sums[tile] = jnp.sum(partial[...], axis=1)
        return carry

    lax.fori_loop(0, tiles, one_tile, 0)
    for tile in range(half_tiles):
        cols = slice(tile * LANES, (tile + 1) * LANES)
        sums_own[:, cols] = sums[side * half_tiles + tile].astype(sums_own.dtype)
        sums_other[:, cols] = sums[(1 - side) * half_tiles + tile].astype(sums_other.dtype)
    for tile in range(tiles):
        cols = slice(tile * LANES, (tile + 1) * LANES)
        pltpu.make_async_copy(block_out.at[:, cols], block_hbm.at[:, cols], out_sems.at[tile]).wait()


def backward_kernel(length_ref, cotan_ref, normed, wide_grad, params, inv_rows, grad_hbm, grad_hat, mean_one, mean_two, hidden_grad, out_sems):
    rows, features = cotan_ref.shape
    tiles = features // LANES
    position = lax.axis_index("ctx") * rows + lax.broadcasted_iota(jnp.int32, (rows, 1), 0)
    live_rows = (position < length_ref[0]).astype(jnp.float32)
    mean_one[...] = jnp.zeros_like(mean_one)
    mean_two[...] = jnp.zeros_like(mean_two)

    def one_tile(tile, carry):
        grad = jnp.zeros((rows, LANES), jnp.float32)
        for rest, offsets in enumerate(by_residue(1, TAPS)):
            shifted = wide_grad[tile, rest : rest + rows + 24]
            for offset in offsets:
                at = offset - rest
                tap = TAPS - offset
                grad += params[tile, tap : tap + 1] * shifted[at : at + rows]
        grad = live_rows * grad
        grad_hat[tile] = grad
        mean_one[...] += grad
        mean_two[...] += grad * normed[tile, WIDE : WIDE + rows]
        return carry

    lax.fori_loop(0, tiles, one_tile, 0)
    first_mean = jnp.sum(mean_one[...], axis=1, keepdims=True) * (1.0 / features)
    second_mean = jnp.sum(mean_two[...], axis=1, keepdims=True) * (1.0 / features)
    for tile in range(tiles):
        cols = slice(tile * LANES, (tile + 1) * LANES)
        inner = grad_hat[tile] - first_mean - normed[tile, WIDE : WIDE + rows] * second_mean
        hidden_grad[:, cols] = (
            cotan_ref[:, cols].astype(jnp.float32) + inner * inv_rows[...]
        ).astype(hidden_grad.dtype)
        pltpu.make_async_copy(hidden_grad.at[:, cols], grad_hbm.at[:, cols], out_sems.at[tile]).start()
    for tile in range(tiles):
        cols = slice(tile * LANES, (tile + 1) * LANES)
        pltpu.make_async_copy(hidden_grad.at[:, cols], grad_hbm.at[:, cols], out_sems.at[tile]).wait()


def finish_kernel(factor, mine, one, two, three, params, kernel_out, bias_out, gain_out, terms):
    place = lax.axis_index("ctx")
    for step, source in enumerate((mine, one, two, three)):
        terms[place ^ step] = source[...].astype(jnp.float32)
    total = (((terms[0] + terms[1]) + terms[2]) + terms[3]) * factor
    kernel_out[...] = total[:TAPS] * params[TAPS + 1 : TAPS + 2]
    bias_out[...] = total[TAPS]
    gain_out[...] = jnp.sum(total[:TAPS] * params[:TAPS], axis=0)


def fast_shards(
    query_in,
    key_in,
    value_in,
    utt_lengths,
    frames_in,
    out_weight,
    conv_kernel,
    conv_bias,
    ln_gain,
    cotangent,
):
    count = lax.axis_size("ctx")
    rows, width = query_in.shape[1], query_in.shape[2]
    features, half = frames_in.shape[2], out_weight.shape[1]
    place = lax.axis_index("ctx")
    vmem = pl.BlockSpec(memory_space=pltpu.VMEM)
    smem = pl.BlockSpec(memory_space=pltpu.SMEM)
    hbm = pl.BlockSpec(memory_space=pltpu.HBM)
    swap = [(0, 1), (1, 0)]

    ends = (features // LANES) * (WIDE + NEAR)
    sent = [
        (3 * rows + ends, LANES),
        *[(3 * rows, LANES)] * (3 * CHUNKS - 1),
        (WIDE + NEAR, features),
        (width // 2 + 2 * PARAM_ROWS, half),
    ]
    *pieces, edge, w_sent = pl.pallas_call(
        pack_kernel,
        name="pack",
        out_shape=[jax.ShapeDtypeStruct(shape, jnp.bfloat16) for shape in sent],
        in_specs=[hbm] * 9,
        out_specs=[vmem] * len(sent),
        scratch_shapes=[
            pltpu.VMEM((3, rows, width), jnp.bfloat16),
            pltpu.VMEM((2, WIDE + NEAR, features), jnp.bfloat16),
            pltpu.VMEM((TAPS, half), jnp.float32),
            pltpu.VMEM((half,), jnp.float32),
            pltpu.VMEM((half,), jnp.float32),
            pltpu.SemaphoreType.DMA((32,)),
        ],
        compiler_params=pltpu.CompilerParams(vmem_limit_bytes=32 << 20),
    )(
        *(
            pltpu.with_memory_space_constraint(one, pltpu.HBM)
            for one in (
                query_in,
                key_in,
                value_in,
                frames_in,
                cotangent,
                out_weight,
                conv_kernel,
                conv_bias,
                ln_gain,
            )
        )
    )
    parts = [
        lax.ppermute(one, "ctx", facing(count, index % 3 + 1)) for index, one in enumerate(pieces)
    ]
    edge = lax.ppermute(edge, "ctx", [(1, 2), (2, 1)])
    w_near = lax.ppermute(w_sent, "fsdp", swap)

    replies = []
    for chunk in range(CHUNKS):
        ready = parts[3 * chunk : 3 * chunk + 3]
        if chunk == CHUNKS - 1:
            ready, edge, _ = lax.optimization_barrier((ready, edge, attended))
        attended = pl.pallas_call(
            functools.partial(attend_kernel, chunk),
            name="attend",
            out_shape=[jax.ShapeDtypeStruct((rows + 2 * WIDE, LANES), jnp.bfloat16)] * count,
            in_specs=[smem] + [hbm] * 3 + [vmem] * 3,
            out_specs=[vmem] * count,
            scratch_shapes=[pltpu.VMEM((count * rows, LANES), jnp.bfloat16)] * 3
            + [pltpu.VMEM((count * rows + 2 * WIDE, LANES), jnp.bfloat16)]
            + [pltpu.SemaphoreType.DMA((3,))],
            compiler_params=pltpu.CompilerParams(vmem_limit_bytes=40 << 20),
            cost_estimate=pl.CostEstimate(flops=1, bytes_accessed=1, transcendentals=0),
        )(utt_lengths, query_in, key_in, value_in, *ready)
        replies += [
            reply if step == 0 else lax.ppermute(reply, "ctx", facing(count, step))
            for step, reply in enumerate(attended)
        ]
    _, w_near = lax.optimization_barrier((attended, w_near))
    w_far = lax.ppermute(w_near, "dp", swap)
    frames, cotan = frames_in[0], cotangent[0]

    ext, near = rows + 2 * WIDE, rows + 2 * NEAR
    tiles = features // LANES
    block_out, normed, wide_grad, params, inv_rows, sums_own, sums_other, par_mine = pl.pallas_call(
        module_kernel,
        name="conv_module",
        out_shape=[
            jax.ShapeDtypeStruct((rows, features), jnp.bfloat16),
            jax.ShapeDtypeStruct((tiles, ext + 8, LANES), jnp.float32),
            jax.ShapeDtypeStruct((tiles, near + 8, LANES), jnp.float32),
            jax.ShapeDtypeStruct((tiles, PARAM_ROWS, LANES), jnp.float32),
            jax.ShapeDtypeStruct((rows, LANES), jnp.float32),
            jax.ShapeDtypeStruct((TAPS + 1, half), jnp.bfloat16),
            jax.ShapeDtypeStruct((TAPS + 1, half), jnp.bfloat16),
            jax.ShapeDtypeStruct((PARAM_ROWS, half), jnp.float32),
        ],
        in_specs=[smem] + [vmem] * (count * CHUNKS + 10),
        out_specs=[hbm] + [vmem] * 7,
        scratch_shapes=[
            pltpu.VMEM((2, WIDE + NEAR, features), jnp.bfloat16),
            pltpu.VMEM((count, ext, SHARE), jnp.bfloat16),
            pltpu.VMEM((tiles, TAPS + 1, LANES), jnp.float32),
            pltpu.VMEM((TAPS + 1, 8, LANES), jnp.float32),
            pltpu.VMEM((rows, features), jnp.bfloat16),
            pltpu.SemaphoreType.DMA((tiles,)),
        ],
        compiler_params=pltpu.CompilerParams(vmem_limit_bytes=32 << 20),
        cost_estimate=pl.CostEstimate(
            flops=2 * ext * width * features + 4 * TAPS * rows * features,
            bytes_accessed=2 * width * features + 12 * rows * features,
            transcendentals=near * features,
        ),
    )(
        utt_lengths,
        *replies,
        frames,
        cotan,
        parts[0],
        edge,
        out_weight,
        w_near,
        w_far,
        conv_kernel,
        conv_bias,
        ln_gain,
    )

    pairs = [
        lax.ppermute(sums_other, "fsdp", swap),
        lax.ppermute(sums_other, ("fsdp", "dp"), [(0, 3), (3, 0), (1, 2), (2, 1)]),
        lax.ppermute(sums_own, "dp", swap),
    ]
    hidden_grad = pl.pallas_call(
        backward_kernel,
        name="conv_backward",
        out_shape=jax.ShapeDtypeStruct((rows, features), jnp.bfloat16),
        in_specs=[smem] + [vmem] * 5,
        out_specs=hbm,
        scratch_shapes=[pltpu.VMEM((tiles, rows, LANES), jnp.float32)]
        + [pltpu.VMEM((rows, LANES), jnp.float32)] * 2
        + [pltpu.VMEM((rows, features), jnp.bfloat16), pltpu.SemaphoreType.DMA((tiles,))],
        compiler_params=pltpu.CompilerParams(vmem_limit_bytes=32 << 20),
        cost_estimate=pl.CostEstimate(
            flops=2 * TAPS * rows * features,
            bytes_accessed=12 * rows * features,
            transcendentals=0,
        ),
    )(utt_lengths, cotan, normed, wide_grad, params, inv_rows)
    pairs, hidden_grad = lax.optimization_barrier((pairs, hidden_grad))
    across_x, diagonal, sibling = (one.astype(jnp.float32) for one in pairs)
    found = (sums_own.astype(jnp.float32) + sibling) + (across_x + diagonal)
    found = found.astype(jnp.bfloat16)
    arrived = [lax.ppermute(found, "ctx", facing(count, step)) for step in range(1, count)]
    factor = 1.0 / math.sqrt(lax.axis_size("fsdp") * lax.axis_size("dp") * rows * count)
    grad_kernel, grad_bias, grad_gain = pl.pallas_call(
        functools.partial(finish_kernel, factor),
        name="finish",
        out_shape=[
            jax.ShapeDtypeStruct((TAPS, half), jnp.float32),
            jax.ShapeDtypeStruct((half,), jnp.float32),
            jax.ShapeDtypeStruct((half,), jnp.float32),
        ],
        in_specs=[vmem] * 5,
        out_specs=[vmem] * 3,
        scratch_shapes=[pltpu.VMEM((count, TAPS + 1, half), jnp.float32)],
        compiler_params=pltpu.CompilerParams(vmem_limit_bytes=32 << 20),
    )(found, *arrived, par_mine)
    return (block_out[None], hidden_grad[None], grad_kernel, grad_bias, grad_gain)


def solution(mesh):
    in_specs = (
        P(("groups", "fsdp", "dp"), "ctx", None),
        P(("groups", "fsdp", "dp"), "ctx", None),
        P(("groups", "fsdp", "dp"), "ctx", None),
        P(("groups", "fsdp", "dp")),
        P(("groups", "fsdp", "dp"), "ctx", None),
        P(None, "fsdp"),
        P(None, "fsdp"),
        P("fsdp"),
        P("fsdp"),
        P(("groups", "fsdp", "dp"), "ctx", None),
    )
    out_specs = (
        P(("groups", "fsdp", "dp"), "ctx", None),
        P(("groups", "fsdp", "dp"), "ctx", None),
        P("groups", "fsdp"),
        P(("groups", "fsdp")),
        P(("groups", "fsdp")),
    )

    def shards(*blocks):
        run = fast_shards if fits_fast(mesh, blocks) else general_shards
        return run(*blocks)

    return jax.shard_map(shards, mesh=mesh, in_specs=in_specs, out_specs=out_specs, check_vma=False)
```

```python
import functools
import math

import jax
import jax.numpy as jnp
from jax import lax
from jax.experimental import pallas as pl
from jax.experimental.pallas import tpu as pltpu
from jax.sharding import PartitionSpec as P

HD = 64
TAPS = 31
HALF = TAPS // 2
LANES = 128
WIDE = 32
NEAR = 16
PARAM_ROWS = 40
SHARE = 256
QUERY_ROWS = 128
CHUNKS = SHARE // LANES

NEG_FILL = -1e30


def extended(block, sides, width):
    for axis, dim in sides:
        count = lax.axis_size(axis)
        forward = [(i, i + 1) for i in range(count - 1)]
        backward = [(target, source) for source, target in forward]
        low = lax.ppermute(
            lax.slice_in_dim(block, block.shape[dim] - width, None, axis=dim), axis, forward
        )
        high = lax.ppermute(lax.slice_in_dim(block, 0, width, axis=dim), axis, backward)
        block = jnp.concatenate([low, block, high], axis=dim)
    return block


def absorb_block(state, query_heads, key_heads, value_heads, key_start, valid_len):
    run_max, run_sum, summed = state
    scores = jnp.einsum(
        "qhd,khd->qhk", query_heads, key_heads, preferred_element_type=jnp.float32
    ) * (1.0 / math.sqrt(HD))
    usable = key_start + jnp.arange(key_heads.shape[0]) < valid_len
    scores = jnp.where(usable, scores, NEG_FILL)
    new_max = jnp.maximum(run_max, jnp.max(scores, axis=-1))
    rescale = jnp.exp(run_max - new_max)
    weights = jnp.where(usable, jnp.exp(scores - new_max[..., None]), 0.0)
    run_sum = run_sum * rescale + jnp.sum(weights, axis=-1)
    summed = summed * rescale[..., None] + jnp.einsum(
        "qhk,khd->qhd",
        weights.astype(jnp.bfloat16),
        value_heads,
        preferred_element_type=jnp.float32,
    )
    return (new_max, run_sum, summed)


def normalize(block):
    as_float = block.astype(jnp.float32)
    average = jnp.mean(as_float, axis=-1, keepdims=True)
    centered = as_float - average
    variance = jnp.mean(centered * centered, axis=-1, keepdims=True)
    inv_scale = lax.rsqrt(variance + 1e-05)
    return (centered * inv_scale, inv_scale)


def convolve(conv_in, kernel_all, bias_all, out_rows):
    pre_act = bias_all + jnp.zeros((out_rows, conv_in.shape[1]), jnp.float32)
    for tap_index in range(TAPS):
        pre_act = pre_act + kernel_all[tap_index] * conv_in[tap_index : tap_index + out_rows]
    return pre_act


def live_of(positions, valid_len):
    return ((positions >= 0) & (positions < valid_len)).astype(jnp.float32)[:, None]


def general_shards(
    query_in,
    key_in,
    value_in,
    utt_lengths,
    frames_in,
    out_weight,
    conv_kernel,
    conv_bias,
    ln_gain,
    cotangent,
):
    row_count = query_in.shape[1]
    feat_width = query_in.shape[2]
    head_count = feat_width // HD
    valid_len = utt_lengths[0]
    ctx_count = lax.axis_size("ctx")
    row_offset = lax.axis_index("ctx") * row_count
    half_taps = TAPS // 2
    query_heads = query_in[0].reshape(row_count, head_count, HD)
    start_state = (
        jnp.full((row_count, head_count), NEG_FILL, jnp.float32),
        jnp.zeros((row_count, head_count), jnp.float32),
        jnp.zeros((row_count, head_count, HD), jnp.float32),
    )
    state = start_state
    first_row = jnp.int32(0)
    key_part = lax.all_gather(key_in, "ctx", axis=1, tiled=True)
    value_part = lax.all_gather(value_in, "ctx", axis=1, tiled=True)
    piece_rows = key_part.shape[1]
    block_len = math.gcd(piece_rows, 512)
    for block_start in range(0, piece_rows, block_len):
        key_heads = key_part[0, block_start : block_start + block_len].reshape(
            block_len, head_count, HD
        )
        value_heads = value_part[0, block_start : block_start + block_len].reshape(
            block_len, head_count, HD
        )
        state = absorb_block(
            state, query_heads, key_heads, value_heads, first_row + block_start, valid_len
        )
    run_max, run_sum, summed = state
    attended = (summed / run_sum[..., None]).reshape(row_count, feat_width).astype(jnp.bfloat16)
    projected = jnp.dot(
        attended,
        lax.all_gather(out_weight, "fsdp", axis=1, tiled=True),
        preferred_element_type=jnp.float32,
    )
    hidden = (frames_in[0].astype(jnp.float32) + projected).astype(jnp.bfloat16)
    kernel_all, bias_all, gain_all = (
        lax.all_gather(conv_kernel, "fsdp", axis=1, tiled=True),
        lax.all_gather(conv_bias, "fsdp", axis=0, tiled=True),
        lax.all_gather(ln_gain, "fsdp", axis=0, tiled=True),
    )
    grad_in = cotangent[0].astype(jnp.float32)
    live_mask = live_of(row_offset + jnp.arange(row_count), valid_len)
    widened = extended(hidden, (("ctx", 0),), half_taps)
    normed_ext, inv_ext = normalize(widened)
    conv_in = (
        live_of(row_offset - half_taps + jnp.arange(row_count + 2 * half_taps), valid_len)
        * normed_ext
        * gain_all
    )
    pre_act = convolve(conv_in, kernel_all, bias_all, row_count)
    gate_val = jax.nn.sigmoid(pre_act)
    grad_pre = grad_in * live_mask * gate_val * (1.0 + pre_act * (1.0 - gate_val))
    grad_wide = extended(grad_pre.astype(jnp.bfloat16), (("ctx", 0),), half_taps).astype(
        grad_pre.dtype
    )
    normed = normed_ext[half_taps : half_taps + row_count]
    inv_scale = inv_ext[half_taps : half_taps + row_count]
    block_out = (hidden.astype(jnp.float32) + live_mask * pre_act * gate_val).astype(jnp.bfloat16)
    grad_conv = jnp.zeros((row_count, grad_pre.shape[1]), jnp.float32)
    kernel_rows = []
    for tap_index in range(TAPS):
        back = 2 * half_taps - tap_index
        grad_conv = grad_conv + kernel_all[tap_index] * grad_wide[back : back + row_count]
        kernel_rows.append(jnp.sum(grad_pre * conv_in[tap_index : tap_index + row_count], axis=0))
    grad_conv = live_mask * grad_conv
    grad_hat = grad_conv * gain_all
    first_mean = jnp.mean(grad_hat, axis=-1, keepdims=True)
    second_mean = jnp.mean(grad_hat * normed, axis=-1, keepdims=True)
    hidden_grad = (grad_in + (grad_hat - first_mean - normed * second_mean) * inv_scale).astype(
        jnp.bfloat16
    )
    factor = 1.0 / math.sqrt(lax.axis_size("fsdp") * lax.axis_size("dp") * row_count * ctx_count)
    kernel_term = jnp.stack(kernel_rows) * factor
    bias_term = (jnp.sum(grad_pre, axis=0) * factor)[None]
    gain_term = (jnp.sum(grad_conv * normed, axis=0) * factor)[None]
    shares = (
        lax.psum_scatter(
            kernel_term.astype(jnp.bfloat16), "fsdp", scatter_dimension=1, tiled=True
        ).astype(jnp.float32),
        lax.psum_scatter(
            bias_term.astype(jnp.bfloat16), "fsdp", scatter_dimension=1, tiled=True
        ).astype(jnp.float32),
        lax.psum_scatter(
            gain_term.astype(jnp.bfloat16), "fsdp", scatter_dimension=1, tiled=True
        ).astype(jnp.float32),
    )
    totals = lax.psum((shares[0], shares[1], shares[2]), ("ctx", "dp"))
    return (block_out[None], hidden_grad[None], totals[0], totals[1][0], totals[2][0])


def fits_fast(mesh, blocks):
    query_in, frames_in, out_weight = blocks[0], blocks[4], blocks[5]
    ctx_count = mesh.shape["ctx"]
    rows, width = query_in.shape[1], query_in.shape[2]
    return (
        query_in.shape[0] == 1
        and mesh.shape["fsdp"] == 2
        and mesh.shape["dp"] == 2
        and ctx_count == 4
        and width == ctx_count * SHARE
        and rows == LANES
        and frames_in.shape[2] == 2 * out_weight.shape[1]
        and out_weight.shape[1] % SHARE == 0
    )


def facing(count, step):
    return [(i, i ^ step) for i in range(count)]


PIECES = [(1, 0)] + [(step, chunk) for chunk in range(CHUNKS) for step in (2, 3)]


def pack_kernel(*refs):
    (
        query_ref, key_ref, value_ref, frames_ref, cotan_ref, weight_ref, taps_ref, bias_ref, gain_ref,
        *outs,
    ) = refs[: 9 + len(PIECES) + 2]
    whole, edges, taps, bias, gain, in_sems = refs[-6:]
    *outs, edge, weight_out = outs
    place, core = lax.axis_index("ctx"), lax.axis_index("dp")
    rows = query_ref.shape[1]
    depth = weight_out.shape[0] - 2 * PARAM_ROWS
    arriving = []

    def fetch(source, target):
        arriving.append(pltpu.make_async_copy(source, target, in_sems.at[len(arriving)]))
        arriving[-1].start()

    per_input = rows // NEAR // 2
    for which, source in enumerate((query_ref, key_ref, value_ref)):
        for part in range(per_input):
            span = slice(part * 2 * NEAR, (part + 1) * 2 * NEAR)
            fetch(source.at[0, span, :], whole.at[which, span, :])
    odd = lax.rem(place, 2)
    for side in range(2):
        high = odd if side else 1 - odd
        wide = pl.multiple_of(high * (rows - WIDE), WIDE)
        near = pl.multiple_of(high * (rows - NEAR), NEAR)
        fetch(frames_ref.at[0, pl.ds(wide, WIDE), :], edges.at[side, 0:WIDE, :])
        fetch(cotan_ref.at[0, pl.ds(near, NEAR), :], edges.at[side, WIDE : WIDE + NEAR, :])
    for part in range(0, depth, 64):
        first = pl.multiple_of(core * depth + part, 64)
        fetch(weight_ref.at[pl.ds(first, 64), :], weight_out.at[part : part + 64, :])
    for source, target in ((taps_ref, taps), (bias_ref, bias), (gain_ref, gain)):
        fetch(source, target)
    for which in range(3):
        for part in range(per_input):
            arriving[which * per_input + part].wait()
        at = slice(which * rows, (which + 1) * rows)
        for out, (step, chunk) in zip(outs, PIECES):
            first = (place ^ step) * SHARE + chunk * LANES
            size = out.shape[1]
            out[at, :] = whole[which, :, pl.ds(pl.multiple_of(first, LANES), size)]
    seen = 3 * per_input
    for copy in arriving[seen : seen + 4]:
        copy.wait()
    for block in range(edges.shape[2] // SHARE):
        base = 3 * rows + block * (WIDE + NEAR)
        outs[0][base : base + WIDE + NEAR, :] = edges[0, :, block * SHARE : (block + 1) * SHARE]
    edge[...] = edges[1]
    for copy in arriving[-3:]:
        copy.wait()
    params = parameters(taps, bias, gain)
    rounded = params.astype(jnp.bfloat16)
    weight_out[depth : depth + PARAM_ROWS, :] = rounded
    weight_out[depth + PARAM_ROWS :, :] = (params - rounded.astype(jnp.float32)).astype(jnp.bfloat16)
    for copy in arriving[seen + 4 : -3]:
        copy.wait()


def parameters(taps_ref, bias_ref, gain_ref):
    half = taps_ref.shape[1]
    return jnp.concatenate(
        [
            taps_ref[...],
            bias_ref[...].reshape(1, half),
            gain_ref[...].reshape(1, half),
            jnp.zeros((PARAM_ROWS - TAPS - 2, half), jnp.float32),
        ],
        axis=0,
    )


def attend_kernel(chunk, length_ref, query_ref, key_ref, value_ref, *refs):
    parts, refs = refs[:3], refs[3:]
    before, refs = refs[:chunk], refs[chunk:]
    outs = refs[:4]
    query_all, key_all, value_all, attended, sems = refs[4:]
    place, valid_len = lax.axis_index("ctx"), length_ref[0]
    frames, width = query_all.shape
    rows = frames // 4
    targets = (query_all, key_all, value_all)
    mine = pl.ds(pl.multiple_of(place * rows, rows), rows)
    heads = pl.ds(pl.multiple_of(place * SHARE + chunk * LANES, LANES), LANES)
    copies = [
        pltpu.make_async_copy(source.at[0, :, heads], target.at[mine, :], sems.at[which])
        for which, (source, target) in enumerate(zip((query_ref, key_ref, value_ref), targets))
    ]
    for copy in copies:
        copy.start()
    for step, part in enumerate(parts, 1):
        span = pl.ds(pl.multiple_of((place ^ step) * rows, rows), rows)
        for which, target in enumerate(targets):
            cols = slice(chunk * LANES, (chunk + 1) * LANES) if step == 1 else slice(None)
            target[span, :] = part[which * rows : (which + 1) * rows, cols]
    for copy in copies:
        copy.wait()
    attended[0:WIDE, :] = jnp.zeros((WIDE, width), attended.dtype)
    attended[WIDE + frames : 2 * WIDE + frames, :] = jnp.zeros((WIDE, width), attended.dtype)
    usable = lax.broadcasted_iota(jnp.int32, (1, frames), 1) < valid_len
    lane = lax.broadcasted_iota(jnp.int32, (1, LANES), 1)
    for pair in range(width // LANES):
        cols = slice(pair * LANES, (pair + 1) * LANES)
        keys, values = key_all[:, cols], value_all[:, cols]
        heads = [
            (jnp.where(mine, keys, 0).astype(keys.dtype), jnp.where(mine, values, 0).astype(values.dtype))
            for mine in (lane < HD, lane >= HD)
        ]
        for start in range(0, frames, QUERY_ROWS):
            queries = query_all[start : start + QUERY_ROWS, cols]
            total = jnp.zeros((QUERY_ROWS, LANES), jnp.float32)
            for key_head, value_head in heads:
                scores = lax.dot_general(
                    queries, key_head, (((1,), (1,)), ((), ())), preferred_element_type=jnp.float32
                ) * (1.0 / math.sqrt(HD))
                scores = jnp.where(usable, scores, NEG_FILL)
                weights = jnp.exp(scores - jnp.max(scores, axis=1, keepdims=True))
                sums = jnp.sum(weights, axis=1, keepdims=True)
                total += (
                    jnp.dot(
                        weights.astype(jnp.bfloat16), value_head, preferred_element_type=jnp.float32
                    )
                    / sums
                )
            attended[WIDE + start : WIDE + start + QUERY_ROWS, cols] = total.astype(attended.dtype)
    for step in range(4):
        owner = place ^ step
        found = attended[pl.ds(pl.multiple_of(owner * rows, rows), rows + 2 * WIDE), :]
        if step == 1 and chunk:
            outs[step][:, :LANES] = before[0][...]
            outs[step][:, LANES:] = found
        else:
            outs[step][...] = found


def by_residue(first, last):
    return [[o for o in range(first, last + 1) if o % 8 == r] for r in range(8)]


def module_kernel(*refs):
    count = 4
    length_ref, *replies = refs[: 1 + count * CHUNKS - 1]
    (
        frames_ref, cotan_ref, beside_ref, edge_ref, w_own, w_near, w_far, taps_ref, bias_ref, gain_ref,
        block_hbm, normed, wide_grad, params, inv_rows, sums_own, sums_other, par_mine,
        edges, attended, sums, partial, block_out, out_sems,
    ) = refs[count * CHUNKS :]
    place, side, core = lax.axis_index("ctx"), lax.axis_index("fsdp"), lax.axis_index("dp")
    valid_len = length_ref[0]
    rows, features = frames_ref.shape
    half = features // 2
    tiles, half_tiles = features // LANES, half // LANES
    ext, near = rows + 2 * WIDE, rows + 2 * NEAR
    depth = SHARE
    weight_rows = w_near.shape[0] - 2 * PARAM_ROWS
    per_part = weight_rows // depth

    even = 1 - lax.rem(place, 2)
    for block in range(features // SHARE):
        base = 3 * rows + block * (WIDE + NEAR)
        edges[even, :, block * SHARE : (block + 1) * SHARE] = beside_ref[base : base + WIDE + NEAR, :]
    edges[1 - even] = edge_ref[...]

    def live(first, length):
        position = place * rows + first + lax.broadcasted_iota(jnp.int32, (length, 1), 0)
        return ((position >= 0) & (position < valid_len)).astype(jnp.float32)

    for step in range(count):
        if step == 1:
            attended[place ^ step] = replies[1][...]
            continue
        for chunk in range(CHUNKS):
            cols = slice(chunk * LANES, (chunk + 1) * LANES)
            attended[place ^ step, :, cols] = replies[(0, 4)[chunk] + (step - chunk if step else 0)][...]
    par_own = parameters(taps_ref, bias_ref, gain_ref)
    par_mine[...] = par_own
    par_other = w_near[weight_rows : weight_rows + PARAM_ROWS, :].astype(jnp.float32)
    par_other += w_near[weight_rows + PARAM_ROWS :, :].astype(jnp.float32)
    for tile in range(half_tiles):
        cols = slice(tile * LANES, (tile + 1) * LANES)
        for source, base in ((par_own, side * half_tiles), (par_other, (1 - side) * half_tiles)):
            values = source[:, cols]
            gain = values[TAPS + 1 : TAPS + 2]
            row = lax.broadcasted_iota(jnp.int32, (PARAM_ROWS, 1), 0)
            params[base + tile] = jnp.where(row < TAPS, values * gain, values)

    for tile in range(half_tiles):
        cols = slice(tile * LANES, (tile + 1) * LANES)
        for mine in (True, False):
            at = (side if mine else 1 - side) * half_tiles + tile
            span = pl.ds(pl.multiple_of(at * LANES, LANES), LANES)
            product = jnp.zeros((ext, LANES), jnp.float32)
            for part in range(count):
                if mine:
                    index, weight = part, w_own[part * depth : (part + 1) * depth, cols]
                else:
                    inner = part % per_part
                    source = w_near if part < per_part else w_far
                    index = (core if part < per_part else 1 - core) * per_part + inner
                    weight = source[inner * depth : (inner + 1) * depth, cols]
                product += jnp.dot(attended[index], weight, preferred_element_type=jnp.float32)
            residual = jnp.concatenate(
                [edges[0, 0:WIDE, span], frames_ref[:, span], edges[1, 0:WIDE, span]], axis=0
            )
            hidden = (residual.astype(jnp.float32) + product).astype(jnp.bfloat16)
            block_out[:, span] = hidden[WIDE : WIDE + rows]
            normed[at, 0:ext] = hidden.astype(jnp.float32)

    total = normed[0, 0:ext]
    for tile in range(1, tiles):
        total += normed[tile, 0:ext]
    average = jnp.sum(total, axis=1, keepdims=True) * (1.0 / features)
    total = jnp.zeros((ext, LANES), jnp.float32)
    for tile in range(tiles):
        centered = normed[tile, 0:ext] - average
        total += centered * centered
    variance = jnp.sum(total, axis=1, keepdims=True) * (1.0 / features)
    inv_scale = lax.rsqrt(variance + 1e-05)
    scale = inv_scale * live(-WIDE, ext)
    for tile in range(tiles):
        normed[tile, 0:ext] = (normed[tile, 0:ext] - average) * scale

    live_near = live(-NEAR, near)
    live_rows = live(0, rows)
    inv_rows[...] = jnp.broadcast_to(inv_scale[WIDE : WIDE + rows], inv_rows.shape)

    def one_tile(tile, carry):
        span = pl.ds(pl.multiple_of(tile * LANES, LANES), LANES)
        pre_act = jnp.broadcast_to(params[tile, TAPS : TAPS + 1], (near, LANES))
        for rest, offsets in enumerate(by_residue(1, TAPS)):
            shifted = normed[tile, rest : rest + near + 24]
            for offset in offsets:
                at = offset - rest
                pre_act += params[tile, offset - 1 : offset] * shifted[at : at + near]
        gate = jax.nn.sigmoid(pre_act)
        here = slice(NEAR, NEAR + rows)
        block_out[:, span] = (
            block_out[:, span].astype(jnp.float32) + live_rows * (pre_act * gate)[here]
        ).astype(block_out.dtype)
        pltpu.make_async_copy(
            block_out.at[:, span], block_hbm.at[:, span], out_sems.at[tile]
        ).start()
        cotan = jnp.concatenate(
            [edges[0, WIDE:, span], cotan_ref[:, span], edges[1, WIDE:, span]], axis=0
        ).astype(jnp.float32)
        grad_pre = cotan * live_near * gate * (1.0 + pre_act * (1.0 - gate))
        wide_grad[tile, 0:near] = grad_pre
        own_grad = grad_pre[here]
        first = WIDE - HALF
        for rest, offsets in enumerate(by_residue(first, first + TAPS - 1)):
            low = offsets[0]
            shifted = normed[tile, low : low + rows + 24]
            for offset in offsets:
                at = offset - low
                partial[offset - first] = jnp.sum(
                    (own_grad * shifted[at : at + rows]).reshape(rows // 8, 8, LANES), axis=0
                )
        partial[TAPS] = jnp.sum(own_grad.reshape(rows // 8, 8, LANES), axis=0)
        sums[tile] = jnp.sum(partial[...], axis=1)
        return carry

    lax.fori_loop(0, tiles, one_tile, 0)
    for tile in range(half_tiles):
        cols = slice(tile * LANES, (tile + 1) * LANES)
        sums_own[:, cols] = sums[side * half_tiles + tile].astype(sums_own.dtype)
        sums_other[:, cols] = sums[(1 - side) * half_tiles + tile].astype(sums_other.dtype)
    for tile in range(tiles):
        cols = slice(tile * LANES, (tile + 1) * LANES)
        pltpu.make_async_copy(block_out.at[:, cols], block_hbm.at[:, cols], out_sems.at[tile]).wait()


def backward_kernel(length_ref, cotan_ref, normed, wide_grad, params, inv_rows, grad_hbm, grad_hat, mean_one, mean_two, hidden_grad, out_sems):
    rows, features = cotan_ref.shape
    tiles = features // LANES
    position = lax.axis_index("ctx") * rows + lax.broadcasted_iota(jnp.int32, (rows, 1), 0)
    live_rows = (position < length_ref[0]).astype(jnp.float32)
    mean_one[...] = jnp.zeros_like(mean_one)
    mean_two[...] = jnp.zeros_like(mean_two)

    def one_tile(tile, carry):
        grad = jnp.zeros((rows, LANES), jnp.float32)
        for rest, offsets in enumerate(by_residue(1, TAPS)):
            shifted = wide_grad[tile, rest : rest + rows + 24]
            for offset in offsets:
                at = offset - rest
                tap = TAPS - offset
                grad += params[tile, tap : tap + 1] * shifted[at : at + rows]
        grad = live_rows * grad
        grad_hat[tile] = grad
        mean_one[...] += grad
        mean_two[...] += grad * normed[tile, WIDE : WIDE + rows]
        return carry

    lax.fori_loop(0, tiles, one_tile, 0)
    first_mean = jnp.sum(mean_one[...], axis=1, keepdims=True) * (1.0 / features)
    second_mean = jnp.sum(mean_two[...], axis=1, keepdims=True) * (1.0 / features)
    for tile in range(tiles):
        cols = slice(tile * LANES, (tile + 1) * LANES)
        inner = grad_hat[tile] - first_mean - normed[tile, WIDE : WIDE + rows] * second_mean
        hidden_grad[:, cols] = (
            cotan_ref[:, cols].astype(jnp.float32) + inner * inv_rows[...]
        ).astype(hidden_grad.dtype)
        pltpu.make_async_copy(hidden_grad.at[:, cols], grad_hbm.at[:, cols], out_sems.at[tile]).start()
    for tile in range(tiles):
        cols = slice(tile * LANES, (tile + 1) * LANES)
        pltpu.make_async_copy(hidden_grad.at[:, cols], grad_hbm.at[:, cols], out_sems.at[tile]).wait()


def finish_kernel(factor, mine, one, two, three, params, kernel_out, bias_out, gain_out, terms):
    place = lax.axis_index("ctx")
    for step, source in enumerate((mine, one, two, three)):
        terms[place ^ step] = source[...].astype(jnp.float32)
    total = (((terms[0] + terms[1]) + terms[2]) + terms[3]) * factor
    kernel_out[...] = total[:TAPS] * params[TAPS + 1 : TAPS + 2]
    bias_out[...] = total[TAPS]
    gain_out[...] = jnp.sum(total[:TAPS] * params[:TAPS], axis=0)


def fast_shards(
    query_in,
    key_in,
    value_in,
    utt_lengths,
    frames_in,
    out_weight,
    conv_kernel,
    conv_bias,
    ln_gain,
    cotangent,
):
    count = lax.axis_size("ctx")
    rows, width = query_in.shape[1], query_in.shape[2]
    features, half = frames_in.shape[2], out_weight.shape[1]
    place = lax.axis_index("ctx")
    vmem = pl.BlockSpec(memory_space=pltpu.VMEM)
    smem = pl.BlockSpec(memory_space=pltpu.SMEM)
    hbm = pl.BlockSpec(memory_space=pltpu.HBM)
    swap = [(0, 1), (1, 0)]

    ends = (features // SHARE) * (WIDE + NEAR)
    sent = [
        (3 * rows + ends, SHARE),
        *[(3 * rows, LANES)] * (len(PIECES) - 1),
        (WIDE + NEAR, features),
        (width // 2 + 2 * PARAM_ROWS, half),
    ]
    *pieces, edge, w_sent = pl.pallas_call(
        pack_kernel,
        name="pack",
        out_shape=[jax.ShapeDtypeStruct(shape, jnp.bfloat16) for shape in sent],
        in_specs=[hbm] * 9,
        out_specs=[vmem] * len(sent),
        scratch_shapes=[
            pltpu.VMEM((3, rows, width), jnp.bfloat16),
            pltpu.VMEM((2, WIDE + NEAR, features), jnp.bfloat16),
            pltpu.VMEM((TAPS, half), jnp.float32),
            pltpu.VMEM((half,), jnp.float32),
            pltpu.VMEM((half,), jnp.float32),
            pltpu.SemaphoreType.DMA((32,)),
        ],
        compiler_params=pltpu.CompilerParams(vmem_limit_bytes=32 << 20),
    )(
        *(
            pltpu.with_memory_space_constraint(one, pltpu.HBM)
            for one in (
                query_in,
                key_in,
                value_in,
                frames_in,
                cotangent,
                out_weight,
                conv_kernel,
                conv_bias,
                ln_gain,
            )
        )
    )
    parts = [
        lax.ppermute(one, "ctx", facing(count, step)) for one, (step, _) in zip(pieces, PIECES)
    ]
    edge = lax.ppermute(edge, "ctx", [(1, 2), (2, 1)])
    w_near = lax.ppermute(w_sent, "fsdp", swap)

    replies, attended = [], []
    for chunk in range(CHUNKS):
        ready = [parts[0], *parts[2 * chunk + 1 : 2 * chunk + 3]]
        before = []
        if chunk:
            before = [attended[1]]
            ready, edge = lax.optimization_barrier((ready, edge))
        attended = pl.pallas_call(
            functools.partial(attend_kernel, chunk),
            name="attend",
            out_shape=[
                jax.ShapeDtypeStruct(
                    (rows + 2 * WIDE, SHARE if chunk and step == 1 else LANES), jnp.bfloat16
                )
                for step in range(count)
            ],
            in_specs=[smem] + [hbm] * 3 + [vmem] * (3 + len(before)),
            out_specs=[vmem] * count,
            scratch_shapes=[pltpu.VMEM((count * rows, LANES), jnp.bfloat16)] * 3
            + [pltpu.VMEM((count * rows + 2 * WIDE, LANES), jnp.bfloat16)]
            + [pltpu.SemaphoreType.DMA((3,))],
            compiler_params=pltpu.CompilerParams(vmem_limit_bytes=40 << 20),
            cost_estimate=pl.CostEstimate(flops=1, bytes_accessed=1, transcendentals=0),
        )(utt_lengths, query_in, key_in, value_in, *ready, *before)
        replies += [
            lax.ppermute(reply, "ctx", facing(count, step))
            if step > 1 or (step == 1 and chunk)
            else reply
            for step, reply in enumerate(attended)
        ]
    replies = [replies[0], replies[5], replies[2], replies[3], replies[4], *replies[6:]]
    _, w_near = lax.optimization_barrier((attended, w_near))
    w_far = lax.ppermute(w_near, "dp", swap)
    frames, cotan = frames_in[0], cotangent[0]

    ext, near = rows + 2 * WIDE, rows + 2 * NEAR
    tiles = features // LANES
    block_out, normed, wide_grad, params, inv_rows, sums_own, sums_other, par_mine = pl.pallas_call(
        module_kernel,
        name="conv_module",
        out_shape=[
            jax.ShapeDtypeStruct((rows, features), jnp.bfloat16),
            jax.ShapeDtypeStruct((tiles, ext + 8, LANES), jnp.float32),
            jax.ShapeDtypeStruct((tiles, near + 8, LANES), jnp.float32),
            jax.ShapeDtypeStruct((tiles, PARAM_ROWS, LANES), jnp.float32),
            jax.ShapeDtypeStruct((rows, LANES), jnp.float32),
            jax.ShapeDtypeStruct((TAPS + 1, half), jnp.bfloat16),
            jax.ShapeDtypeStruct((TAPS + 1, half), jnp.bfloat16),
            jax.ShapeDtypeStruct((PARAM_ROWS, half), jnp.float32),
        ],
        in_specs=[smem] + [vmem] * (count * CHUNKS + 9),
        out_specs=[hbm] + [vmem] * 7,
        scratch_shapes=[
            pltpu.VMEM((2, WIDE + NEAR, features), jnp.bfloat16),
            pltpu.VMEM((count, ext, SHARE), jnp.bfloat16),
            pltpu.VMEM((tiles, TAPS + 1, LANES), jnp.float32),
            pltpu.VMEM((TAPS + 1, 8, LANES), jnp.float32),
            pltpu.VMEM((rows, features), jnp.bfloat16),
            pltpu.SemaphoreType.DMA((tiles,)),
        ],
        compiler_params=pltpu.CompilerParams(vmem_limit_bytes=32 << 20),
        cost_estimate=pl.CostEstimate(
            flops=2 * ext * width * features + 4 * TAPS * rows * features,
            bytes_accessed=2 * width * features + 12 * rows * features,
            transcendentals=near * features,
        ),
    )(
        utt_lengths,
        *replies,
        frames,
        cotan,
        parts[0],
        edge,
        out_weight,
        w_near,
        w_far,
        conv_kernel,
        conv_bias,
        ln_gain,
    )

    pairs = [
        lax.ppermute(sums_other, "fsdp", swap),
        lax.ppermute(sums_other, ("fsdp", "dp"), [(0, 3), (3, 0), (1, 2), (2, 1)]),
        lax.ppermute(sums_own, "dp", swap),
    ]
    hidden_grad = pl.pallas_call(
        backward_kernel,
        name="conv_backward",
        out_shape=jax.ShapeDtypeStruct((rows, features), jnp.bfloat16),
        in_specs=[smem] + [vmem] * 5,
        out_specs=hbm,
        scratch_shapes=[pltpu.VMEM((tiles, rows, LANES), jnp.float32)]
        + [pltpu.VMEM((rows, LANES), jnp.float32)] * 2
        + [pltpu.VMEM((rows, features), jnp.bfloat16), pltpu.SemaphoreType.DMA((tiles,))],
        compiler_params=pltpu.CompilerParams(vmem_limit_bytes=32 << 20),
        cost_estimate=pl.CostEstimate(
            flops=2 * TAPS * rows * features,
            bytes_accessed=12 * rows * features,
            transcendentals=0,
        ),
    )(utt_lengths, cotan, normed, wide_grad, params, inv_rows)
    pairs, hidden_grad = lax.optimization_barrier((pairs, hidden_grad))
    across_x, diagonal, sibling = (one.astype(jnp.float32) for one in pairs)
    found = (sums_own.astype(jnp.float32) + sibling) + (across_x + diagonal)
    found = found.astype(jnp.bfloat16)
    arrived = [lax.ppermute(found, "ctx", facing(count, step)) for step in range(1, count)]
    factor = 1.0 / math.sqrt(lax.axis_size("fsdp") * lax.axis_size("dp") * rows * count)
    grad_kernel, grad_bias, grad_gain = pl.pallas_call(
        functools.partial(finish_kernel, factor),
        name="finish",
        out_shape=[
            jax.ShapeDtypeStruct((TAPS, half), jnp.float32),
            jax.ShapeDtypeStruct((half,), jnp.float32),
            jax.ShapeDtypeStruct((half,), jnp.float32),
        ],
        in_specs=[vmem] * 5,
        out_specs=[vmem] * 3,
        scratch_shapes=[pltpu.VMEM((count, TAPS + 1, half), jnp.float32)],
        compiler_params=pltpu.CompilerParams(vmem_limit_bytes=32 << 20),
    )(found, *arrived, par_mine)
    return (block_out[None], hidden_grad[None], grad_kernel, grad_bias, grad_gain)


def solution(mesh):
    in_specs = (
        P(("groups", "fsdp", "dp"), "ctx", None),
        P(("groups", "fsdp", "dp"), "ctx", None),
        P(("groups", "fsdp", "dp"), "ctx", None),
        P(("groups", "fsdp", "dp")),
        P(("groups", "fsdp", "dp"), "ctx", None),
        P(None, "fsdp"),
        P(None, "fsdp"),
        P("fsdp"),
        P("fsdp"),
        P(("groups", "fsdp", "dp"), "ctx", None),
    )
    out_specs = (
        P(("groups", "fsdp", "dp"), "ctx", None),
        P(("groups", "fsdp", "dp"), "ctx", None),
        P("groups", "fsdp"),
        P(("groups", "fsdp")),
        P(("groups", "fsdp")),
    )

    def shards(*blocks):
        run = fast_shards if fits_fast(mesh, blocks) else general_shards
        return run(*blocks)

    return jax.shard_map(shards, mesh=mesh, in_specs=in_specs, out_specs=out_specs, check_vma=False)
```

```python
import functools
import math

import jax
import jax.numpy as jnp
from jax import lax
from jax.experimental import pallas as pl
from jax.experimental.pallas import tpu as pltpu
from jax.sharding import PartitionSpec as P

HD = 64
TAPS = 31
HALF = TAPS // 2
LANES = 128
WIDE = 32
NEAR = 16
PARAM_ROWS = 40
SHARE = 256
QUERY_ROWS = 128
CHUNKS = SHARE // LANES

NEG_FILL = -1e30


def extended(block, sides, width):
    for axis, dim in sides:
        count = lax.axis_size(axis)
        forward = [(i, i + 1) for i in range(count - 1)]
        backward = [(target, source) for source, target in forward]
        low = lax.ppermute(
            lax.slice_in_dim(block, block.shape[dim] - width, None, axis=dim), axis, forward
        )
        high = lax.ppermute(lax.slice_in_dim(block, 0, width, axis=dim), axis, backward)
        block = jnp.concatenate([low, block, high], axis=dim)
    return block


def absorb_block(state, query_heads, key_heads, value_heads, key_start, valid_len):
    run_max, run_sum, summed = state
    scores = jnp.einsum(
        "qhd,khd->qhk", query_heads, key_heads, preferred_element_type=jnp.float32
    ) * (1.0 / math.sqrt(HD))
    usable = key_start + jnp.arange(key_heads.shape[0]) < valid_len
    scores = jnp.where(usable, scores, NEG_FILL)
    new_max = jnp.maximum(run_max, jnp.max(scores, axis=-1))
    rescale = jnp.exp(run_max - new_max)
    weights = jnp.where(usable, jnp.exp(scores - new_max[..., None]), 0.0)
    run_sum = run_sum * rescale + jnp.sum(weights, axis=-1)
    summed = summed * rescale[..., None] + jnp.einsum(
        "qhk,khd->qhd",
        weights.astype(jnp.bfloat16),
        value_heads,
        preferred_element_type=jnp.float32,
    )
    return (new_max, run_sum, summed)


def normalize(block):
    as_float = block.astype(jnp.float32)
    average = jnp.mean(as_float, axis=-1, keepdims=True)
    centered = as_float - average
    variance = jnp.mean(centered * centered, axis=-1, keepdims=True)
    inv_scale = lax.rsqrt(variance + 1e-05)
    return (centered * inv_scale, inv_scale)


def convolve(conv_in, kernel_all, bias_all, out_rows):
    pre_act = bias_all + jnp.zeros((out_rows, conv_in.shape[1]), jnp.float32)
    for tap_index in range(TAPS):
        pre_act = pre_act + kernel_all[tap_index] * conv_in[tap_index : tap_index + out_rows]
    return pre_act


def live_of(positions, valid_len):
    return ((positions >= 0) & (positions < valid_len)).astype(jnp.float32)[:, None]


def general_shards(
    query_in,
    key_in,
    value_in,
    utt_lengths,
    frames_in,
    out_weight,
    conv_kernel,
    conv_bias,
    ln_gain,
    cotangent,
):
    row_count = query_in.shape[1]
    feat_width = query_in.shape[2]
    head_count = feat_width // HD
    valid_len = utt_lengths[0]
    ctx_count = lax.axis_size("ctx")
    row_offset = lax.axis_index("ctx") * row_count
    half_taps = TAPS // 2
    query_heads = query_in[0].reshape(row_count, head_count, HD)
    start_state = (
        jnp.full((row_count, head_count), NEG_FILL, jnp.float32),
        jnp.zeros((row_count, head_count), jnp.float32),
        jnp.zeros((row_count, head_count, HD), jnp.float32),
    )
    state = start_state
    first_row = jnp.int32(0)
    key_part = lax.all_gather(key_in, "ctx", axis=1, tiled=True)
    value_part = lax.all_gather(value_in, "ctx", axis=1, tiled=True)
    piece_rows = key_part.shape[1]
    block_len = math.gcd(piece_rows, 512)
    for block_start in range(0, piece_rows, block_len):
        key_heads = key_part[0, block_start : block_start + block_len].reshape(
            block_len, head_count, HD
        )
        value_heads = value_part[0, block_start : block_start + block_len].reshape(
            block_len, head_count, HD
        )
        state = absorb_block(
            state, query_heads, key_heads, value_heads, first_row + block_start, valid_len
        )
    run_max, run_sum, summed = state
    attended = (summed / run_sum[..., None]).reshape(row_count, feat_width).astype(jnp.bfloat16)
    projected = jnp.dot(
        attended,
        lax.all_gather(out_weight, "fsdp", axis=1, tiled=True),
        preferred_element_type=jnp.float32,
    )
    hidden = (frames_in[0].astype(jnp.float32) + projected).astype(jnp.bfloat16)
    kernel_all, bias_all, gain_all = (
        lax.all_gather(conv_kernel, "fsdp", axis=1, tiled=True),
        lax.all_gather(conv_bias, "fsdp", axis=0, tiled=True),
        lax.all_gather(ln_gain, "fsdp", axis=0, tiled=True),
    )
    grad_in = cotangent[0].astype(jnp.float32)
    live_mask = live_of(row_offset + jnp.arange(row_count), valid_len)
    widened = extended(hidden, (("ctx", 0),), half_taps)
    normed_ext, inv_ext = normalize(widened)
    conv_in = (
        live_of(row_offset - half_taps + jnp.arange(row_count + 2 * half_taps), valid_len)
        * normed_ext
        * gain_all
    )
    pre_act = convolve(conv_in, kernel_all, bias_all, row_count)
    gate_val = jax.nn.sigmoid(pre_act)
    grad_pre = grad_in * live_mask * gate_val * (1.0 + pre_act * (1.0 - gate_val))
    grad_wide = extended(grad_pre.astype(jnp.bfloat16), (("ctx", 0),), half_taps).astype(
        grad_pre.dtype
    )
    normed = normed_ext[half_taps : half_taps + row_count]
    inv_scale = inv_ext[half_taps : half_taps + row_count]
    block_out = (hidden.astype(jnp.float32) + live_mask * pre_act * gate_val).astype(jnp.bfloat16)
    grad_conv = jnp.zeros((row_count, grad_pre.shape[1]), jnp.float32)
    kernel_rows = []
    for tap_index in range(TAPS):
        back = 2 * half_taps - tap_index
        grad_conv = grad_conv + kernel_all[tap_index] * grad_wide[back : back + row_count]
        kernel_rows.append(jnp.sum(grad_pre * conv_in[tap_index : tap_index + row_count], axis=0))
    grad_conv = live_mask * grad_conv
    grad_hat = grad_conv * gain_all
    first_mean = jnp.mean(grad_hat, axis=-1, keepdims=True)
    second_mean = jnp.mean(grad_hat * normed, axis=-1, keepdims=True)
    hidden_grad = (grad_in + (grad_hat - first_mean - normed * second_mean) * inv_scale).astype(
        jnp.bfloat16
    )
    factor = 1.0 / math.sqrt(lax.axis_size("fsdp") * lax.axis_size("dp") * row_count * ctx_count)
    kernel_term = jnp.stack(kernel_rows) * factor
    bias_term = (jnp.sum(grad_pre, axis=0) * factor)[None]
    gain_term = (jnp.sum(grad_conv * normed, axis=0) * factor)[None]
    shares = (
        lax.psum_scatter(
            kernel_term.astype(jnp.bfloat16), "fsdp", scatter_dimension=1, tiled=True
        ).astype(jnp.float32),
        lax.psum_scatter(
            bias_term.astype(jnp.bfloat16), "fsdp", scatter_dimension=1, tiled=True
        ).astype(jnp.float32),
        lax.psum_scatter(
            gain_term.astype(jnp.bfloat16), "fsdp", scatter_dimension=1, tiled=True
        ).astype(jnp.float32),
    )
    totals = lax.psum((shares[0], shares[1], shares[2]), ("ctx", "dp"))
    return (block_out[None], hidden_grad[None], totals[0], totals[1][0], totals[2][0])


def fits_fast(mesh, blocks):
    query_in, frames_in, out_weight = blocks[0], blocks[4], blocks[5]
    ctx_count = mesh.shape["ctx"]
    rows, width = query_in.shape[1], query_in.shape[2]
    return (
        query_in.shape[0] == 1
        and mesh.shape["fsdp"] == 2
        and mesh.shape["dp"] == 2
        and ctx_count == 4
        and width == ctx_count * SHARE
        and rows == LANES
        and frames_in.shape[2] == 2 * out_weight.shape[1]
        and out_weight.shape[1] % SHARE == 0
    )


def facing(count, step):
    return [(i, i ^ step) for i in range(count)]


PIECES = [(1, 0)] + [(step, chunk) for chunk in range(CHUNKS) for step in (2, 3)]


def pack_kernel(*refs):
    (
        query_ref, key_ref, value_ref, frames_ref, cotan_ref, weight_ref, taps_ref, bias_ref, gain_ref,
        *outs,
    ) = refs[: 9 + len(PIECES) + 2]
    whole, edges, taps, bias, gain, in_sems = refs[-6:]
    *outs, edge, weight_out = outs
    place, core = lax.axis_index("ctx"), lax.axis_index("dp")
    rows = query_ref.shape[1]
    depth = weight_out.shape[0] - 2 * PARAM_ROWS
    arriving = []

    def fetch(source, target):
        arriving.append(pltpu.make_async_copy(source, target, in_sems.at[len(arriving)]))
        arriving[-1].start()

    per_input = rows // NEAR // 2
    for which, source in enumerate((query_ref, key_ref, value_ref)):
        for part in range(per_input):
            span = slice(part * 2 * NEAR, (part + 1) * 2 * NEAR)
            fetch(source.at[0, span, :], whole.at[which, span, :])
    odd = lax.rem(place, 2)
    for side in range(2):
        high = odd if side else 1 - odd
        wide = pl.multiple_of(high * (rows - WIDE), WIDE)
        near = pl.multiple_of(high * (rows - NEAR), NEAR)
        fetch(frames_ref.at[0, pl.ds(wide, WIDE), :], edges.at[side, 0:WIDE, :])
        fetch(cotan_ref.at[0, pl.ds(near, NEAR), :], edges.at[side, WIDE : WIDE + NEAR, :])
    for part in range(0, depth, 64):
        first = pl.multiple_of(core * depth + part, 64)
        fetch(weight_ref.at[pl.ds(first, 64), :], weight_out.at[part : part + 64, :])
    for source, target in ((taps_ref, taps), (bias_ref, bias), (gain_ref, gain)):
        fetch(source, target)
    for which in range(3):
        for part in range(per_input):
            arriving[which * per_input + part].wait()
        at = slice(which * rows, (which + 1) * rows)
        for out, (step, chunk) in zip(outs, PIECES):
            first = (place ^ step) * SHARE + chunk * LANES
            size = out.shape[1]
            out[at, :] = whole[which, :, pl.ds(pl.multiple_of(first, LANES), size)]
    seen = 3 * per_input
    for copy in arriving[seen : seen + 4]:
        copy.wait()
    for block in range(edges.shape[2] // SHARE):
        base = 3 * rows + block * (WIDE + NEAR)
        outs[0][base : base + WIDE + NEAR, :] = edges[0, :, block * SHARE : (block + 1) * SHARE]
    edge[...] = edges[1]
    for copy in arriving[-3:]:
        copy.wait()
    params = parameters(taps, bias, gain)
    rounded = params.astype(jnp.bfloat16)
    weight_out[depth : depth + PARAM_ROWS, :] = rounded
    weight_out[depth + PARAM_ROWS :, :] = (params - rounded.astype(jnp.float32)).astype(jnp.bfloat16)
    for copy in arriving[seen + 4 : -3]:
        copy.wait()


def parameters(taps_ref, bias_ref, gain_ref):
    half = taps_ref.shape[1]
    return jnp.concatenate(
        [
            taps_ref[...],
            bias_ref[...].reshape(1, half),
            gain_ref[...].reshape(1, half),
            jnp.zeros((PARAM_ROWS - TAPS - 2, half), jnp.float32),
        ],
        axis=0,
    )


def attend_kernel(chunk, length_ref, query_ref, key_ref, value_ref, *refs):
    parts, refs = refs[:3], refs[3:]
    before, refs = refs[: 4 * chunk], refs[4 * chunk :]
    outs = refs[:4]
    query_all, key_all, value_all, attended, sems = refs[4:]
    place, valid_len = lax.axis_index("ctx"), length_ref[0]
    frames, width = query_all.shape
    rows = frames // 4
    targets = (query_all, key_all, value_all)
    mine = pl.ds(pl.multiple_of(place * rows, rows), rows)
    heads = pl.ds(pl.multiple_of(place * SHARE + chunk * LANES, LANES), LANES)
    copies = [
        pltpu.make_async_copy(source.at[0, :, heads], target.at[mine, :], sems.at[which])
        for which, (source, target) in enumerate(zip((query_ref, key_ref, value_ref), targets))
    ]
    for copy in copies:
        copy.start()
    for step, part in enumerate(parts, 1):
        span = pl.ds(pl.multiple_of((place ^ step) * rows, rows), rows)
        for which, target in enumerate(targets):
            cols = slice(chunk * LANES, (chunk + 1) * LANES) if step == 1 else slice(None)
            target[span, :] = part[which * rows : (which + 1) * rows, cols]
    for copy in copies:
        copy.wait()
    attended[0:WIDE, :] = jnp.zeros((WIDE, width), attended.dtype)
    attended[WIDE + frames : 2 * WIDE + frames, :] = jnp.zeros((WIDE, width), attended.dtype)
    usable = lax.broadcasted_iota(jnp.int32, (1, frames), 1) < valid_len
    lane = lax.broadcasted_iota(jnp.int32, (1, LANES), 1)
    for pair in range(width // LANES):
        cols = slice(pair * LANES, (pair + 1) * LANES)
        keys, values = key_all[:, cols], value_all[:, cols]
        heads = [
            (jnp.where(mine, keys, 0).astype(keys.dtype), jnp.where(mine, values, 0).astype(values.dtype))
            for mine in (lane < HD, lane >= HD)
        ]
        for start in range(0, frames, QUERY_ROWS):
            queries = query_all[start : start + QUERY_ROWS, cols]
            total = jnp.zeros((QUERY_ROWS, LANES), jnp.float32)
            for key_head, value_head in heads:
                scores = lax.dot_general(
                    queries, key_head, (((1,), (1,)), ((), ())), preferred_element_type=jnp.float32
                ) * (1.0 / math.sqrt(HD))
                scores = jnp.where(usable, scores, NEG_FILL)
                weights = jnp.exp(scores - jnp.max(scores, axis=1, keepdims=True))
                sums = jnp.sum(weights, axis=1, keepdims=True)
                total += (
                    jnp.dot(
                        weights.astype(jnp.bfloat16), value_head, preferred_element_type=jnp.float32
                    )
                    / sums
                )
            attended[WIDE + start : WIDE + start + QUERY_ROWS, cols] = total.astype(attended.dtype)
    for step in range(4):
        owner = place ^ step
        found = attended[pl.ds(pl.multiple_of(owner * rows, rows), rows + 2 * WIDE), :]
        if chunk:
            outs[step][:, :LANES] = before[step][...]
            outs[step][:, LANES:] = found
        else:
            outs[step][...] = found


def by_residue(first, last):
    return [[o for o in range(first, last + 1) if o % 8 == r] for r in range(8)]


def live_at(length_ref, rows, first, length):
    position = lax.axis_index("ctx") * rows + first + lax.broadcasted_iota(jnp.int32, (length, 1), 0)
    return ((position >= 0) & (position < length_ref[0])).astype(jnp.float32)


def weight_block(w_own, w_near, w_far, part, tile, mine):
    cols = slice(tile * LANES, (tile + 1) * LANES)
    if mine:
        return w_own[pl.ds(pl.multiple_of(part * SHARE, SHARE), SHARE), cols]
    per_part = (w_near.shape[0] - 2 * PARAM_ROWS) // SHARE
    rows = pl.ds(pl.multiple_of(lax.rem(part, per_part) * SHARE, SHARE), SHARE)
    near = lax.div(part, per_part) == lax.axis_index("dp")
    return jnp.where(near, w_near[rows, cols], w_far[rows, cols])


def prepare_kernel(*refs):
    (
        length_ref, own_ref, frames_ref, cotan_ref, beside_ref, edge_ref, w_own, w_near, w_far,
        taps_ref, bias_ref, gain_ref, base, cotan_live, params, par_mine, edges,
    ) = refs
    place, side = lax.axis_index("ctx"), lax.axis_index("fsdp")
    rows, features = frames_ref.shape
    half_tiles = features // 2 // LANES
    weight_rows = w_near.shape[0] - 2 * PARAM_ROWS
    even = 1 - lax.rem(place, 2)
    for block in range(features // SHARE):
        first = 3 * rows + block * (WIDE + NEAR)
        edges[even, :, block * SHARE : (block + 1) * SHARE] = beside_ref[first : first + WIDE + NEAR, :]
    edges[1 - even] = edge_ref[...]
    par_own = parameters(taps_ref, bias_ref, gain_ref)
    par_mine[...] = par_own
    par_other = w_near[weight_rows : weight_rows + PARAM_ROWS, :].astype(jnp.float32)
    par_other += w_near[weight_rows + PARAM_ROWS :, :].astype(jnp.float32)
    live_near = live_at(length_ref, rows, -NEAR, rows + 2 * NEAR)
    own = own_ref[...]
    row = lax.broadcasted_iota(jnp.int32, (PARAM_ROWS, 1), 0)
    for tile in range(half_tiles):
        cols = slice(tile * LANES, (tile + 1) * LANES)
        for mine, source in ((True, par_own), (False, par_other)):
            at = (side if mine else 1 - side) * half_tiles + tile
            values = source[:, cols]
            params[at] = jnp.where(row < TAPS, values * values[TAPS + 1 : TAPS + 2], values)
            span = pl.ds(pl.multiple_of(at * LANES, LANES), LANES)
            weight = weight_block(w_own, w_near, w_far, place, tile, mine)
            base[at] = jnp.dot(own, weight, preferred_element_type=jnp.float32) + jnp.concatenate(
                [edges[0, 0:WIDE, span], frames_ref[:, span], edges[1, 0:WIDE, span]], axis=0
            ).astype(jnp.float32)
            cotan_live[at] = live_near * jnp.concatenate(
                [edges[0, WIDE:, span], cotan_ref[:, span], edges[1, WIDE:, span]], axis=0
            ).astype(jnp.float32)


def module_kernel(*refs):
    (
        length_ref, reply_one, reply_two, reply_three, base, cotan_live, params, w_own, w_near, w_far,
        block_hbm, normed, wide_grad, inv_rows, sums_own, sums_other,
        sums, partial, block_out, out_sems,
    ) = refs
    place, side = lax.axis_index("ctx"), lax.axis_index("fsdp")
    tiles, ext = base.shape[:2]
    rows, features = ext - 2 * WIDE, tiles * LANES
    half_tiles, near = tiles // 2, rows + 2 * NEAR
    for tile in range(half_tiles):
        for mine in (True, False):
            at = (side if mine else 1 - side) * half_tiles + tile
            span = pl.ds(pl.multiple_of(at * LANES, LANES), LANES)
            product = base[at]
            for step, reply in enumerate((reply_one, reply_two, reply_three), 1):
                weight = weight_block(w_own, w_near, w_far, place ^ step, tile, mine)
                product += jnp.dot(reply[...], weight, preferred_element_type=jnp.float32)
            hidden = product.astype(jnp.bfloat16)
            block_out[:, span] = hidden[WIDE : WIDE + rows]
            normed[at, 0:ext] = hidden.astype(jnp.float32)

    total = normed[0, 0:ext]
    for tile in range(1, tiles):
        total += normed[tile, 0:ext]
    average = jnp.sum(total, axis=1, keepdims=True) * (1.0 / features)
    total = jnp.zeros((ext, LANES), jnp.float32)
    for tile in range(tiles):
        centered = normed[tile, 0:ext] - average
        total += centered * centered
    variance = jnp.sum(total, axis=1, keepdims=True) * (1.0 / features)
    inv_scale = lax.rsqrt(variance + 1e-05)
    scale = inv_scale * live_at(length_ref, rows, -WIDE, ext)
    for tile in range(tiles):
        normed[tile, 0:ext] = (normed[tile, 0:ext] - average) * scale

    live_rows = live_at(length_ref, rows, 0, rows)
    inv_rows[...] = jnp.broadcast_to(inv_scale[WIDE : WIDE + rows], inv_rows.shape)

    def one_tile(tile, carry):
        span = pl.ds(pl.multiple_of(tile * LANES, LANES), LANES)
        pre_act = jnp.broadcast_to(params[tile, TAPS : TAPS + 1], (near, LANES))
        for rest, offsets in enumerate(by_residue(1, TAPS)):
            shifted = normed[tile, rest : rest + near + 24]
            for offset in offsets:
                at = offset - rest
                pre_act += params[tile, offset - 1 : offset] * shifted[at : at + near]
        gate = jax.nn.sigmoid(pre_act)
        here = slice(NEAR, NEAR + rows)
        block_out[:, span] = (
            block_out[:, span].astype(jnp.float32) + live_rows * (pre_act * gate)[here]
        ).astype(block_out.dtype)
        pltpu.make_async_copy(
            block_out.at[:, span], block_hbm.at[:, span], out_sems.at[tile]
        ).start()
        grad_pre = cotan_live[tile] * gate * (1.0 + pre_act * (1.0 - gate))
        wide_grad[tile, 0:near] = grad_pre
        own_grad = grad_pre[here]
        first = WIDE - HALF
        for rest, offsets in enumerate(by_residue(first, first + TAPS - 1)):
            low = offsets[0]
            shifted = normed[tile, low : low + rows + 24]
            for offset in offsets:
                at = offset - low
                partial[offset - first] = jnp.sum(
                    (own_grad * shifted[at : at + rows]).reshape(rows // 8, 8, LANES), axis=0
                )
        partial[TAPS] = jnp.sum(own_grad.reshape(rows // 8, 8, LANES), axis=0)
        sums[tile] = jnp.sum(partial[...], axis=1)
        return carry

    lax.fori_loop(0, tiles, one_tile, 0)
    for tile in range(half_tiles):
        cols = slice(tile * LANES, (tile + 1) * LANES)
        sums_own[:, cols] = sums[side * half_tiles + tile].astype(sums_own.dtype)
        sums_other[:, cols] = sums[(1 - side) * half_tiles + tile].astype(sums_other.dtype)
    for tile in range(tiles):
        cols = slice(tile * LANES, (tile + 1) * LANES)
        pltpu.make_async_copy(block_out.at[:, cols], block_hbm.at[:, cols], out_sems.at[tile]).wait()


def backward_kernel(length_ref, normed, wide_grad, params, grad_hat, means, mean_one, mean_two):
    tiles, rows = grad_hat.shape[:2]
    live_rows = live_at(length_ref, rows, 0, rows)
    mean_one[...] = jnp.zeros_like(mean_one)
    mean_two[...] = jnp.zeros_like(mean_two)

    def one_tile(tile, carry):
        grad = jnp.zeros((rows, LANES), jnp.float32)
        for rest, offsets in enumerate(by_residue(1, TAPS)):
            shifted = wide_grad[tile, rest : rest + rows + 24]
            for offset in offsets:
                at = offset - rest
                tap = TAPS - offset
                grad += params[tile, tap : tap + 1] * shifted[at : at + rows]
        grad = live_rows * grad
        grad_hat[tile] = grad
        mean_one[...] += grad
        mean_two[...] += grad * normed[tile, WIDE : WIDE + rows]
        return carry

    lax.fori_loop(0, tiles, one_tile, 0)
    for index, total in enumerate((mean_one, mean_two)):
        mean = jnp.sum(total[...], axis=1, keepdims=True) * (1.0 / (tiles * LANES))
        means[index] = jnp.broadcast_to(mean, (rows, LANES))


def hidden_grad_kernel(cotan_ref, normed, inv_rows, grad_hat, means, grad_hbm, hidden_grad, out_sems):
    tiles, rows = grad_hat.shape[:2]
    copies = []
    for tile in range(tiles):
        cols = slice(tile * LANES, (tile + 1) * LANES)
        inner = grad_hat[tile] - means[0] - normed[tile, WIDE : WIDE + rows] * means[1]
        hidden_grad[:, cols] = (
            cotan_ref[:, cols].astype(jnp.float32) + inner * inv_rows[...]
        ).astype(hidden_grad.dtype)
        copies.append(
            pltpu.make_async_copy(hidden_grad.at[:, cols], grad_hbm.at[:, cols], out_sems.at[tile])
        )
        copies[-1].start()
    for copy in copies:
        copy.wait()


def finish_kernel(factor, mine, one, two, three, params, kernel_out, bias_out, gain_out, terms):
    place = lax.axis_index("ctx")
    for step, source in enumerate((mine, one, two, three)):
        terms[place ^ step] = source[...].astype(jnp.float32)
    total = (((terms[0] + terms[1]) + terms[2]) + terms[3]) * factor
    kernel_out[...] = total[:TAPS] * params[TAPS + 1 : TAPS + 2]
    bias_out[...] = total[TAPS]
    gain_out[...] = jnp.sum(total[:TAPS] * params[:TAPS], axis=0)


def fast_shards(
    query_in,
    key_in,
    value_in,
    utt_lengths,
    frames_in,
    out_weight,
    conv_kernel,
    conv_bias,
    ln_gain,
    cotangent,
):
    count = lax.axis_size("ctx")
    rows, width = query_in.shape[1], query_in.shape[2]
    features, half = frames_in.shape[2], out_weight.shape[1]
    place = lax.axis_index("ctx")
    vmem = pl.BlockSpec(memory_space=pltpu.VMEM)
    smem = pl.BlockSpec(memory_space=pltpu.SMEM)
    hbm = pl.BlockSpec(memory_space=pltpu.HBM)
    swap = [(0, 1), (1, 0)]

    ends = (features // SHARE) * (WIDE + NEAR)
    sent = [
        (3 * rows + ends, SHARE),
        *[(3 * rows, LANES)] * (len(PIECES) - 1),
        (WIDE + NEAR, features),
        (width // 2 + 2 * PARAM_ROWS, half),
    ]
    *pieces, edge, w_sent = pl.pallas_call(
        pack_kernel,
        name="pack",
        out_shape=[jax.ShapeDtypeStruct(shape, jnp.bfloat16) for shape in sent],
        in_specs=[hbm] * 9,
        out_specs=[vmem] * len(sent),
        scratch_shapes=[
            pltpu.VMEM((3, rows, width), jnp.bfloat16),
            pltpu.VMEM((2, WIDE + NEAR, features), jnp.bfloat16),
            pltpu.VMEM((TAPS, half), jnp.float32),
            pltpu.VMEM((half,), jnp.float32),
            pltpu.VMEM((half,), jnp.float32),
            pltpu.SemaphoreType.DMA((32,)),
        ],
        compiler_params=pltpu.CompilerParams(vmem_limit_bytes=32 << 20),
    )(
        *(
            pltpu.with_memory_space_constraint(one, pltpu.HBM)
            for one in (
                query_in,
                key_in,
                value_in,
                frames_in,
                cotangent,
                out_weight,
                conv_kernel,
                conv_bias,
                ln_gain,
            )
        )
    )
    parts = [
        lax.ppermute(one, "ctx", facing(count, step)) for one, (step, _) in zip(pieces, PIECES)
    ]
    edge = lax.ppermute(edge, "ctx", [(1, 2), (2, 1)])
    w_near = lax.ppermute(w_sent, "fsdp", swap)

    attended = []
    for chunk in range(CHUNKS):
        ready = [parts[0], *parts[2 * chunk + 1 : 2 * chunk + 3]]
        before = []
        if chunk:
            before = attended
            ready, edge = lax.optimization_barrier((ready, edge))
        attended = pl.pallas_call(
            functools.partial(attend_kernel, chunk),
            name="attend",
            out_shape=[
                jax.ShapeDtypeStruct((rows + 2 * WIDE, (chunk + 1) * LANES), jnp.bfloat16)
            ]
            * count,
            in_specs=[smem] + [hbm] * 3 + [vmem] * (3 + len(before)),
            out_specs=[vmem] * count,
            scratch_shapes=[pltpu.VMEM((count * rows, LANES), jnp.bfloat16)] * 3
            + [pltpu.VMEM((count * rows + 2 * WIDE, LANES), jnp.bfloat16)]
            + [pltpu.SemaphoreType.DMA((3,))],
            compiler_params=pltpu.CompilerParams(vmem_limit_bytes=40 << 20),
            cost_estimate=pl.CostEstimate(flops=1, bytes_accessed=1, transcendentals=0),
        )(utt_lengths, query_in, key_in, value_in, *ready, *before)
    own, *replies = [
        reply if step == 0 else lax.ppermute(reply, "ctx", facing(count, step))
        for step, reply in enumerate(attended)
    ]
    _, w_near = lax.optimization_barrier((attended, w_near))
    w_far = lax.ppermute(w_near, "dp", swap)
    frames, cotan = frames_in[0], cotangent[0]

    ext, near = rows + 2 * WIDE, rows + 2 * NEAR
    tiles = features // LANES
    base, cotan_live, params, par_mine = pl.pallas_call(
        prepare_kernel,
        name="prepare",
        out_shape=[
            jax.ShapeDtypeStruct((tiles, ext, LANES), jnp.float32),
            jax.ShapeDtypeStruct((tiles, near, LANES), jnp.float32),
            jax.ShapeDtypeStruct((tiles, PARAM_ROWS, LANES), jnp.float32),
            jax.ShapeDtypeStruct((PARAM_ROWS, half), jnp.float32),
        ],
        in_specs=[smem] + [vmem] * 11,
        out_specs=[vmem] * 4,
        scratch_shapes=[pltpu.VMEM((2, WIDE + NEAR, features), jnp.bfloat16)],
        compiler_params=pltpu.CompilerParams(vmem_limit_bytes=32 << 20),
        cost_estimate=pl.CostEstimate(
            flops=2 * ext * SHARE * features, bytes_accessed=8 * rows * features, transcendentals=0
        ),
    )(
        utt_lengths,
        own,
        frames,
        cotan,
        parts[0],
        edge,
        out_weight,
        w_near,
        w_far,
        conv_kernel,
        conv_bias,
        ln_gain,
    )
    block_out, normed, wide_grad, inv_rows, sums_own, sums_other = pl.pallas_call(
        module_kernel,
        name="conv_module",
        out_shape=[
            jax.ShapeDtypeStruct((rows, features), jnp.bfloat16),
            jax.ShapeDtypeStruct((tiles, ext + 8, LANES), jnp.float32),
            jax.ShapeDtypeStruct((tiles, near + 8, LANES), jnp.float32),
            jax.ShapeDtypeStruct((rows, LANES), jnp.float32),
            jax.ShapeDtypeStruct((TAPS + 1, half), jnp.bfloat16),
            jax.ShapeDtypeStruct((TAPS + 1, half), jnp.bfloat16),
        ],
        in_specs=[smem] + [vmem] * 9,
        out_specs=[hbm] + [vmem] * 5,
        scratch_shapes=[
            pltpu.VMEM((tiles, TAPS + 1, LANES), jnp.float32),
            pltpu.VMEM((TAPS + 1, 8, LANES), jnp.float32),
            pltpu.VMEM((rows, features), jnp.bfloat16),
            pltpu.SemaphoreType.DMA((tiles,)),
        ],
        compiler_params=pltpu.CompilerParams(vmem_limit_bytes=32 << 20),
        cost_estimate=pl.CostEstimate(
            flops=2 * ext * width * features + 4 * TAPS * rows * features,
            bytes_accessed=2 * width * features + 12 * rows * features,
            transcendentals=near * features,
        ),
    )(
        utt_lengths,
        *replies,
        base,
        cotan_live,
        params,
        out_weight,
        w_near,
        w_far,
    )

    pairs = [
        lax.ppermute(sums_other, "fsdp", swap),
        lax.ppermute(sums_other, ("fsdp", "dp"), [(0, 3), (3, 0), (1, 2), (2, 1)]),
        lax.ppermute(sums_own, "dp", swap),
    ]
    grad_hat, means = pl.pallas_call(
        backward_kernel,
        name="conv_backward",
        out_shape=[
            jax.ShapeDtypeStruct((tiles, rows, LANES), jnp.float32),
            jax.ShapeDtypeStruct((2, rows, LANES), jnp.float32),
        ],
        in_specs=[smem] + [vmem] * 3,
        out_specs=[vmem] * 2,
        scratch_shapes=[pltpu.VMEM((rows, LANES), jnp.float32)] * 2,
        compiler_params=pltpu.CompilerParams(vmem_limit_bytes=32 << 20),
        cost_estimate=pl.CostEstimate(
            flops=2 * TAPS * rows * features,
            bytes_accessed=12 * rows * features,
            transcendentals=0,
        ),
    )(utt_lengths, normed, wide_grad, params)
    pairs, grad_hat = lax.optimization_barrier((pairs, grad_hat))
    across_x, diagonal, sibling = (one.astype(jnp.float32) for one in pairs)
    found = (sums_own.astype(jnp.float32) + sibling) + (across_x + diagonal)
    found = found.astype(jnp.bfloat16)
    arrived = [lax.ppermute(found, "ctx", facing(count, step)) for step in range(1, count)]
    hidden_grad = pl.pallas_call(
        hidden_grad_kernel,
        name="hidden_grad",
        out_shape=jax.ShapeDtypeStruct((rows, features), jnp.bfloat16),
        in_specs=[vmem] * 5,
        out_specs=hbm,
        scratch_shapes=[
            pltpu.VMEM((rows, features), jnp.bfloat16),
            pltpu.SemaphoreType.DMA((tiles,)),
        ],
        compiler_params=pltpu.CompilerParams(vmem_limit_bytes=32 << 20),
        cost_estimate=pl.CostEstimate(
            flops=6 * rows * features, bytes_accessed=12 * rows * features, transcendentals=0
        ),
    )(cotan, normed, inv_rows, grad_hat, means)
    arrived, hidden_grad = lax.optimization_barrier((arrived, hidden_grad))
    factor = 1.0 / math.sqrt(lax.axis_size("fsdp") * lax.axis_size("dp") * rows * count)
    grad_kernel, grad_bias, grad_gain = pl.pallas_call(
        functools.partial(finish_kernel, factor),
        name="finish",
        out_shape=[
            jax.ShapeDtypeStruct((TAPS, half), jnp.float32),
            jax.ShapeDtypeStruct((half,), jnp.float32),
            jax.ShapeDtypeStruct((half,), jnp.float32),
        ],
        in_specs=[vmem] * 5,
        out_specs=[vmem] * 3,
        scratch_shapes=[pltpu.VMEM((count, TAPS + 1, half), jnp.float32)],
        compiler_params=pltpu.CompilerParams(vmem_limit_bytes=32 << 20),
    )(found, *arrived, par_mine)
    return (block_out[None], hidden_grad[None], grad_kernel, grad_bias, grad_gain)


def solution(mesh):
    in_specs = (
        P(("groups", "fsdp", "dp"), "ctx", None),
        P(("groups", "fsdp", "dp"), "ctx", None),
        P(("groups", "fsdp", "dp"), "ctx", None),
        P(("groups", "fsdp", "dp")),
        P(("groups", "fsdp", "dp"), "ctx", None),
        P(None, "fsdp"),
        P(None, "fsdp"),
        P("fsdp"),
        P("fsdp"),
        P(("groups", "fsdp", "dp"), "ctx", None),
    )
    out_specs = (
        P(("groups", "fsdp", "dp"), "ctx", None),
        P(("groups", "fsdp", "dp"), "ctx", None),
        P("groups", "fsdp"),
        P(("groups", "fsdp")),
        P(("groups", "fsdp")),
    )

    def shards(*blocks):
        run = fast_shards if fits_fast(mesh, blocks) else general_shards
        return run(*blocks)

    return jax.shard_map(shards, mesh=mesh, in_specs=in_specs, out_specs=out_specs, check_vma=False)
```

```python
import functools
import math

import jax
import jax.numpy as jnp
from jax import lax
from jax.experimental import pallas as pl
from jax.experimental.pallas import tpu as pltpu
from jax.sharding import PartitionSpec as P

HD = 64
TAPS = 31
HALF = TAPS // 2
LANES = 128
WIDE = 32
NEAR = 16
PARAM_ROWS = 40
SHARE = 256
QUERY_ROWS = 128
CHUNKS = SHARE // LANES

NEG_FILL = -1e30


def extended(block, sides, width):
    for axis, dim in sides:
        count = lax.axis_size(axis)
        forward = [(i, i + 1) for i in range(count - 1)]
        backward = [(target, source) for source, target in forward]
        low = lax.ppermute(
            lax.slice_in_dim(block, block.shape[dim] - width, None, axis=dim), axis, forward
        )
        high = lax.ppermute(lax.slice_in_dim(block, 0, width, axis=dim), axis, backward)
        block = jnp.concatenate([low, block, high], axis=dim)
    return block


def absorb_block(state, query_heads, key_heads, value_heads, key_start, valid_len):
    run_max, run_sum, summed = state
    scores = jnp.einsum(
        "qhd,khd->qhk", query_heads, key_heads, preferred_element_type=jnp.float32
    ) * (1.0 / math.sqrt(HD))
    usable = key_start + jnp.arange(key_heads.shape[0]) < valid_len
    scores = jnp.where(usable, scores, NEG_FILL)
    new_max = jnp.maximum(run_max, jnp.max(scores, axis=-1))
    rescale = jnp.exp(run_max - new_max)
    weights = jnp.where(usable, jnp.exp(scores - new_max[..., None]), 0.0)
    run_sum = run_sum * rescale + jnp.sum(weights, axis=-1)
    summed = summed * rescale[..., None] + jnp.einsum(
        "qhk,khd->qhd",
        weights.astype(jnp.bfloat16),
        value_heads,
        preferred_element_type=jnp.float32,
    )
    return (new_max, run_sum, summed)


def normalize(block):
    as_float = block.astype(jnp.float32)
    average = jnp.mean(as_float, axis=-1, keepdims=True)
    centered = as_float - average
    variance = jnp.mean(centered * centered, axis=-1, keepdims=True)
    inv_scale = lax.rsqrt(variance + 1e-05)
    return (centered * inv_scale, inv_scale)


def convolve(conv_in, kernel_all, bias_all, out_rows):
    pre_act = bias_all + jnp.zeros((out_rows, conv_in.shape[1]), jnp.float32)
    for tap_index in range(TAPS):
        pre_act = pre_act + kernel_all[tap_index] * conv_in[tap_index : tap_index + out_rows]
    return pre_act


def live_of(positions, valid_len):
    return ((positions >= 0) & (positions < valid_len)).astype(jnp.float32)[:, None]


def general_shards(
    query_in,
    key_in,
    value_in,
    utt_lengths,
    frames_in,
    out_weight,
    conv_kernel,
    conv_bias,
    ln_gain,
    cotangent,
):
    row_count = query_in.shape[1]
    feat_width = query_in.shape[2]
    head_count = feat_width // HD
    valid_len = utt_lengths[0]
    ctx_count = lax.axis_size("ctx")
    row_offset = lax.axis_index("ctx") * row_count
    half_taps = TAPS // 2
    query_heads = query_in[0].reshape(row_count, head_count, HD)
    start_state = (
        jnp.full((row_count, head_count), NEG_FILL, jnp.float32),
        jnp.zeros((row_count, head_count), jnp.float32),
        jnp.zeros((row_count, head_count, HD), jnp.float32),
    )
    state = start_state
    first_row = jnp.int32(0)
    key_part = lax.all_gather(key_in, "ctx", axis=1, tiled=True)
    value_part = lax.all_gather(value_in, "ctx", axis=1, tiled=True)
    piece_rows = key_part.shape[1]
    block_len = math.gcd(piece_rows, 512)
    for block_start in range(0, piece_rows, block_len):
        key_heads = key_part[0, block_start : block_start + block_len].reshape(
            block_len, head_count, HD
        )
        value_heads = value_part[0, block_start : block_start + block_len].reshape(
            block_len, head_count, HD
        )
        state = absorb_block(
            state, query_heads, key_heads, value_heads, first_row + block_start, valid_len
        )
    run_max, run_sum, summed = state
    attended = (summed / run_sum[..., None]).reshape(row_count, feat_width).astype(jnp.bfloat16)
    projected = jnp.dot(
        attended,
        lax.all_gather(out_weight, "fsdp", axis=1, tiled=True),
        preferred_element_type=jnp.float32,
    )
    hidden = (frames_in[0].astype(jnp.float32) + projected).astype(jnp.bfloat16)
    kernel_all, bias_all, gain_all = (
        lax.all_gather(conv_kernel, "fsdp", axis=1, tiled=True),
        lax.all_gather(conv_bias, "fsdp", axis=0, tiled=True),
        lax.all_gather(ln_gain, "fsdp", axis=0, tiled=True),
    )
    grad_in = cotangent[0].astype(jnp.float32)
    live_mask = live_of(row_offset + jnp.arange(row_count), valid_len)
    widened = extended(hidden, (("ctx", 0),), half_taps)
    normed_ext, inv_ext = normalize(widened)
    conv_in = (
        live_of(row_offset - half_taps + jnp.arange(row_count + 2 * half_taps), valid_len)
        * normed_ext
        * gain_all
    )
    pre_act = convolve(conv_in, kernel_all, bias_all, row_count)
    gate_val = jax.nn.sigmoid(pre_act)
    grad_pre = grad_in * live_mask * gate_val * (1.0 + pre_act * (1.0 - gate_val))
    grad_wide = extended(grad_pre.astype(jnp.bfloat16), (("ctx", 0),), half_taps).astype(
        grad_pre.dtype
    )
    normed = normed_ext[half_taps : half_taps + row_count]
    inv_scale = inv_ext[half_taps : half_taps + row_count]
    block_out = (hidden.astype(jnp.float32) + live_mask * pre_act * gate_val).astype(jnp.bfloat16)
    grad_conv = jnp.zeros((row_count, grad_pre.shape[1]), jnp.float32)
    kernel_rows = []
    for tap_index in range(TAPS):
        back = 2 * half_taps - tap_index
        grad_conv = grad_conv + kernel_all[tap_index] * grad_wide[back : back + row_count]
        kernel_rows.append(jnp.sum(grad_pre * conv_in[tap_index : tap_index + row_count], axis=0))
    grad_conv = live_mask * grad_conv
    grad_hat = grad_conv * gain_all
    first_mean = jnp.mean(grad_hat, axis=-1, keepdims=True)
    second_mean = jnp.mean(grad_hat * normed, axis=-1, keepdims=True)
    hidden_grad = (grad_in + (grad_hat - first_mean - normed * second_mean) * inv_scale).astype(
        jnp.bfloat16
    )
    factor = 1.0 / math.sqrt(lax.axis_size("fsdp") * lax.axis_size("dp") * row_count * ctx_count)
    kernel_term = jnp.stack(kernel_rows) * factor
    bias_term = (jnp.sum(grad_pre, axis=0) * factor)[None]
    gain_term = (jnp.sum(grad_conv * normed, axis=0) * factor)[None]
    shares = (
        lax.psum_scatter(
            kernel_term.astype(jnp.bfloat16), "fsdp", scatter_dimension=1, tiled=True
        ).astype(jnp.float32),
        lax.psum_scatter(
            bias_term.astype(jnp.bfloat16), "fsdp", scatter_dimension=1, tiled=True
        ).astype(jnp.float32),
        lax.psum_scatter(
            gain_term.astype(jnp.bfloat16), "fsdp", scatter_dimension=1, tiled=True
        ).astype(jnp.float32),
    )
    totals = lax.psum((shares[0], shares[1], shares[2]), ("ctx", "dp"))
    return (block_out[None], hidden_grad[None], totals[0], totals[1][0], totals[2][0])


def fits_fast(mesh, blocks):
    query_in, frames_in, out_weight = blocks[0], blocks[4], blocks[5]
    ctx_count = mesh.shape["ctx"]
    rows, width = query_in.shape[1], query_in.shape[2]
    return (
        query_in.shape[0] == 1
        and mesh.shape["fsdp"] == 2
        and mesh.shape["dp"] == 2
        and ctx_count == 4
        and width == ctx_count * SHARE
        and rows == LANES
        and frames_in.shape[2] == 2 * out_weight.shape[1]
        and out_weight.shape[1] % SHARE == 0
    )


def facing(count, step):
    return [(i, i ^ step) for i in range(count)]


PIECES = [(1, 0)] + [(step, chunk) for chunk in range(CHUNKS) for step in (2, 3)]


def pack_kernel(*refs):
    (
        query_ref, key_ref, value_ref, frames_ref, cotan_ref, weight_ref, taps_ref, bias_ref, gain_ref,
        *outs,
    ) = refs[: 9 + len(PIECES) + 2]
    whole, edges, taps, bias, gain, in_sems = refs[-6:]
    *outs, edge, weight_out = outs
    place, core = lax.axis_index("ctx"), lax.axis_index("dp")
    rows = query_ref.shape[1]
    depth = weight_out.shape[0] - 2 * PARAM_ROWS
    arriving = []

    def fetch(source, target):
        arriving.append(pltpu.make_async_copy(source, target, in_sems.at[len(arriving)]))
        arriving[-1].start()

    per_input = rows // NEAR // 2
    for which, source in enumerate((query_ref, key_ref, value_ref)):
        for part in range(per_input):
            span = slice(part * 2 * NEAR, (part + 1) * 2 * NEAR)
            fetch(source.at[0, span, :], whole.at[which, span, :])
    odd = lax.rem(place, 2)
    for side in range(2):
        high = odd if side else 1 - odd
        wide = pl.multiple_of(high * (rows - WIDE), WIDE)
        near = pl.multiple_of(high * (rows - NEAR), NEAR)
        fetch(frames_ref.at[0, pl.ds(wide, WIDE), :], edges.at[side, 0:WIDE, :])
        fetch(cotan_ref.at[0, pl.ds(near, NEAR), :], edges.at[side, WIDE : WIDE + NEAR, :])
    for part in range(0, depth, 64):
        first = pl.multiple_of(core * depth + part, 64)
        fetch(weight_ref.at[pl.ds(first, 64), :], weight_out.at[part : part + 64, :])
    for source, target in ((taps_ref, taps), (bias_ref, bias), (gain_ref, gain)):
        fetch(source, target)
    for which in range(3):
        for part in range(per_input):
            arriving[which * per_input + part].wait()
        at = slice(which * rows, (which + 1) * rows)
        for out, (step, chunk) in zip(outs, PIECES):
            first = (place ^ step) * SHARE + chunk * LANES
            size = out.shape[1]
            out[at, :] = whole[which, :, pl.ds(pl.multiple_of(first, LANES), size)]
    seen = 3 * per_input
    for copy in arriving[seen : seen + 4]:
        copy.wait()
    for block in range(edges.shape[2] // SHARE):
        base = 3 * rows + block * (WIDE + NEAR)
        outs[0][base : base + WIDE + NEAR, :] = edges[0, :, block * SHARE : (block + 1) * SHARE]
    edge[...] = edges[1]
    for copy in arriving[-3:]:
        copy.wait()
    params = parameters(taps, bias, gain)
    rounded = params.astype(jnp.bfloat16)
    weight_out[depth : depth + PARAM_ROWS, :] = rounded
    weight_out[depth + PARAM_ROWS :, :] = (params - rounded.astype(jnp.float32)).astype(jnp.bfloat16)
    for copy in arriving[seen + 4 : -3]:
        copy.wait()


def parameters(taps_ref, bias_ref, gain_ref):
    half = taps_ref.shape[1]
    return jnp.concatenate(
        [
            taps_ref[...],
            bias_ref[...].reshape(1, half),
            gain_ref[...].reshape(1, half),
            jnp.zeros((PARAM_ROWS - TAPS - 2, half), jnp.float32),
        ],
        axis=0,
    )


def attend_kernel(chunk, length_ref, query_ref, key_ref, value_ref, *refs):
    parts, refs = refs[:3], refs[3:]
    before, refs = refs[: 4 * chunk], refs[4 * chunk :]
    outs = refs[:4]
    query_all, key_all, value_all, attended, sems = refs[4:]
    place, valid_len = lax.axis_index("ctx"), length_ref[0]
    frames, width = query_all.shape
    rows = frames // 4
    targets = (query_all, key_all, value_all)
    mine = pl.ds(pl.multiple_of(place * rows, rows), rows)
    heads = pl.ds(pl.multiple_of(place * SHARE + chunk * LANES, LANES), LANES)
    copies = [
        pltpu.make_async_copy(source.at[0, :, heads], target.at[mine, :], sems.at[which])
        for which, (source, target) in enumerate(zip((query_ref, key_ref, value_ref), targets))
    ]
    for copy in copies:
        copy.start()
    for step, part in enumerate(parts, 1):
        span = pl.ds(pl.multiple_of((place ^ step) * rows, rows), rows)
        for which, target in enumerate(targets):
            cols = slice(chunk * LANES, (chunk + 1) * LANES) if step == 1 else slice(None)
            target[span, :] = part[which * rows : (which + 1) * rows, cols]
    for copy in copies:
        copy.wait()
    attended[0:WIDE, :] = jnp.zeros((WIDE, width), attended.dtype)
    attended[WIDE + frames : 2 * WIDE + frames, :] = jnp.zeros((WIDE, width), attended.dtype)
    usable = lax.broadcasted_iota(jnp.int32, (1, frames), 1) < valid_len
    lane = lax.broadcasted_iota(jnp.int32, (1, LANES), 1)
    for pair in range(width // LANES):
        cols = slice(pair * LANES, (pair + 1) * LANES)
        keys, values = key_all[:, cols], value_all[:, cols]
        heads = [
            (jnp.where(mine, keys, 0).astype(keys.dtype), jnp.where(mine, values, 0).astype(values.dtype))
            for mine in (lane < HD, lane >= HD)
        ]
        for start in range(0, frames, QUERY_ROWS):
            queries = query_all[start : start + QUERY_ROWS, cols]
            total = jnp.zeros((QUERY_ROWS, LANES), jnp.float32)
            for key_head, value_head in heads:
                scores = lax.dot_general(
                    queries, key_head, (((1,), (1,)), ((), ())), preferred_element_type=jnp.float32
                ) * (1.0 / math.sqrt(HD))
                scores = jnp.where(usable, scores, NEG_FILL)
                weights = jnp.exp(scores - jnp.max(scores, axis=1, keepdims=True))
                sums = jnp.sum(weights, axis=1, keepdims=True)
                total += (
                    jnp.dot(
                        weights.astype(jnp.bfloat16), value_head, preferred_element_type=jnp.float32
                    )
                    / sums
                )
            attended[WIDE + start : WIDE + start + QUERY_ROWS, cols] = total.astype(attended.dtype)
    for step in range(4):
        owner = place ^ step
        found = attended[pl.ds(pl.multiple_of(owner * rows, rows), rows + 2 * WIDE), :]
        if chunk:
            outs[step][:, :LANES] = before[step][...]
            outs[step][:, LANES:] = found
        else:
            outs[step][...] = found


def by_residue(first, last):
    return [[o for o in range(first, last + 1) if o % 8 == r] for r in range(8)]


def live_at(length_ref, rows, first, length):
    position = lax.axis_index("ctx") * rows + first + lax.broadcasted_iota(jnp.int32, (length, 1), 0)
    return ((position >= 0) & (position < length_ref[0])).astype(jnp.float32)


def weight_block(w_own, w_near, w_far, part, tile, mine):
    cols = slice(tile * LANES, (tile + 1) * LANES)
    if mine:
        return w_own[pl.ds(pl.multiple_of(part * SHARE, SHARE), SHARE), cols]
    per_part = (w_near.shape[0] - 2 * PARAM_ROWS) // SHARE
    rows = pl.ds(pl.multiple_of(lax.rem(part, per_part) * SHARE, SHARE), SHARE)
    near = lax.div(part, per_part) == lax.axis_index("dp")
    return jnp.where(near, w_near[rows, cols], w_far[rows, cols])


def prepare_kernel(*refs):
    (
        length_ref, own_ref, frames_ref, cotan_ref, beside_ref, edge_ref, w_own, w_near, w_far,
        taps_ref, bias_ref, gain_ref, base, cotan_live, params, par_mine, edges,
    ) = refs
    place, side = lax.axis_index("ctx"), lax.axis_index("fsdp")
    rows, features = frames_ref.shape
    half_tiles = features // 2 // LANES
    weight_rows = w_near.shape[0] - 2 * PARAM_ROWS
    even = 1 - lax.rem(place, 2)
    for block in range(features // SHARE):
        first = 3 * rows + block * (WIDE + NEAR)
        edges[even, :, block * SHARE : (block + 1) * SHARE] = beside_ref[first : first + WIDE + NEAR, :]
    edges[1 - even] = edge_ref[...]
    par_own = parameters(taps_ref, bias_ref, gain_ref)
    par_mine[...] = par_own
    par_other = w_near[weight_rows : weight_rows + PARAM_ROWS, :].astype(jnp.float32)
    par_other += w_near[weight_rows + PARAM_ROWS :, :].astype(jnp.float32)
    live_near = live_at(length_ref, rows, -NEAR, rows + 2 * NEAR)
    own = own_ref[...]
    row = lax.broadcasted_iota(jnp.int32, (PARAM_ROWS, 1), 0)
    for tile in range(half_tiles):
        cols = slice(tile * LANES, (tile + 1) * LANES)
        for mine, source in ((True, par_own), (False, par_other)):
            at = (side if mine else 1 - side) * half_tiles + tile
            values = source[:, cols]
            params[at] = jnp.where(row < TAPS, values * values[TAPS + 1 : TAPS + 2], values)
            span = pl.ds(pl.multiple_of(at * LANES, LANES), LANES)
            weight = weight_block(w_own, w_near, w_far, place, tile, mine)
            base[at] = jnp.dot(own, weight, preferred_element_type=jnp.float32) + jnp.concatenate(
                [edges[0, 0:WIDE, span], frames_ref[:, span], edges[1, 0:WIDE, span]], axis=0
            ).astype(jnp.float32)
            cotan_live[at] = live_near * jnp.concatenate(
                [edges[0, WIDE:, span], cotan_ref[:, span], edges[1, WIDE:, span]], axis=0
            ).astype(jnp.float32)


def module_kernel(*refs):
    (
        length_ref, reply_one, reply_two, reply_three, base, cotan_live, params, w_own, w_near, w_far,
        block_hbm, normed, wide_grad, inv_rows, sums_own, sums_other,
        sums, partial, block_out, out_sems,
    ) = refs
    place, side = lax.axis_index("ctx"), lax.axis_index("fsdp")
    tiles, ext = base.shape[:2]
    rows, features = ext - 2 * WIDE, tiles * LANES
    half_tiles, near = tiles // 2, rows + 2 * NEAR
    for tile in range(half_tiles):
        for mine in (True, False):
            at = (side if mine else 1 - side) * half_tiles + tile
            span = pl.ds(pl.multiple_of(at * LANES, LANES), LANES)
            product = base[at]
            for step, reply in enumerate((reply_one, reply_two, reply_three), 1):
                weight = weight_block(w_own, w_near, w_far, place ^ step, tile, mine)
                product += jnp.dot(reply[...], weight, preferred_element_type=jnp.float32)
            hidden = product.astype(jnp.bfloat16)
            block_out[:, span] = hidden[WIDE : WIDE + rows]
            normed[at, 0:ext] = hidden.astype(jnp.float32)

    total = normed[0, 0:ext]
    for tile in range(1, tiles):
        total += normed[tile, 0:ext]
    average = jnp.sum(total, axis=1, keepdims=True) * (1.0 / features)
    total = jnp.zeros((ext, LANES), jnp.float32)
    for tile in range(tiles):
        centered = normed[tile, 0:ext] - average
        total += centered * centered
    variance = jnp.sum(total, axis=1, keepdims=True) * (1.0 / features)
    inv_scale = lax.rsqrt(variance + 1e-05)
    scale = inv_scale * live_at(length_ref, rows, -WIDE, ext)
    for tile in range(tiles):
        normed[tile, 0:ext] = (normed[tile, 0:ext] - average) * scale

    live_rows = live_at(length_ref, rows, 0, rows)
    inv_rows[...] = jnp.broadcast_to(inv_scale[WIDE : WIDE + rows], inv_rows.shape)

    def one_tile(tile, carry):
        span = pl.ds(pl.multiple_of(tile * LANES, LANES), LANES)
        pre_act = jnp.broadcast_to(params[tile, TAPS : TAPS + 1], (near, LANES))
        for rest, offsets in enumerate(by_residue(1, TAPS)):
            shifted = normed[tile, rest : rest + near + 24]
            for offset in offsets:
                at = offset - rest
                pre_act += params[tile, offset - 1 : offset] * shifted[at : at + near]
        gate = jax.nn.sigmoid(pre_act)
        here = slice(NEAR, NEAR + rows)
        block_out[:, span] = (
            block_out[:, span].astype(jnp.float32) + live_rows * (pre_act * gate)[here]
        ).astype(block_out.dtype)
        pltpu.make_async_copy(
            block_out.at[:, span], block_hbm.at[:, span], out_sems.at[tile]
        ).start()
        grad_pre = cotan_live[tile] * gate * (1.0 + pre_act * (1.0 - gate))
        wide_grad[tile, 0:near] = grad_pre
        own_grad = grad_pre[here]
        first = WIDE - HALF
        for rest, offsets in enumerate(by_residue(first, first + TAPS - 1)):
            low = offsets[0]
            shifted = normed[tile, low : low + rows + 24]
            for offset in offsets:
                at = offset - low
                partial[offset - first] = jnp.sum(
                    (own_grad * shifted[at : at + rows]).reshape(rows // 8, 8, LANES), axis=0
                )
        partial[TAPS] = jnp.sum(own_grad.reshape(rows // 8, 8, LANES), axis=0)
        sums[tile] = jnp.sum(partial[...], axis=1)
        return carry

    lax.fori_loop(0, tiles, one_tile, 0, unroll=2)
    for tile in range(half_tiles):
        cols = slice(tile * LANES, (tile + 1) * LANES)
        sums_own[:, cols] = sums[side * half_tiles + tile].astype(sums_own.dtype)
        sums_other[:, cols] = sums[(1 - side) * half_tiles + tile].astype(sums_other.dtype)
    for tile in range(tiles):
        cols = slice(tile * LANES, (tile + 1) * LANES)
        pltpu.make_async_copy(block_out.at[:, cols], block_hbm.at[:, cols], out_sems.at[tile]).wait()


def backward_kernel(length_ref, normed, wide_grad, params, grad_hat, means, mean_one, mean_two):
    tiles, rows = grad_hat.shape[:2]
    live_rows = live_at(length_ref, rows, 0, rows)
    mean_one[...] = jnp.zeros_like(mean_one)
    mean_two[...] = jnp.zeros_like(mean_two)

    def one_tile(tile, carry):
        grad = jnp.zeros((rows, LANES), jnp.float32)
        for rest, offsets in enumerate(by_residue(1, TAPS)):
            shifted = wide_grad[tile, rest : rest + rows + 24]
            for offset in offsets:
                at = offset - rest
                tap = TAPS - offset
                grad += params[tile, tap : tap + 1] * shifted[at : at + rows]
        grad = live_rows * grad
        grad_hat[tile] = grad
        mean_one[...] += grad
        mean_two[...] += grad * normed[tile, WIDE : WIDE + rows]
        return carry

    lax.fori_loop(0, tiles, one_tile, 0, unroll=2)
    for index, total in enumerate((mean_one, mean_two)):
        mean = jnp.sum(total[...], axis=1, keepdims=True) * (1.0 / (tiles * LANES))
        means[index] = jnp.broadcast_to(mean, (rows, LANES))


def hidden_grad_kernel(cotan_ref, normed, inv_rows, grad_hat, means, grad_hbm, hidden_grad, out_sems):
    tiles, rows = grad_hat.shape[:2]
    copies = []
    for tile in range(tiles):
        cols = slice(tile * LANES, (tile + 1) * LANES)
        inner = grad_hat[tile] - means[0] - normed[tile, WIDE : WIDE + rows] * means[1]
        hidden_grad[:, cols] = (
            cotan_ref[:, cols].astype(jnp.float32) + inner * inv_rows[...]
        ).astype(hidden_grad.dtype)
        copies.append(
            pltpu.make_async_copy(hidden_grad.at[:, cols], grad_hbm.at[:, cols], out_sems.at[tile])
        )
        copies[-1].start()
    for copy in copies:
        copy.wait()


def finish_kernel(factor, mine, one, two, three, params, kernel_out, bias_out, gain_out, terms):
    place = lax.axis_index("ctx")
    for step, source in enumerate((mine, one, two, three)):
        terms[place ^ step] = source[...].astype(jnp.float32)
    total = (((terms[0] + terms[1]) + terms[2]) + terms[3]) * factor
    kernel_out[...] = total[:TAPS] * params[TAPS + 1 : TAPS + 2]
    bias_out[...] = total[TAPS]
    gain_out[...] = jnp.sum(total[:TAPS] * params[:TAPS], axis=0)


def fast_shards(
    query_in,
    key_in,
    value_in,
    utt_lengths,
    frames_in,
    out_weight,
    conv_kernel,
    conv_bias,
    ln_gain,
    cotangent,
):
    count = lax.axis_size("ctx")
    rows, width = query_in.shape[1], query_in.shape[2]
    features, half = frames_in.shape[2], out_weight.shape[1]
    place = lax.axis_index("ctx")
    vmem = pl.BlockSpec(memory_space=pltpu.VMEM)
    smem = pl.BlockSpec(memory_space=pltpu.SMEM)
    hbm = pl.BlockSpec(memory_space=pltpu.HBM)
    swap = [(0, 1), (1, 0)]

    ends = (features // SHARE) * (WIDE + NEAR)
    sent = [
        (3 * rows + ends, SHARE),
        *[(3 * rows, LANES)] * (len(PIECES) - 1),
        (WIDE + NEAR, features),
        (width // 2 + 2 * PARAM_ROWS, half),
    ]
    *pieces, edge, w_sent = pl.pallas_call(
        pack_kernel,
        name="pack",
        out_shape=[jax.ShapeDtypeStruct(shape, jnp.bfloat16) for shape in sent],
        in_specs=[hbm] * 9,
        out_specs=[vmem] * len(sent),
        scratch_shapes=[
            pltpu.VMEM((3, rows, width), jnp.bfloat16),
            pltpu.VMEM((2, WIDE + NEAR, features), jnp.bfloat16),
            pltpu.VMEM((TAPS, half), jnp.float32),
            pltpu.VMEM((half,), jnp.float32),
            pltpu.VMEM((half,), jnp.float32),
            pltpu.SemaphoreType.DMA((32,)),
        ],
        compiler_params=pltpu.CompilerParams(vmem_limit_bytes=32 << 20),
    )(
        *(
            pltpu.with_memory_space_constraint(one, pltpu.HBM)
            for one in (
                query_in,
                key_in,
                value_in,
                frames_in,
                cotangent,
                out_weight,
                conv_kernel,
                conv_bias,
                ln_gain,
            )
        )
    )
    parts = [
        lax.ppermute(one, "ctx", facing(count, step)) for one, (step, _) in zip(pieces, PIECES)
    ]
    edge = lax.ppermute(edge, "ctx", [(1, 2), (2, 1)])
    w_near = lax.ppermute(w_sent, "fsdp", swap)

    attended = []
    for chunk in range(CHUNKS):
        ready = [parts[0], *parts[2 * chunk + 1 : 2 * chunk + 3]]
        before = []
        if chunk:
            before = attended
            ready, edge = lax.optimization_barrier((ready, edge))
        attended = pl.pallas_call(
            functools.partial(attend_kernel, chunk),
            name="attend",
            out_shape=[
                jax.ShapeDtypeStruct((rows + 2 * WIDE, (chunk + 1) * LANES), jnp.bfloat16)
            ]
            * count,
            in_specs=[smem] + [hbm] * 3 + [vmem] * (3 + len(before)),
            out_specs=[vmem] * count,
            scratch_shapes=[pltpu.VMEM((count * rows, LANES), jnp.bfloat16)] * 3
            + [pltpu.VMEM((count * rows + 2 * WIDE, LANES), jnp.bfloat16)]
            + [pltpu.SemaphoreType.DMA((3,))],
            compiler_params=pltpu.CompilerParams(vmem_limit_bytes=40 << 20),
            cost_estimate=pl.CostEstimate(flops=1, bytes_accessed=1, transcendentals=0),
        )(utt_lengths, query_in, key_in, value_in, *ready, *before)
    own, *replies = [
        reply if step == 0 else lax.ppermute(reply, "ctx", facing(count, step))
        for step, reply in enumerate(attended)
    ]
    _, w_near = lax.optimization_barrier((attended, w_near))
    w_far = lax.ppermute(w_near, "dp", swap)
    frames, cotan = frames_in[0], cotangent[0]

    ext, near = rows + 2 * WIDE, rows + 2 * NEAR
    tiles = features // LANES
    base, cotan_live, params, par_mine = pl.pallas_call(
        prepare_kernel,
        name="prepare",
        out_shape=[
            jax.ShapeDtypeStruct((tiles, ext, LANES), jnp.float32),
            jax.ShapeDtypeStruct((tiles, near, LANES), jnp.float32),
            jax.ShapeDtypeStruct((tiles, PARAM_ROWS, LANES), jnp.float32),
            jax.ShapeDtypeStruct((PARAM_ROWS, half), jnp.float32),
        ],
        in_specs=[smem] + [vmem] * 11,
        out_specs=[vmem] * 4,
        scratch_shapes=[pltpu.VMEM((2, WIDE + NEAR, features), jnp.bfloat16)],
        compiler_params=pltpu.CompilerParams(vmem_limit_bytes=32 << 20),
        cost_estimate=pl.CostEstimate(
            flops=2 * ext * SHARE * features, bytes_accessed=8 * rows * features, transcendentals=0
        ),
    )(
        utt_lengths,
        own,
        frames,
        cotan,
        parts[0],
        edge,
        out_weight,
        w_near,
        w_far,
        conv_kernel,
        conv_bias,
        ln_gain,
    )
    block_out, normed, wide_grad, inv_rows, sums_own, sums_other = pl.pallas_call(
        module_kernel,
        name="conv_module",
        out_shape=[
            jax.ShapeDtypeStruct((rows, features), jnp.bfloat16),
            jax.ShapeDtypeStruct((tiles, ext + 8, LANES), jnp.float32),
            jax.ShapeDtypeStruct((tiles, near + 8, LANES), jnp.float32),
            jax.ShapeDtypeStruct((rows, LANES), jnp.float32),
            jax.ShapeDtypeStruct((TAPS + 1, half), jnp.bfloat16),
            jax.ShapeDtypeStruct((TAPS + 1, half), jnp.bfloat16),
        ],
        in_specs=[smem] + [vmem] * 9,
        out_specs=[hbm] + [vmem] * 5,
        scratch_shapes=[
            pltpu.VMEM((tiles, TAPS + 1, LANES), jnp.float32),
            pltpu.VMEM((TAPS + 1, 8, LANES), jnp.float32),
            pltpu.VMEM((rows, features), jnp.bfloat16),
            pltpu.SemaphoreType.DMA((tiles,)),
        ],
        compiler_params=pltpu.CompilerParams(vmem_limit_bytes=32 << 20),
        cost_estimate=pl.CostEstimate(
            flops=2 * ext * width * features + 4 * TAPS * rows * features,
            bytes_accessed=2 * width * features + 12 * rows * features,
            transcendentals=near * features,
        ),
    )(
        utt_lengths,
        *replies,
        base,
        cotan_live,
        params,
        out_weight,
        w_near,
        w_far,
    )

    pairs = [
        lax.ppermute(sums_other, "fsdp", swap),
        lax.ppermute(sums_other, ("fsdp", "dp"), [(0, 3), (3, 0), (1, 2), (2, 1)]),
        lax.ppermute(sums_own, "dp", swap),
    ]
    grad_hat, means = pl.pallas_call(
        backward_kernel,
        name="conv_backward",
        out_shape=[
            jax.ShapeDtypeStruct((tiles, rows, LANES), jnp.float32),
            jax.ShapeDtypeStruct((2, rows, LANES), jnp.float32),
        ],
        in_specs=[smem] + [vmem] * 3,
        out_specs=[vmem] * 2,
        scratch_shapes=[pltpu.VMEM((rows, LANES), jnp.float32)] * 2,
        compiler_params=pltpu.CompilerParams(vmem_limit_bytes=32 << 20),
        cost_estimate=pl.CostEstimate(
            flops=2 * TAPS * rows * features,
            bytes_accessed=12 * rows * features,
            transcendentals=0,
        ),
    )(utt_lengths, normed, wide_grad, params)
    pairs, grad_hat = lax.optimization_barrier((pairs, grad_hat))
    across_x, diagonal, sibling = (one.astype(jnp.float32) for one in pairs)
    found = (sums_own.astype(jnp.float32) + sibling) + (across_x + diagonal)
    found = found.astype(jnp.bfloat16)
    arrived = [lax.ppermute(found, "ctx", facing(count, step)) for step in range(1, count)]
    hidden_grad = pl.pallas_call(
        hidden_grad_kernel,
        name="hidden_grad",
        out_shape=jax.ShapeDtypeStruct((rows, features), jnp.bfloat16),
        in_specs=[vmem] * 5,
        out_specs=hbm,
        scratch_shapes=[
            pltpu.VMEM((rows, features), jnp.bfloat16),
            pltpu.SemaphoreType.DMA((tiles,)),
        ],
        compiler_params=pltpu.CompilerParams(vmem_limit_bytes=32 << 20),
        cost_estimate=pl.CostEstimate(
            flops=6 * rows * features, bytes_accessed=12 * rows * features, transcendentals=0
        ),
    )(cotan, normed, inv_rows, grad_hat, means)
    arrived, hidden_grad = lax.optimization_barrier((arrived, hidden_grad))
    factor = 1.0 / math.sqrt(lax.axis_size("fsdp") * lax.axis_size("dp") * rows * count)
    grad_kernel, grad_bias, grad_gain = pl.pallas_call(
        functools.partial(finish_kernel, factor),
        name="finish",
        out_shape=[
            jax.ShapeDtypeStruct((TAPS, half), jnp.float32),
            jax.ShapeDtypeStruct((half,), jnp.float32),
            jax.ShapeDtypeStruct((half,), jnp.float32),
        ],
        in_specs=[vmem] * 5,
        out_specs=[vmem] * 3,
        scratch_shapes=[pltpu.VMEM((count, TAPS + 1, half), jnp.float32)],
        compiler_params=pltpu.CompilerParams(vmem_limit_bytes=32 << 20),
    )(found, *arrived, par_mine)
    return (block_out[None], hidden_grad[None], grad_kernel, grad_bias, grad_gain)


def solution(mesh):
    in_specs = (
        P(("groups", "fsdp", "dp"), "ctx", None),
        P(("groups", "fsdp", "dp"), "ctx", None),
        P(("groups", "fsdp", "dp"), "ctx", None),
        P(("groups", "fsdp", "dp")),
        P(("groups", "fsdp", "dp"), "ctx", None),
        P(None, "fsdp"),
        P(None, "fsdp"),
        P("fsdp"),
        P("fsdp"),
        P(("groups", "fsdp", "dp"), "ctx", None),
    )
    out_specs = (
        P(("groups", "fsdp", "dp"), "ctx", None),
        P(("groups", "fsdp", "dp"), "ctx", None),
        P("groups", "fsdp"),
        P(("groups", "fsdp")),
        P(("groups", "fsdp")),
    )

    def shards(*blocks):
        run = fast_shards if fits_fast(mesh, blocks) else general_shards
        return run(*blocks)

    return jax.shard_map(shards, mesh=mesh, in_specs=in_specs, out_specs=out_specs, check_vma=False)
```

```python
import functools
import math

import jax
import jax.numpy as jnp
from jax import lax
from jax.experimental import pallas as pl
from jax.experimental.pallas import tpu as pltpu
from jax.sharding import PartitionSpec as P

HD = 64
TAPS = 31
HALF = TAPS // 2
LANES = 128
WIDE = 32
NEAR = 16
PARAM_ROWS = 40
SHARE = 256
QUERY_ROWS = 128
CHUNKS = SHARE // LANES

NEG_FILL = -1e30


def extended(block, sides, width):
    for axis, dim in sides:
        count = lax.axis_size(axis)
        forward = [(i, i + 1) for i in range(count - 1)]
        backward = [(target, source) for source, target in forward]
        low = lax.ppermute(
            lax.slice_in_dim(block, block.shape[dim] - width, None, axis=dim), axis, forward
        )
        high = lax.ppermute(lax.slice_in_dim(block, 0, width, axis=dim), axis, backward)
        block = jnp.concatenate([low, block, high], axis=dim)
    return block


def absorb_block(state, query_heads, key_heads, value_heads, key_start, valid_len):
    run_max, run_sum, summed = state
    scores = jnp.einsum(
        "qhd,khd->qhk", query_heads, key_heads, preferred_element_type=jnp.float32
    ) * (1.0 / math.sqrt(HD))
    usable = key_start + jnp.arange(key_heads.shape[0]) < valid_len
    scores = jnp.where(usable, scores, NEG_FILL)
    new_max = jnp.maximum(run_max, jnp.max(scores, axis=-1))
    rescale = jnp.exp(run_max - new_max)
    weights = jnp.where(usable, jnp.exp(scores - new_max[..., None]), 0.0)
    run_sum = run_sum * rescale + jnp.sum(weights, axis=-1)
    summed = summed * rescale[..., None] + jnp.einsum(
        "qhk,khd->qhd",
        weights.astype(jnp.bfloat16),
        value_heads,
        preferred_element_type=jnp.float32,
    )
    return (new_max, run_sum, summed)


def normalize(block):
    as_float = block.astype(jnp.float32)
    average = jnp.mean(as_float, axis=-1, keepdims=True)
    centered = as_float - average
    variance = jnp.mean(centered * centered, axis=-1, keepdims=True)
    inv_scale = lax.rsqrt(variance + 1e-05)
    return (centered * inv_scale, inv_scale)


def convolve(conv_in, kernel_all, bias_all, out_rows):
    pre_act = bias_all + jnp.zeros((out_rows, conv_in.shape[1]), jnp.float32)
    for tap_index in range(TAPS):
        pre_act = pre_act + kernel_all[tap_index] * conv_in[tap_index : tap_index + out_rows]
    return pre_act


def live_of(positions, valid_len):
    return ((positions >= 0) & (positions < valid_len)).astype(jnp.float32)[:, None]


def general_shards(
    query_in,
    key_in,
    value_in,
    utt_lengths,
    frames_in,
    out_weight,
    conv_kernel,
    conv_bias,
    ln_gain,
    cotangent,
):
    row_count = query_in.shape[1]
    feat_width = query_in.shape[2]
    head_count = feat_width // HD
    valid_len = utt_lengths[0]
    ctx_count = lax.axis_size("ctx")
    row_offset = lax.axis_index("ctx") * row_count
    half_taps = TAPS // 2
    query_heads = query_in[0].reshape(row_count, head_count, HD)
    start_state = (
        jnp.full((row_count, head_count), NEG_FILL, jnp.float32),
        jnp.zeros((row_count, head_count), jnp.float32),
        jnp.zeros((row_count, head_count, HD), jnp.float32),
    )
    state = start_state
    first_row = jnp.int32(0)
    key_part = lax.all_gather(key_in, "ctx", axis=1, tiled=True)
    value_part = lax.all_gather(value_in, "ctx", axis=1, tiled=True)
    piece_rows = key_part.shape[1]
    block_len = math.gcd(piece_rows, 512)
    for block_start in range(0, piece_rows, block_len):
        key_heads = key_part[0, block_start : block_start + block_len].reshape(
            block_len, head_count, HD
        )
        value_heads = value_part[0, block_start : block_start + block_len].reshape(
            block_len, head_count, HD
        )
        state = absorb_block(
            state, query_heads, key_heads, value_heads, first_row + block_start, valid_len
        )
    run_max, run_sum, summed = state
    attended = (summed / run_sum[..., None]).reshape(row_count, feat_width).astype(jnp.bfloat16)
    projected = jnp.dot(
        attended,
        lax.all_gather(out_weight, "fsdp", axis=1, tiled=True),
        preferred_element_type=jnp.float32,
    )
    hidden = (frames_in[0].astype(jnp.float32) + projected).astype(jnp.bfloat16)
    kernel_all, bias_all, gain_all = (
        lax.all_gather(conv_kernel, "fsdp", axis=1, tiled=True),
        lax.all_gather(conv_bias, "fsdp", axis=0, tiled=True),
        lax.all_gather(ln_gain, "fsdp", axis=0, tiled=True),
    )
    grad_in = cotangent[0].astype(jnp.float32)
    live_mask = live_of(row_offset + jnp.arange(row_count), valid_len)
    widened = extended(hidden, (("ctx", 0),), half_taps)
    normed_ext, inv_ext = normalize(widened)
    conv_in = (
        live_of(row_offset - half_taps + jnp.arange(row_count + 2 * half_taps), valid_len)
        * normed_ext
        * gain_all
    )
    pre_act = convolve(conv_in, kernel_all, bias_all, row_count)
    gate_val = jax.nn.sigmoid(pre_act)
    grad_pre = grad_in * live_mask * gate_val * (1.0 + pre_act * (1.0 - gate_val))
    grad_wide = extended(grad_pre.astype(jnp.bfloat16), (("ctx", 0),), half_taps).astype(
        grad_pre.dtype
    )
    normed = normed_ext[half_taps : half_taps + row_count]
    inv_scale = inv_ext[half_taps : half_taps + row_count]
    block_out = (hidden.astype(jnp.float32) + live_mask * pre_act * gate_val).astype(jnp.bfloat16)
    grad_conv = jnp.zeros((row_count, grad_pre.shape[1]), jnp.float32)
    kernel_rows = []
    for tap_index in range(TAPS):
        back = 2 * half_taps - tap_index
        grad_conv = grad_conv + kernel_all[tap_index] * grad_wide[back : back + row_count]
        kernel_rows.append(jnp.sum(grad_pre * conv_in[tap_index : tap_index + row_count], axis=0))
    grad_conv = live_mask * grad_conv
    grad_hat = grad_conv * gain_all
    first_mean = jnp.mean(grad_hat, axis=-1, keepdims=True)
    second_mean = jnp.mean(grad_hat * normed, axis=-1, keepdims=True)
    hidden_grad = (grad_in + (grad_hat - first_mean - normed * second_mean) * inv_scale).astype(
        jnp.bfloat16
    )
    factor = 1.0 / math.sqrt(lax.axis_size("fsdp") * lax.axis_size("dp") * row_count * ctx_count)
    kernel_term = jnp.stack(kernel_rows) * factor
    bias_term = (jnp.sum(grad_pre, axis=0) * factor)[None]
    gain_term = (jnp.sum(grad_conv * normed, axis=0) * factor)[None]
    shares = (
        lax.psum_scatter(
            kernel_term.astype(jnp.bfloat16), "fsdp", scatter_dimension=1, tiled=True
        ).astype(jnp.float32),
        lax.psum_scatter(
            bias_term.astype(jnp.bfloat16), "fsdp", scatter_dimension=1, tiled=True
        ).astype(jnp.float32),
        lax.psum_scatter(
            gain_term.astype(jnp.bfloat16), "fsdp", scatter_dimension=1, tiled=True
        ).astype(jnp.float32),
    )
    totals = lax.psum((shares[0], shares[1], shares[2]), ("ctx", "dp"))
    return (block_out[None], hidden_grad[None], totals[0], totals[1][0], totals[2][0])


def fits_fast(mesh, blocks):
    query_in, frames_in, out_weight = blocks[0], blocks[4], blocks[5]
    ctx_count = mesh.shape["ctx"]
    rows, width = query_in.shape[1], query_in.shape[2]
    return (
        query_in.shape[0] == 1
        and mesh.shape["fsdp"] == 2
        and mesh.shape["dp"] == 2
        and ctx_count == 4
        and width == ctx_count * SHARE
        and rows == LANES
        and frames_in.shape[2] == 2 * out_weight.shape[1]
        and out_weight.shape[1] % SHARE == 0
    )


def facing(count, step):
    return [(i, i ^ step) for i in range(count)]


PIECES = [(1, 0)] + [(step, chunk) for chunk in range(CHUNKS) for step in (2, 3)]


def pack_kernel(*refs):
    (
        query_ref, key_ref, value_ref, frames_ref, cotan_ref, weight_ref, taps_ref, bias_ref, gain_ref,
        *outs,
    ) = refs[: 9 + len(PIECES) + 2]
    whole, edges, taps, bias, gain, in_sems = refs[-6:]
    *outs, edge, weight_out = outs
    place, core = lax.axis_index("ctx"), lax.axis_index("dp")
    rows = query_ref.shape[1]
    depth = weight_out.shape[0] - 2 * PARAM_ROWS
    arriving = []

    def fetch(source, target):
        arriving.append(pltpu.make_async_copy(source, target, in_sems.at[len(arriving)]))
        arriving[-1].start()

    per_input = rows // NEAR // 2
    for which, source in enumerate((query_ref, key_ref, value_ref)):
        for part in range(per_input):
            span = slice(part * 2 * NEAR, (part + 1) * 2 * NEAR)
            fetch(source.at[0, span, :], whole.at[which, span, :])
    odd = lax.rem(place, 2)
    for side in range(2):
        high = odd if side else 1 - odd
        wide = pl.multiple_of(high * (rows - WIDE), WIDE)
        near = pl.multiple_of(high * (rows - NEAR), NEAR)
        fetch(frames_ref.at[0, pl.ds(wide, WIDE), :], edges.at[side, 0:WIDE, :])
        fetch(cotan_ref.at[0, pl.ds(near, NEAR), :], edges.at[side, WIDE : WIDE + NEAR, :])
    for part in range(0, depth, 64):
        first = pl.multiple_of(core * depth + part, 64)
        fetch(weight_ref.at[pl.ds(first, 64), :], weight_out.at[part : part + 64, :])
    for source, target in ((taps_ref, taps), (bias_ref, bias), (gain_ref, gain)):
        fetch(source, target)
    for which in range(3):
        for part in range(per_input):
            arriving[which * per_input + part].wait()
        at = slice(which * rows, (which + 1) * rows)
        for out, (step, chunk) in zip(outs, PIECES):
            first = (place ^ step) * SHARE + chunk * LANES
            size = out.shape[1]
            out[at, :] = whole[which, :, pl.ds(pl.multiple_of(first, LANES), size)]
    seen = 3 * per_input
    for copy in arriving[seen : seen + 4]:
        copy.wait()
    for block in range(edges.shape[2] // SHARE):
        base = 3 * rows + block * (WIDE + NEAR)
        outs[0][base : base + WIDE + NEAR, :] = edges[0, :, block * SHARE : (block + 1) * SHARE]
    edge[...] = edges[1]
    for copy in arriving[-3:]:
        copy.wait()
    params = parameters(taps, bias, gain)
    rounded = params.astype(jnp.bfloat16)
    weight_out[depth : depth + PARAM_ROWS, :] = rounded
    weight_out[depth + PARAM_ROWS :, :] = (params - rounded.astype(jnp.float32)).astype(jnp.bfloat16)
    for copy in arriving[seen + 4 : -3]:
        copy.wait()


def parameters(taps_ref, bias_ref, gain_ref):
    half = taps_ref.shape[1]
    return jnp.concatenate(
        [
            taps_ref[...],
            bias_ref[...].reshape(1, half),
            gain_ref[...].reshape(1, half),
            jnp.zeros((PARAM_ROWS - TAPS - 2, half), jnp.float32),
        ],
        axis=0,
    )


def attend_kernel(chunk, length_ref, query_ref, key_ref, value_ref, *refs):
    parts, refs = refs[:3], refs[3:]
    before, refs = refs[: 4 * chunk], refs[4 * chunk :]
    outs = refs[:4]
    query_all, key_all, value_all, attended, sems = refs[4:]
    place, valid_len = lax.axis_index("ctx"), length_ref[0]
    frames, width = query_all.shape
    rows = frames // 4
    targets = (query_all, key_all, value_all)
    mine = pl.ds(pl.multiple_of(place * rows, rows), rows)
    heads = pl.ds(pl.multiple_of(place * SHARE + chunk * LANES, LANES), LANES)
    copies = [
        pltpu.make_async_copy(source.at[0, :, heads], target.at[mine, :], sems.at[which])
        for which, (source, target) in enumerate(zip((query_ref, key_ref, value_ref), targets))
    ]
    for copy in copies:
        copy.start()
    for step, part in enumerate(parts, 1):
        span = pl.ds(pl.multiple_of((place ^ step) * rows, rows), rows)
        for which, target in enumerate(targets):
            cols = slice(chunk * LANES, (chunk + 1) * LANES) if step == 1 else slice(None)
            target[span, :] = part[which * rows : (which + 1) * rows, cols]
    for copy in copies:
        copy.wait()
    attended[0:WIDE, :] = jnp.zeros((WIDE, width), attended.dtype)
    attended[WIDE + frames : 2 * WIDE + frames, :] = jnp.zeros((WIDE, width), attended.dtype)
    usable = lax.broadcasted_iota(jnp.int32, (1, frames), 1) < valid_len
    lane = lax.broadcasted_iota(jnp.int32, (1, LANES), 1)
    for pair in range(width // LANES):
        cols = slice(pair * LANES, (pair + 1) * LANES)
        keys, values = key_all[:, cols], value_all[:, cols]
        heads = [
            (jnp.where(mine, keys, 0).astype(keys.dtype), jnp.where(mine, values, 0).astype(values.dtype))
            for mine in (lane < HD, lane >= HD)
        ]
        for start in range(0, frames, QUERY_ROWS):
            queries = query_all[start : start + QUERY_ROWS, cols]
            total = jnp.zeros((QUERY_ROWS, LANES), jnp.float32)
            for key_head, value_head in heads:
                scores = lax.dot_general(
                    queries, key_head, (((1,), (1,)), ((), ())), preferred_element_type=jnp.float32
                ) * (1.0 / math.sqrt(HD))
                scores = jnp.where(usable, scores, NEG_FILL)
                weights = jnp.exp(scores - jnp.max(scores, axis=1, keepdims=True))
                sums = jnp.sum(weights, axis=1, keepdims=True)
                total += (
                    jnp.dot(
                        weights.astype(jnp.bfloat16), value_head, preferred_element_type=jnp.float32
                    )
                    / sums
                )
            attended[WIDE + start : WIDE + start + QUERY_ROWS, cols] = total.astype(attended.dtype)
    for step in range(4):
        owner = place ^ step
        found = attended[pl.ds(pl.multiple_of(owner * rows, rows), rows + 2 * WIDE), :]
        if chunk:
            outs[step][:, :LANES] = before[step][...]
            outs[step][:, LANES:] = found
        else:
            outs[step][...] = found


def by_residue(first, last):
    return [[o for o in range(first, last + 1) if o % 8 == r] for r in range(8)]


def live_at(length_ref, rows, first, length):
    position = lax.axis_index("ctx") * rows + first + lax.broadcasted_iota(jnp.int32, (length, 1), 0)
    return ((position >= 0) & (position < length_ref[0])).astype(jnp.float32)


def weight_block(w_own, w_near, w_far, part, tile, mine):
    cols = slice(tile * LANES, (tile + 1) * LANES)
    if mine:
        return w_own[pl.ds(pl.multiple_of(part * SHARE, SHARE), SHARE), cols]
    per_part = (w_near.shape[0] - 2 * PARAM_ROWS) // SHARE
    rows = pl.ds(pl.multiple_of(lax.rem(part, per_part) * SHARE, SHARE), SHARE)
    near = lax.div(part, per_part) == lax.axis_index("dp")
    return jnp.where(near, w_near[rows, cols], w_far[rows, cols])


def prepare_kernel(*refs):
    (
        length_ref, own_ref, frames_ref, cotan_ref, beside_ref, edge_ref, w_own, w_near, w_far,
        taps_ref, bias_ref, gain_ref, base, cotan_live, params, par_mine, edges,
    ) = refs
    place, side = lax.axis_index("ctx"), lax.axis_index("fsdp")
    rows, features = frames_ref.shape
    half_tiles = features // 2 // LANES
    weight_rows = w_near.shape[0] - 2 * PARAM_ROWS
    even = 1 - lax.rem(place, 2)
    for block in range(features // SHARE):
        first = 3 * rows + block * (WIDE + NEAR)
        edges[even, :, block * SHARE : (block + 1) * SHARE] = beside_ref[first : first + WIDE + NEAR, :]
    edges[1 - even] = edge_ref[...]
    par_own = parameters(taps_ref, bias_ref, gain_ref)
    par_mine[...] = par_own
    par_other = w_near[weight_rows : weight_rows + PARAM_ROWS, :].astype(jnp.float32)
    par_other += w_near[weight_rows + PARAM_ROWS :, :].astype(jnp.float32)
    live_near = live_at(length_ref, rows, -NEAR, rows + 2 * NEAR)
    own = own_ref[...]
    row = lax.broadcasted_iota(jnp.int32, (PARAM_ROWS, 1), 0)
    for tile in range(half_tiles):
        cols = slice(tile * LANES, (tile + 1) * LANES)
        for mine, source in ((True, par_own), (False, par_other)):
            at = (side if mine else 1 - side) * half_tiles + tile
            values = source[:, cols]
            params[at] = jnp.where(row < TAPS, values * values[TAPS + 1 : TAPS + 2], values)
            span = pl.ds(pl.multiple_of(at * LANES, LANES), LANES)
            weight = weight_block(w_own, w_near, w_far, place, tile, mine)
            base[at] = jnp.dot(own, weight, preferred_element_type=jnp.float32) + jnp.concatenate(
                [edges[0, 0:WIDE, span], frames_ref[:, span], edges[1, 0:WIDE, span]], axis=0
            ).astype(jnp.float32)
            cotan_live[at] = live_near * jnp.concatenate(
                [edges[0, WIDE:, span], cotan_ref[:, span], edges[1, WIDE:, span]], axis=0
            ).astype(jnp.float32)


def module_kernel(*refs):
    (
        length_ref, reply_one, reply_two, reply_three, base, cotan_live, params, w_own, w_near, w_far,
        block_hbm, normed, wide_grad, inv_rows, sums_own, sums_other,
        sums, partial, block_out, out_sems,
    ) = refs
    place, side = lax.axis_index("ctx"), lax.axis_index("fsdp")
    tiles, ext = base.shape[:2]
    rows, features = ext - 2 * WIDE, tiles * LANES
    half_tiles, near = tiles // 2, rows + 2 * NEAR
    for tile in range(half_tiles):
        for mine in (True, False):
            at = (side if mine else 1 - side) * half_tiles + tile
            span = pl.ds(pl.multiple_of(at * LANES, LANES), LANES)
            product = base[at]
            for step, reply in enumerate((reply_one, reply_two, reply_three), 1):
                weight = weight_block(w_own, w_near, w_far, place ^ step, tile, mine)
                product += jnp.dot(reply[...], weight, preferred_element_type=jnp.float32)
            hidden = product.astype(jnp.bfloat16)
            block_out[:, span] = hidden[WIDE : WIDE + rows]
            normed[at, 0:ext] = hidden.astype(jnp.float32)

    total = normed[0, 0:ext]
    for tile in range(1, tiles):
        total += normed[tile, 0:ext]
    average = jnp.sum(total, axis=1, keepdims=True) * (1.0 / features)
    total = jnp.zeros((ext, LANES), jnp.float32)
    for tile in range(tiles):
        centered = normed[tile, 0:ext] - average
        total += centered * centered
    variance = jnp.sum(total, axis=1, keepdims=True) * (1.0 / features)
    inv_scale = lax.rsqrt(variance + 1e-05)
    scale = inv_scale * live_at(length_ref, rows, -WIDE, ext)
    for tile in range(tiles):
        normed[tile, 0:ext] = (normed[tile, 0:ext] - average) * scale

    live_rows = live_at(length_ref, rows, 0, rows)
    inv_rows[...] = jnp.broadcast_to(inv_scale[WIDE : WIDE + rows], inv_rows.shape)

    def one_tile(tile, carry):
        span = pl.ds(pl.multiple_of(tile * LANES, LANES), LANES)
        pre_act = jnp.broadcast_to(params[tile, TAPS : TAPS + 1], (near, LANES))
        for rest, offsets in enumerate(by_residue(1, TAPS)):
            shifted = normed[tile, rest : rest + near + 24]
            for offset in offsets:
                at = offset - rest
                pre_act += params[tile, offset - 1 : offset] * shifted[at : at + near]
        gate = jax.nn.sigmoid(pre_act)
        here = slice(NEAR, NEAR + rows)
        block_out[:, span] = (
            block_out[:, span].astype(jnp.float32) + live_rows * (pre_act * gate)[here]
        ).astype(block_out.dtype)
        pltpu.make_async_copy(
            block_out.at[:, span], block_hbm.at[:, span], out_sems.at[tile]
        ).start()
        grad_pre = cotan_live[tile] * gate * (1.0 + pre_act * (1.0 - gate))
        wide_grad[tile, 0:near] = grad_pre
        own_grad = grad_pre[here]
        first = WIDE - HALF
        for rest, offsets in enumerate(by_residue(first, first + TAPS - 1)):
            low = offsets[0]
            shifted = normed[tile, low : low + rows + 24]
            for offset in offsets:
                at = offset - low
                partial[offset - first] = jnp.sum(
                    (own_grad * shifted[at : at + rows]).reshape(rows // 8, 8, LANES), axis=0
                )
        partial[TAPS] = jnp.sum(own_grad.reshape(rows // 8, 8, LANES), axis=0)
        sums[tile] = jnp.sum(partial[...], axis=1)
        return carry

    lax.fori_loop(0, tiles, one_tile, 0, unroll=4)
    for tile in range(half_tiles):
        cols = slice(tile * LANES, (tile + 1) * LANES)
        sums_own[:, cols] = sums[side * half_tiles + tile].astype(sums_own.dtype)
        sums_other[:, cols] = sums[(1 - side) * half_tiles + tile].astype(sums_other.dtype)
    for tile in range(tiles):
        cols = slice(tile * LANES, (tile + 1) * LANES)
        pltpu.make_async_copy(block_out.at[:, cols], block_hbm.at[:, cols], out_sems.at[tile]).wait()


def backward_kernel(length_ref, normed, wide_grad, params, grad_hat, means, mean_one, mean_two):
    tiles, rows = grad_hat.shape[:2]
    live_rows = live_at(length_ref, rows, 0, rows)
    mean_one[...] = jnp.zeros_like(mean_one)
    mean_two[...] = jnp.zeros_like(mean_two)

    def one_tile(tile, carry):
        grad = jnp.zeros((rows, LANES), jnp.float32)
        for rest, offsets in enumerate(by_residue(1, TAPS)):
            shifted = wide_grad[tile, rest : rest + rows + 24]
            for offset in offsets:
                at = offset - rest
                tap = TAPS - offset
                grad += params[tile, tap : tap + 1] * shifted[at : at + rows]
        grad = live_rows * grad
        grad_hat[tile] = grad
        mean_one[...] += grad
        mean_two[...] += grad * normed[tile, WIDE : WIDE + rows]
        return carry

    lax.fori_loop(0, tiles, one_tile, 0, unroll=4)
    for index, total in enumerate((mean_one, mean_two)):
        mean = jnp.sum(total[...], axis=1, keepdims=True) * (1.0 / (tiles * LANES))
        means[index] = jnp.broadcast_to(mean, (rows, LANES))


def hidden_grad_kernel(cotan_ref, normed, inv_rows, grad_hat, means, grad_hbm, hidden_grad, out_sems):
    tiles, rows = grad_hat.shape[:2]
    copies = []
    for tile in range(tiles):
        cols = slice(tile * LANES, (tile + 1) * LANES)
        inner = grad_hat[tile] - means[0] - normed[tile, WIDE : WIDE + rows] * means[1]
        hidden_grad[:, cols] = (
            cotan_ref[:, cols].astype(jnp.float32) + inner * inv_rows[...]
        ).astype(hidden_grad.dtype)
        copies.append(
            pltpu.make_async_copy(hidden_grad.at[:, cols], grad_hbm.at[:, cols], out_sems.at[tile])
        )
        copies[-1].start()
    for copy in copies:
        copy.wait()


def finish_kernel(factor, mine, one, two, three, params, kernel_out, bias_out, gain_out, terms):
    place = lax.axis_index("ctx")
    for step, source in enumerate((mine, one, two, three)):
        terms[place ^ step] = source[...].astype(jnp.float32)
    total = (((terms[0] + terms[1]) + terms[2]) + terms[3]) * factor
    kernel_out[...] = total[:TAPS] * params[TAPS + 1 : TAPS + 2]
    bias_out[...] = total[TAPS]
    gain_out[...] = jnp.sum(total[:TAPS] * params[:TAPS], axis=0)


def fast_shards(
    query_in,
    key_in,
    value_in,
    utt_lengths,
    frames_in,
    out_weight,
    conv_kernel,
    conv_bias,
    ln_gain,
    cotangent,
):
    count = lax.axis_size("ctx")
    rows, width = query_in.shape[1], query_in.shape[2]
    features, half = frames_in.shape[2], out_weight.shape[1]
    place = lax.axis_index("ctx")
    vmem = pl.BlockSpec(memory_space=pltpu.VMEM)
    smem = pl.BlockSpec(memory_space=pltpu.SMEM)
    hbm = pl.BlockSpec(memory_space=pltpu.HBM)
    swap = [(0, 1), (1, 0)]

    ends = (features // SHARE) * (WIDE + NEAR)
    sent = [
        (3 * rows + ends, SHARE),
        *[(3 * rows, LANES)] * (len(PIECES) - 1),
        (WIDE + NEAR, features),
        (width // 2 + 2 * PARAM_ROWS, half),
    ]
    *pieces, edge, w_sent = pl.pallas_call(
        pack_kernel,
        name="pack",
        out_shape=[jax.ShapeDtypeStruct(shape, jnp.bfloat16) for shape in sent],
        in_specs=[hbm] * 9,
        out_specs=[vmem] * len(sent),
        scratch_shapes=[
            pltpu.VMEM((3, rows, width), jnp.bfloat16),
            pltpu.VMEM((2, WIDE + NEAR, features), jnp.bfloat16),
            pltpu.VMEM((TAPS, half), jnp.float32),
            pltpu.VMEM((half,), jnp.float32),
            pltpu.VMEM((half,), jnp.float32),
            pltpu.SemaphoreType.DMA((32,)),
        ],
        compiler_params=pltpu.CompilerParams(vmem_limit_bytes=32 << 20),
    )(
        *(
            pltpu.with_memory_space_constraint(one, pltpu.HBM)
            for one in (
                query_in,
                key_in,
                value_in,
                frames_in,
                cotangent,
                out_weight,
                conv_kernel,
                conv_bias,
                ln_gain,
            )
        )
    )
    parts = [
        lax.ppermute(one, "ctx", facing(count, step)) for one, (step, _) in zip(pieces, PIECES)
    ]
    edge = lax.ppermute(edge, "ctx", [(1, 2), (2, 1)])
    w_near = lax.ppermute(w_sent, "fsdp", swap)

    attended = []
    for chunk in range(CHUNKS):
        ready = [parts[0], *parts[2 * chunk + 1 : 2 * chunk + 3]]
        before = []
        if chunk:
            before = attended
            ready, edge = lax.optimization_barrier((ready, edge))
        attended = pl.pallas_call(
            functools.partial(attend_kernel, chunk),
            name="attend",
            out_shape=[
                jax.ShapeDtypeStruct((rows + 2 * WIDE, (chunk + 1) * LANES), jnp.bfloat16)
            ]
            * count,
            in_specs=[smem] + [hbm] * 3 + [vmem] * (3 + len(before)),
            out_specs=[vmem] * count,
            scratch_shapes=[pltpu.VMEM((count * rows, LANES), jnp.bfloat16)] * 3
            + [pltpu.VMEM((count * rows + 2 * WIDE, LANES), jnp.bfloat16)]
            + [pltpu.SemaphoreType.DMA((3,))],
            compiler_params=pltpu.CompilerParams(vmem_limit_bytes=40 << 20),
            cost_estimate=pl.CostEstimate(flops=1, bytes_accessed=1, transcendentals=0),
        )(utt_lengths, query_in, key_in, value_in, *ready, *before)
    own, *replies = [
        reply if step == 0 else lax.ppermute(reply, "ctx", facing(count, step))
        for step, reply in enumerate(attended)
    ]
    _, w_near = lax.optimization_barrier((attended, w_near))
    w_far = lax.ppermute(w_near, "dp", swap)
    frames, cotan = frames_in[0], cotangent[0]

    ext, near = rows + 2 * WIDE, rows + 2 * NEAR
    tiles = features // LANES
    base, cotan_live, params, par_mine = pl.pallas_call(
        prepare_kernel,
        name="prepare",
        out_shape=[
            jax.ShapeDtypeStruct((tiles, ext, LANES), jnp.float32),
            jax.ShapeDtypeStruct((tiles, near, LANES), jnp.float32),
            jax.ShapeDtypeStruct((tiles, PARAM_ROWS, LANES), jnp.float32),
            jax.ShapeDtypeStruct((PARAM_ROWS, half), jnp.float32),
        ],
        in_specs=[smem] + [vmem] * 11,
        out_specs=[vmem] * 4,
        scratch_shapes=[pltpu.VMEM((2, WIDE + NEAR, features), jnp.bfloat16)],
        compiler_params=pltpu.CompilerParams(vmem_limit_bytes=32 << 20),
        cost_estimate=pl.CostEstimate(
            flops=2 * ext * SHARE * features, bytes_accessed=8 * rows * features, transcendentals=0
        ),
    )(
        utt_lengths,
        own,
        frames,
        cotan,
        parts[0],
        edge,
        out_weight,
        w_near,
        w_far,
        conv_kernel,
        conv_bias,
        ln_gain,
    )
    block_out, normed, wide_grad, inv_rows, sums_own, sums_other = pl.pallas_call(
        module_kernel,
        name="conv_module",
        out_shape=[
            jax.ShapeDtypeStruct((rows, features), jnp.bfloat16),
            jax.ShapeDtypeStruct((tiles, ext + 8, LANES), jnp.float32),
            jax.ShapeDtypeStruct((tiles, near + 8, LANES), jnp.float32),
            jax.ShapeDtypeStruct((rows, LANES), jnp.float32),
            jax.ShapeDtypeStruct((TAPS + 1, half), jnp.bfloat16),
            jax.ShapeDtypeStruct((TAPS + 1, half), jnp.bfloat16),
        ],
        in_specs=[smem] + [vmem] * 9,
        out_specs=[hbm] + [vmem] * 5,
        scratch_shapes=[
            pltpu.VMEM((tiles, TAPS + 1, LANES), jnp.float32),
            pltpu.VMEM((TAPS + 1, 8, LANES), jnp.float32),
            pltpu.VMEM((rows, features), jnp.bfloat16),
            pltpu.SemaphoreType.DMA((tiles,)),
        ],
        compiler_params=pltpu.CompilerParams(vmem_limit_bytes=32 << 20),
        cost_estimate=pl.CostEstimate(
            flops=2 * ext * width * features + 4 * TAPS * rows * features,
            bytes_accessed=2 * width * features + 12 * rows * features,
            transcendentals=near * features,
        ),
    )(
        utt_lengths,
        *replies,
        base,
        cotan_live,
        params,
        out_weight,
        w_near,
        w_far,
    )

    pairs = [
        lax.ppermute(sums_other, "fsdp", swap),
        lax.ppermute(sums_other, ("fsdp", "dp"), [(0, 3), (3, 0), (1, 2), (2, 1)]),
        lax.ppermute(sums_own, "dp", swap),
    ]
    grad_hat, means = pl.pallas_call(
        backward_kernel,
        name="conv_backward",
        out_shape=[
            jax.ShapeDtypeStruct((tiles, rows, LANES), jnp.float32),
            jax.ShapeDtypeStruct((2, rows, LANES), jnp.float32),
        ],
        in_specs=[smem] + [vmem] * 3,
        out_specs=[vmem] * 2,
        scratch_shapes=[pltpu.VMEM((rows, LANES), jnp.float32)] * 2,
        compiler_params=pltpu.CompilerParams(vmem_limit_bytes=32 << 20),
        cost_estimate=pl.CostEstimate(
            flops=2 * TAPS * rows * features,
            bytes_accessed=12 * rows * features,
            transcendentals=0,
        ),
    )(utt_lengths, normed, wide_grad, params)
    pairs, grad_hat = lax.optimization_barrier((pairs, grad_hat))
    across_x, diagonal, sibling = (one.astype(jnp.float32) for one in pairs)
    found = (sums_own.astype(jnp.float32) + sibling) + (across_x + diagonal)
    found = found.astype(jnp.bfloat16)
    arrived = [lax.ppermute(found, "ctx", facing(count, step)) for step in range(1, count)]
    hidden_grad = pl.pallas_call(
        hidden_grad_kernel,
        name="hidden_grad",
        out_shape=jax.ShapeDtypeStruct((rows, features), jnp.bfloat16),
        in_specs=[vmem] * 5,
        out_specs=hbm,
        scratch_shapes=[
            pltpu.VMEM((rows, features), jnp.bfloat16),
            pltpu.SemaphoreType.DMA((tiles,)),
        ],
        compiler_params=pltpu.CompilerParams(vmem_limit_bytes=32 << 20),
        cost_estimate=pl.CostEstimate(
            flops=6 * rows * features, bytes_accessed=12 * rows * features, transcendentals=0
        ),
    )(cotan, normed, inv_rows, grad_hat, means)
    arrived, hidden_grad = lax.optimization_barrier((arrived, hidden_grad))
    factor = 1.0 / math.sqrt(lax.axis_size("fsdp") * lax.axis_size("dp") * rows * count)
    grad_kernel, grad_bias, grad_gain = pl.pallas_call(
        functools.partial(finish_kernel, factor),
        name="finish",
        out_shape=[
            jax.ShapeDtypeStruct((TAPS, half), jnp.float32),
            jax.ShapeDtypeStruct((half,), jnp.float32),
            jax.ShapeDtypeStruct((half,), jnp.float32),
        ],
        in_specs=[vmem] * 5,
        out_specs=[vmem] * 3,
        scratch_shapes=[pltpu.VMEM((count, TAPS + 1, half), jnp.float32)],
        compiler_params=pltpu.CompilerParams(vmem_limit_bytes=32 << 20),
    )(found, *arrived, par_mine)
    return (block_out[None], hidden_grad[None], grad_kernel, grad_bias, grad_gain)


def solution(mesh):
    in_specs = (
        P(("groups", "fsdp", "dp"), "ctx", None),
        P(("groups", "fsdp", "dp"), "ctx", None),
        P(("groups", "fsdp", "dp"), "ctx", None),
        P(("groups", "fsdp", "dp")),
        P(("groups", "fsdp", "dp"), "ctx", None),
        P(None, "fsdp"),
        P(None, "fsdp"),
        P("fsdp"),
        P("fsdp"),
        P(("groups", "fsdp", "dp"), "ctx", None),
    )
    out_specs = (
        P(("groups", "fsdp", "dp"), "ctx", None),
        P(("groups", "fsdp", "dp"), "ctx", None),
        P("groups", "fsdp"),
        P(("groups", "fsdp")),
        P(("groups", "fsdp")),
    )

    def shards(*blocks):
        run = fast_shards if fits_fast(mesh, blocks) else general_shards
        return run(*blocks)

    return jax.shard_map(shards, mesh=mesh, in_specs=in_specs, out_specs=out_specs, check_vma=False)
```

```python
import functools
import math

import jax
import jax.numpy as jnp
from jax import lax
from jax.experimental import pallas as pl
from jax.experimental.pallas import tpu as pltpu
from jax.sharding import PartitionSpec as P

HD = 64
TAPS = 31
HALF = TAPS // 2
LANES = 128
WIDE = 32
NEAR = 16
PARAM_ROWS = 40
SHARE = 256
QUERY_ROWS = 128
CHUNKS = SHARE // LANES

NEG_FILL = -1e30


def extended(block, sides, width):
    for axis, dim in sides:
        count = lax.axis_size(axis)
        forward = [(i, i + 1) for i in range(count - 1)]
        backward = [(target, source) for source, target in forward]
        low = lax.ppermute(
            lax.slice_in_dim(block, block.shape[dim] - width, None, axis=dim), axis, forward
        )
        high = lax.ppermute(lax.slice_in_dim(block, 0, width, axis=dim), axis, backward)
        block = jnp.concatenate([low, block, high], axis=dim)
    return block


def absorb_block(state, query_heads, key_heads, value_heads, key_start, valid_len):
    run_max, run_sum, summed = state
    scores = jnp.einsum(
        "qhd,khd->qhk", query_heads, key_heads, preferred_element_type=jnp.float32
    ) * (1.0 / math.sqrt(HD))
    usable = key_start + jnp.arange(key_heads.shape[0]) < valid_len
    scores = jnp.where(usable, scores, NEG_FILL)
    new_max = jnp.maximum(run_max, jnp.max(scores, axis=-1))
    rescale = jnp.exp(run_max - new_max)
    weights = jnp.where(usable, jnp.exp(scores - new_max[..., None]), 0.0)
    run_sum = run_sum * rescale + jnp.sum(weights, axis=-1)
    summed = summed * rescale[..., None] + jnp.einsum(
        "qhk,khd->qhd",
        weights.astype(jnp.bfloat16),
        value_heads,
        preferred_element_type=jnp.float32,
    )
    return (new_max, run_sum, summed)


def normalize(block):
    as_float = block.astype(jnp.float32)
    average = jnp.mean(as_float, axis=-1, keepdims=True)
    centered = as_float - average
    variance = jnp.mean(centered * centered, axis=-1, keepdims=True)
    inv_scale = lax.rsqrt(variance + 1e-05)
    return (centered * inv_scale, inv_scale)


def convolve(conv_in, kernel_all, bias_all, out_rows):
    pre_act = bias_all + jnp.zeros((out_rows, conv_in.shape[1]), jnp.float32)
    for tap_index in range(TAPS):
        pre_act = pre_act + kernel_all[tap_index] * conv_in[tap_index : tap_index + out_rows]
    return pre_act


def live_of(positions, valid_len):
    return ((positions >= 0) & (positions < valid_len)).astype(jnp.float32)[:, None]


def general_shards(
    query_in,
    key_in,
    value_in,
    utt_lengths,
    frames_in,
    out_weight,
    conv_kernel,
    conv_bias,
    ln_gain,
    cotangent,
):
    row_count = query_in.shape[1]
    feat_width = query_in.shape[2]
    head_count = feat_width // HD
    valid_len = utt_lengths[0]
    ctx_count = lax.axis_size("ctx")
    row_offset = lax.axis_index("ctx") * row_count
    half_taps = TAPS // 2
    query_heads = query_in[0].reshape(row_count, head_count, HD)
    start_state = (
        jnp.full((row_count, head_count), NEG_FILL, jnp.float32),
        jnp.zeros((row_count, head_count), jnp.float32),
        jnp.zeros((row_count, head_count, HD), jnp.float32),
    )
    state = start_state
    first_row = jnp.int32(0)
    key_part = lax.all_gather(key_in, "ctx", axis=1, tiled=True)
    value_part = lax.all_gather(value_in, "ctx", axis=1, tiled=True)
    piece_rows = key_part.shape[1]
    block_len = math.gcd(piece_rows, 512)
    for block_start in range(0, piece_rows, block_len):
        key_heads = key_part[0, block_start : block_start + block_len].reshape(
            block_len, head_count, HD
        )
        value_heads = value_part[0, block_start : block_start + block_len].reshape(
            block_len, head_count, HD
        )
        state = absorb_block(
            state, query_heads, key_heads, value_heads, first_row + block_start, valid_len
        )
    run_max, run_sum, summed = state
    attended = (summed / run_sum[..., None]).reshape(row_count, feat_width).astype(jnp.bfloat16)
    projected = jnp.dot(
        attended,
        lax.all_gather(out_weight, "fsdp", axis=1, tiled=True),
        preferred_element_type=jnp.float32,
    )
    hidden = (frames_in[0].astype(jnp.float32) + projected).astype(jnp.bfloat16)
    kernel_all, bias_all, gain_all = (
        lax.all_gather(conv_kernel, "fsdp", axis=1, tiled=True),
        lax.all_gather(conv_bias, "fsdp", axis=0, tiled=True),
        lax.all_gather(ln_gain, "fsdp", axis=0, tiled=True),
    )
    grad_in = cotangent[0].astype(jnp.float32)
    live_mask = live_of(row_offset + jnp.arange(row_count), valid_len)
    widened = extended(hidden, (("ctx", 0),), half_taps)
    normed_ext, inv_ext = normalize(widened)
    conv_in = (
        live_of(row_offset - half_taps + jnp.arange(row_count + 2 * half_taps), valid_len)
        * normed_ext
        * gain_all
    )
    pre_act = convolve(conv_in, kernel_all, bias_all, row_count)
    gate_val = jax.nn.sigmoid(pre_act)
    grad_pre = grad_in * live_mask * gate_val * (1.0 + pre_act * (1.0 - gate_val))
    grad_wide = extended(grad_pre.astype(jnp.bfloat16), (("ctx", 0),), half_taps).astype(
        grad_pre.dtype
    )
    normed = normed_ext[half_taps : half_taps + row_count]
    inv_scale = inv_ext[half_taps : half_taps + row_count]
    block_out = (hidden.astype(jnp.float32) + live_mask * pre_act * gate_val).astype(jnp.bfloat16)
    grad_conv = jnp.zeros((row_count, grad_pre.shape[1]), jnp.float32)
    kernel_rows = []
    for tap_index in range(TAPS):
        back = 2 * half_taps - tap_index
        grad_conv = grad_conv + kernel_all[tap_index] * grad_wide[back : back + row_count]
        kernel_rows.append(jnp.sum(grad_pre * conv_in[tap_index : tap_index + row_count], axis=0))
    grad_conv = live_mask * grad_conv
    grad_hat = grad_conv * gain_all
    first_mean = jnp.mean(grad_hat, axis=-1, keepdims=True)
    second_mean = jnp.mean(grad_hat * normed, axis=-1, keepdims=True)
    hidden_grad = (grad_in + (grad_hat - first_mean - normed * second_mean) * inv_scale).astype(
        jnp.bfloat16
    )
    factor = 1.0 / math.sqrt(lax.axis_size("fsdp") * lax.axis_size("dp") * row_count * ctx_count)
    kernel_term = jnp.stack(kernel_rows) * factor
    bias_term = (jnp.sum(grad_pre, axis=0) * factor)[None]
    gain_term = (jnp.sum(grad_conv * normed, axis=0) * factor)[None]
    shares = (
        lax.psum_scatter(
            kernel_term.astype(jnp.bfloat16), "fsdp", scatter_dimension=1, tiled=True
        ).astype(jnp.float32),
        lax.psum_scatter(
            bias_term.astype(jnp.bfloat16), "fsdp", scatter_dimension=1, tiled=True
        ).astype(jnp.float32),
        lax.psum_scatter(
            gain_term.astype(jnp.bfloat16), "fsdp", scatter_dimension=1, tiled=True
        ).astype(jnp.float32),
    )
    totals = lax.psum((shares[0], shares[1], shares[2]), ("ctx", "dp"))
    return (block_out[None], hidden_grad[None], totals[0], totals[1][0], totals[2][0])


def fits_fast(mesh, blocks):
    query_in, frames_in, out_weight = blocks[0], blocks[4], blocks[5]
    ctx_count = mesh.shape["ctx"]
    rows, width = query_in.shape[1], query_in.shape[2]
    return (
        query_in.shape[0] == 1
        and mesh.shape["fsdp"] == 2
        and mesh.shape["dp"] == 2
        and ctx_count == 4
        and width == ctx_count * SHARE
        and rows == LANES
        and frames_in.shape[2] == 2 * out_weight.shape[1]
        and out_weight.shape[1] % SHARE == 0
    )


def facing(count, step):
    return [(i, i ^ step) for i in range(count)]


PIECES = [(1, 0)] + [(step, chunk) for chunk in range(CHUNKS) for step in (2, 3)]


def pack_kernel(*refs):
    (
        query_ref, key_ref, value_ref, frames_ref, cotan_ref, weight_ref, taps_ref, bias_ref, gain_ref,
        *outs,
    ) = refs[: 9 + len(PIECES) + 2]
    whole, edges, taps, bias, gain, in_sems = refs[-6:]
    *outs, edge, weight_out = outs
    place, core = lax.axis_index("ctx"), lax.axis_index("dp")
    rows = query_ref.shape[1]
    depth = weight_out.shape[0] - 2 * PARAM_ROWS
    arriving = []

    def fetch(source, target):
        arriving.append(pltpu.make_async_copy(source, target, in_sems.at[len(arriving)]))
        arriving[-1].start()

    per_input = rows // NEAR // 2
    for which, source in enumerate((query_ref, key_ref, value_ref)):
        for part in range(per_input):
            span = slice(part * 2 * NEAR, (part + 1) * 2 * NEAR)
            fetch(source.at[0, span, :], whole.at[which, span, :])
    odd = lax.rem(place, 2)
    for side in range(2):
        high = odd if side else 1 - odd
        wide = pl.multiple_of(high * (rows - WIDE), WIDE)
        near = pl.multiple_of(high * (rows - NEAR), NEAR)
        fetch(frames_ref.at[0, pl.ds(wide, WIDE), :], edges.at[side, 0:WIDE, :])
        fetch(cotan_ref.at[0, pl.ds(near, NEAR), :], edges.at[side, WIDE : WIDE + NEAR, :])
    for part in range(0, depth, 64):
        first = pl.multiple_of(core * depth + part, 64)
        fetch(weight_ref.at[pl.ds(first, 64), :], weight_out.at[part : part + 64, :])
    for source, target in ((taps_ref, taps), (bias_ref, bias), (gain_ref, gain)):
        fetch(source, target)
    for which in range(3):
        for part in range(per_input):
            arriving[which * per_input + part].wait()
        at = slice(which * rows, (which + 1) * rows)
        for out, (step, chunk) in zip(outs, PIECES):
            first = (place ^ step) * SHARE + chunk * LANES
            size = out.shape[1]
            out[at, :] = whole[which, :, pl.ds(pl.multiple_of(first, LANES), size)]
    seen = 3 * per_input
    for copy in arriving[seen : seen + 4]:
        copy.wait()
    for block in range(edges.shape[2] // SHARE):
        base = 3 * rows + block * (WIDE + NEAR)
        outs[0][base : base + WIDE + NEAR, :] = edges[0, :, block * SHARE : (block + 1) * SHARE]
    edge[...] = edges[1]
    for copy in arriving[-3:]:
        copy.wait()
    params = parameters(taps, bias, gain)
    rounded = params.astype(jnp.bfloat16)
    weight_out[depth : depth + PARAM_ROWS, :] = rounded
    weight_out[depth + PARAM_ROWS :, :] = (params - rounded.astype(jnp.float32)).astype(jnp.bfloat16)
    for copy in arriving[seen + 4 : -3]:
        copy.wait()


def parameters(taps_ref, bias_ref, gain_ref):
    half = taps_ref.shape[1]
    return jnp.concatenate(
        [
            taps_ref[...],
            bias_ref[...].reshape(1, half),
            gain_ref[...].reshape(1, half),
            jnp.zeros((PARAM_ROWS - TAPS - 2, half), jnp.float32),
        ],
        axis=0,
    )


def attend_kernel(chunk, length_ref, query_ref, key_ref, value_ref, *refs):
    parts, refs = refs[:3], refs[3:]
    before, refs = refs[: 4 * chunk], refs[4 * chunk :]
    outs = refs[:4]
    query_all, key_all, value_all, attended, sems = refs[4:]
    place, valid_len = lax.axis_index("ctx"), length_ref[0]
    frames, width = query_all.shape
    rows = frames // 4
    targets = (query_all, key_all, value_all)
    mine = pl.ds(pl.multiple_of(place * rows, rows), rows)
    heads = pl.ds(pl.multiple_of(place * SHARE + chunk * LANES, LANES), LANES)
    copies = [
        pltpu.make_async_copy(source.at[0, :, heads], target.at[mine, :], sems.at[which])
        for which, (source, target) in enumerate(zip((query_ref, key_ref, value_ref), targets))
    ]
    for copy in copies:
        copy.start()
    for step, part in enumerate(parts, 1):
        span = pl.ds(pl.multiple_of((place ^ step) * rows, rows), rows)
        for which, target in enumerate(targets):
            cols = slice(chunk * LANES, (chunk + 1) * LANES) if step == 1 else slice(None)
            target[span, :] = part[which * rows : (which + 1) * rows, cols]
    for copy in copies:
        copy.wait()
    attended[0:WIDE, :] = jnp.zeros((WIDE, width), attended.dtype)
    attended[WIDE + frames : 2 * WIDE + frames, :] = jnp.zeros((WIDE, width), attended.dtype)
    usable = lax.broadcasted_iota(jnp.int32, (1, frames), 1) < valid_len
    lane = lax.broadcasted_iota(jnp.int32, (1, LANES), 1)
    for pair in range(width // LANES):
        cols = slice(pair * LANES, (pair + 1) * LANES)
        keys, values = key_all[:, cols], value_all[:, cols]
        heads = [
            (jnp.where(mine, keys, 0).astype(keys.dtype), jnp.where(mine, values, 0).astype(values.dtype))
            for mine in (lane < HD, lane >= HD)
        ]
        for start in range(0, frames, QUERY_ROWS):
            queries = query_all[start : start + QUERY_ROWS, cols]
            rounded, sums = [], []
            for key_head, _ in heads:
                scores = lax.dot_general(
                    queries, key_head, (((1,), (1,)), ((), ())), preferred_element_type=jnp.float32
                ) * (1.0 / math.sqrt(HD))
                scores = jnp.where(usable, scores, NEG_FILL)
                weights = jnp.exp(scores - jnp.max(scores, axis=1, keepdims=True))
                sums.append(jnp.sum(weights, axis=1, keepdims=True))
                rounded.append(weights.astype(jnp.bfloat16))
            total = jnp.dot(
                jnp.concatenate(rounded, axis=1),
                jnp.concatenate([value_head for _, value_head in heads], axis=0),
                preferred_element_type=jnp.float32,
            ) / jnp.where(lane < HD, sums[0], sums[1])
            attended[WIDE + start : WIDE + start + QUERY_ROWS, cols] = total.astype(attended.dtype)
    for step in range(4):
        owner = place ^ step
        found = attended[pl.ds(pl.multiple_of(owner * rows, rows), rows + 2 * WIDE), :]
        if chunk:
            outs[step][:, :LANES] = before[step][...]
            outs[step][:, LANES:] = found
        else:
            outs[step][...] = found


def by_residue(first, last):
    return [[o for o in range(first, last + 1) if o % 8 == r] for r in range(8)]


def live_at(length_ref, rows, first, length):
    position = lax.axis_index("ctx") * rows + first + lax.broadcasted_iota(jnp.int32, (length, 1), 0)
    return ((position >= 0) & (position < length_ref[0])).astype(jnp.float32)


def weight_block(w_own, w_near, w_far, part, tile, mine):
    cols = slice(tile * LANES, (tile + 1) * LANES)
    if mine:
        return w_own[pl.ds(pl.multiple_of(part * SHARE, SHARE), SHARE), cols]
    per_part = (w_near.shape[0] - 2 * PARAM_ROWS) // SHARE
    rows = pl.ds(pl.multiple_of(lax.rem(part, per_part) * SHARE, SHARE), SHARE)
    near = lax.div(part, per_part) == lax.axis_index("dp")
    return jnp.where(near, w_near[rows, cols], w_far[rows, cols])


def prepare_kernel(*refs):
    (
        length_ref, own_ref, frames_ref, cotan_ref, beside_ref, edge_ref, w_own, w_near, w_far,
        taps_ref, bias_ref, gain_ref, base, cotan_live, params, par_mine, edges,
    ) = refs
    place, side = lax.axis_index("ctx"), lax.axis_index("fsdp")
    rows, features = frames_ref.shape
    half_tiles = features // 2 // LANES
    weight_rows = w_near.shape[0] - 2 * PARAM_ROWS
    even = 1 - lax.rem(place, 2)
    for block in range(features // SHARE):
        first = 3 * rows + block * (WIDE + NEAR)
        edges[even, :, block * SHARE : (block + 1) * SHARE] = beside_ref[first : first + WIDE + NEAR, :]
    edges[1 - even] = edge_ref[...]
    par_own = parameters(taps_ref, bias_ref, gain_ref)
    par_mine[...] = par_own
    par_other = w_near[weight_rows : weight_rows + PARAM_ROWS, :].astype(jnp.float32)
    par_other += w_near[weight_rows + PARAM_ROWS :, :].astype(jnp.float32)
    live_near = live_at(length_ref, rows, -NEAR, rows + 2 * NEAR)
    own = own_ref[...]
    row = lax.broadcasted_iota(jnp.int32, (PARAM_ROWS, 1), 0)
    for tile in range(half_tiles):
        cols = slice(tile * LANES, (tile + 1) * LANES)
        for mine, source in ((True, par_own), (False, par_other)):
            at = (side if mine else 1 - side) * half_tiles + tile
            values = source[:, cols]
            params[at] = jnp.where(row < TAPS, values * values[TAPS + 1 : TAPS + 2], values)
            span = pl.ds(pl.multiple_of(at * LANES, LANES), LANES)
            weight = weight_block(w_own, w_near, w_far, place, tile, mine)
            base[at] = jnp.dot(own, weight, preferred_element_type=jnp.float32) + jnp.concatenate(
                [edges[0, 0:WIDE, span], frames_ref[:, span], edges[1, 0:WIDE, span]], axis=0
            ).astype(jnp.float32)
            cotan_live[at] = live_near * jnp.concatenate(
                [edges[0, WIDE:, span], cotan_ref[:, span], edges[1, WIDE:, span]], axis=0
            ).astype(jnp.float32)


def module_kernel(*refs):
    (
        length_ref, reply_one, reply_two, reply_three, base, cotan_live, params, w_own, w_near, w_far,
        block_hbm, normed, wide_grad, inv_rows, sums_own, sums_other,
        sums, partial, block_out, out_sems,
    ) = refs
    place, side = lax.axis_index("ctx"), lax.axis_index("fsdp")
    tiles, ext = base.shape[:2]
    rows, features = ext - 2 * WIDE, tiles * LANES
    half_tiles, near = tiles // 2, rows + 2 * NEAR
    for tile in range(half_tiles):
        for mine in (True, False):
            at = (side if mine else 1 - side) * half_tiles + tile
            span = pl.ds(pl.multiple_of(at * LANES, LANES), LANES)
            product = base[at]
            for step, reply in enumerate((reply_one, reply_two, reply_three), 1):
                weight = weight_block(w_own, w_near, w_far, place ^ step, tile, mine)
                product += jnp.dot(reply[...], weight, preferred_element_type=jnp.float32)
            hidden = product.astype(jnp.bfloat16)
            block_out[:, span] = hidden[WIDE : WIDE + rows]
            normed[at, 0:ext] = hidden.astype(jnp.float32)

    total = normed[0, 0:ext]
    for tile in range(1, tiles):
        total += normed[tile, 0:ext]
    average = jnp.sum(total, axis=1, keepdims=True) * (1.0 / features)
    total = jnp.zeros((ext, LANES), jnp.float32)
    for tile in range(tiles):
        centered = normed[tile, 0:ext] - average
        total += centered * centered
    variance = jnp.sum(total, axis=1, keepdims=True) * (1.0 / features)
    inv_scale = lax.rsqrt(variance + 1e-05)
    scale = inv_scale * live_at(length_ref, rows, -WIDE, ext)
    for tile in range(tiles):
        normed[tile, 0:ext] = (normed[tile, 0:ext] - average) * scale

    live_rows = live_at(length_ref, rows, 0, rows)
    inv_rows[...] = jnp.broadcast_to(inv_scale[WIDE : WIDE + rows], inv_rows.shape)

    def one_tile(tile, carry):
        span = pl.ds(pl.multiple_of(tile * LANES, LANES), LANES)
        pre_act = jnp.broadcast_to(params[tile, TAPS : TAPS + 1], (near, LANES))
        for rest, offsets in enumerate(by_residue(1, TAPS)):
            shifted = normed[tile, rest : rest + near + 24]
            for offset in offsets:
                at = offset - rest
                pre_act += params[tile, offset - 1 : offset] * shifted[at : at + near]
        gate = jax.nn.sigmoid(pre_act)
        here = slice(NEAR, NEAR + rows)
        block_out[:, span] = (
            block_out[:, span].astype(jnp.float32) + live_rows * (pre_act * gate)[here]
        ).astype(block_out.dtype)
        pltpu.make_async_copy(
            block_out.at[:, span], block_hbm.at[:, span], out_sems.at[tile]
        ).start()
        grad_pre = cotan_live[tile] * gate * (1.0 + pre_act * (1.0 - gate))
        wide_grad[tile, 0:near] = grad_pre
        own_grad = grad_pre[here]
        first = WIDE - HALF
        for rest, offsets in enumerate(by_residue(first, first + TAPS - 1)):
            low = offsets[0]
            shifted = normed[tile, low : low + rows + 24]
            for offset in offsets:
                at = offset - low
                partial[offset - first] = jnp.sum(
                    (own_grad * shifted[at : at + rows]).reshape(rows // 8, 8, LANES), axis=0
                )
        partial[TAPS] = jnp.sum(own_grad.reshape(rows // 8, 8, LANES), axis=0)
        sums[tile] = jnp.sum(partial[...], axis=1)
        return carry

    lax.fori_loop(0, tiles, one_tile, 0, unroll=2)
    for tile in range(half_tiles):
        cols = slice(tile * LANES, (tile + 1) * LANES)
        sums_own[:, cols] = sums[side * half_tiles + tile].astype(sums_own.dtype)
        sums_other[:, cols] = sums[(1 - side) * half_tiles + tile].astype(sums_other.dtype)
    for tile in range(tiles):
        cols = slice(tile * LANES, (tile + 1) * LANES)
        pltpu.make_async_copy(block_out.at[:, cols], block_hbm.at[:, cols], out_sems.at[tile]).wait()


def backward_kernel(length_ref, normed, wide_grad, params, grad_hat, means, mean_one, mean_two):
    tiles, rows = grad_hat.shape[:2]
    live_rows = live_at(length_ref, rows, 0, rows)
    mean_one[...] = jnp.zeros_like(mean_one)
    mean_two[...] = jnp.zeros_like(mean_two)

    def one_tile(tile, carry):
        grad = jnp.zeros((rows, LANES), jnp.float32)
        for rest, offsets in enumerate(by_residue(1, TAPS)):
            shifted = wide_grad[tile, rest : rest + rows + 24]
            for offset in offsets:
                at = offset - rest
                tap = TAPS - offset
                grad += params[tile, tap : tap + 1] * shifted[at : at + rows]
        grad = live_rows * grad
        grad_hat[tile] = grad
        mean_one[...] += grad
        mean_two[...] += grad * normed[tile, WIDE : WIDE + rows]
        return carry

    lax.fori_loop(0, tiles, one_tile, 0, unroll=2)
    for index, total in enumerate((mean_one, mean_two)):
        mean = jnp.sum(total[...], axis=1, keepdims=True) * (1.0 / (tiles * LANES))
        means[index] = jnp.broadcast_to(mean, (rows, LANES))


def hidden_grad_kernel(cotan_ref, normed, inv_rows, grad_hat, means, grad_hbm, hidden_grad, out_sems):
    tiles, rows = grad_hat.shape[:2]
    copies = []
    for tile in range(tiles):
        cols = slice(tile * LANES, (tile + 1) * LANES)
        inner = grad_hat[tile] - means[0] - normed[tile, WIDE : WIDE + rows] * means[1]
        hidden_grad[:, cols] = (
            cotan_ref[:, cols].astype(jnp.float32) + inner * inv_rows[...]
        ).astype(hidden_grad.dtype)
        copies.append(
            pltpu.make_async_copy(hidden_grad.at[:, cols], grad_hbm.at[:, cols], out_sems.at[tile])
        )
        copies[-1].start()
    for copy in copies:
        copy.wait()


def finish_kernel(factor, mine, one, two, three, params, kernel_out, bias_out, gain_out, terms):
    place = lax.axis_index("ctx")
    for step, source in enumerate((mine, one, two, three)):
        terms[place ^ step] = source[...].astype(jnp.float32)
    total = (((terms[0] + terms[1]) + terms[2]) + terms[3]) * factor
    kernel_out[...] = total[:TAPS] * params[TAPS + 1 : TAPS + 2]
    bias_out[...] = total[TAPS]
    gain_out[...] = jnp.sum(total[:TAPS] * params[:TAPS], axis=0)


def fast_shards(
    query_in,
    key_in,
    value_in,
    utt_lengths,
    frames_in,
    out_weight,
    conv_kernel,
    conv_bias,
    ln_gain,
    cotangent,
):
    count = lax.axis_size("ctx")
    rows, width = query_in.shape[1], query_in.shape[2]
    features, half = frames_in.shape[2], out_weight.shape[1]
    place = lax.axis_index("ctx")
    vmem = pl.BlockSpec(memory_space=pltpu.VMEM)
    smem = pl.BlockSpec(memory_space=pltpu.SMEM)
    hbm = pl.BlockSpec(memory_space=pltpu.HBM)
    swap = [(0, 1), (1, 0)]

    ends = (features // SHARE) * (WIDE + NEAR)
    sent = [
        (3 * rows + ends, SHARE),
        *[(3 * rows, LANES)] * (len(PIECES) - 1),
        (WIDE + NEAR, features),
        (width // 2 + 2 * PARAM_ROWS, half),
    ]
    *pieces, edge, w_sent = pl.pallas_call(
        pack_kernel,
        name="pack",
        out_shape=[jax.ShapeDtypeStruct(shape, jnp.bfloat16) for shape in sent],
        in_specs=[hbm] * 9,
        out_specs=[vmem] * len(sent),
        scratch_shapes=[
            pltpu.VMEM((3, rows, width), jnp.bfloat16),
            pltpu.VMEM((2, WIDE + NEAR, features), jnp.bfloat16),
            pltpu.VMEM((TAPS, half), jnp.float32),
            pltpu.VMEM((half,), jnp.float32),
            pltpu.VMEM((half,), jnp.float32),
            pltpu.SemaphoreType.DMA((32,)),
        ],
        compiler_params=pltpu.CompilerParams(vmem_limit_bytes=32 << 20),
    )(
        *(
            pltpu.with_memory_space_constraint(one, pltpu.HBM)
            for one in (
                query_in,
                key_in,
                value_in,
                frames_in,
                cotangent,
                out_weight,
                conv_kernel,
                conv_bias,
                ln_gain,
            )
        )
    )
    parts = [
        lax.ppermute(one, "ctx", facing(count, step)) for one, (step, _) in zip(pieces, PIECES)
    ]
    edge = lax.ppermute(edge, "ctx", [(1, 2), (2, 1)])
    w_near = lax.ppermute(w_sent, "fsdp", swap)

    attended = []
    for chunk in range(CHUNKS):
        ready = [parts[0], *parts[2 * chunk + 1 : 2 * chunk + 3]]
        before = []
        if chunk:
            before = attended
            ready, edge = lax.optimization_barrier((ready, edge))
        attended = pl.pallas_call(
            functools.partial(attend_kernel, chunk),
            name="attend",
            out_shape=[
                jax.ShapeDtypeStruct((rows + 2 * WIDE, (chunk + 1) * LANES), jnp.bfloat16)
            ]
            * count,
            in_specs=[smem] + [hbm] * 3 + [vmem] * (3 + len(before)),
            out_specs=[vmem] * count,
            scratch_shapes=[pltpu.VMEM((count * rows, LANES), jnp.bfloat16)] * 3
            + [pltpu.VMEM((count * rows + 2 * WIDE, LANES), jnp.bfloat16)]
            + [pltpu.SemaphoreType.DMA((3,))],
            compiler_params=pltpu.CompilerParams(vmem_limit_bytes=40 << 20),
            cost_estimate=pl.CostEstimate(flops=1, bytes_accessed=1, transcendentals=0),
        )(utt_lengths, query_in, key_in, value_in, *ready, *before)
    own, *replies = [
        reply if step == 0 else lax.ppermute(reply, "ctx", facing(count, step))
        for step, reply in enumerate(attended)
    ]
    _, w_near = lax.optimization_barrier((attended, w_near))
    w_far = lax.ppermute(w_near, "dp", swap)
    frames, cotan = frames_in[0], cotangent[0]

    ext, near = rows + 2 * WIDE, rows + 2 * NEAR
    tiles = features // LANES
    base, cotan_live, params, par_mine = pl.pallas_call(
        prepare_kernel,
        name="prepare",
        out_shape=[
            jax.ShapeDtypeStruct((tiles, ext, LANES), jnp.float32),
            jax.ShapeDtypeStruct((tiles, near, LANES), jnp.float32),
            jax.ShapeDtypeStruct((tiles, PARAM_ROWS, LANES), jnp.float32),
            jax.ShapeDtypeStruct((PARAM_ROWS, half), jnp.float32),
        ],
        in_specs=[smem] + [vmem] * 11,
        out_specs=[vmem] * 4,
        scratch_shapes=[pltpu.VMEM((2, WIDE + NEAR, features), jnp.bfloat16)],
        compiler_params=pltpu.CompilerParams(vmem_limit_bytes=32 << 20),
        cost_estimate=pl.CostEstimate(
            flops=2 * ext * SHARE * features, bytes_accessed=8 * rows * features, transcendentals=0
        ),
    )(
        utt_lengths,
        own,
        frames,
        cotan,
        parts[0],
        edge,
        out_weight,
        w_near,
        w_far,
        conv_kernel,
        conv_bias,
        ln_gain,
    )
    block_out, normed, wide_grad, inv_rows, sums_own, sums_other = pl.pallas_call(
        module_kernel,
        name="conv_module",
        out_shape=[
            jax.ShapeDtypeStruct((rows, features), jnp.bfloat16),
            jax.ShapeDtypeStruct((tiles, ext + 8, LANES), jnp.float32),
            jax.ShapeDtypeStruct((tiles, near + 8, LANES), jnp.float32),
            jax.ShapeDtypeStruct((rows, LANES), jnp.float32),
            jax.ShapeDtypeStruct((TAPS + 1, half), jnp.bfloat16),
            jax.ShapeDtypeStruct((TAPS + 1, half), jnp.bfloat16),
        ],
        in_specs=[smem] + [vmem] * 9,
        out_specs=[hbm] + [vmem] * 5,
        scratch_shapes=[
            pltpu.VMEM((tiles, TAPS + 1, LANES), jnp.float32),
            pltpu.VMEM((TAPS + 1, 8, LANES), jnp.float32),
            pltpu.VMEM((rows, features), jnp.bfloat16),
            pltpu.SemaphoreType.DMA((tiles,)),
        ],
        compiler_params=pltpu.CompilerParams(vmem_limit_bytes=32 << 20),
        cost_estimate=pl.CostEstimate(
            flops=2 * ext * width * features + 4 * TAPS * rows * features,
            bytes_accessed=2 * width * features + 12 * rows * features,
            transcendentals=near * features,
        ),
    )(
        utt_lengths,
        *replies,
        base,
        cotan_live,
        params,
        out_weight,
        w_near,
        w_far,
    )

    pairs = [
        lax.ppermute(sums_other, "fsdp", swap),
        lax.ppermute(sums_other, ("fsdp", "dp"), [(0, 3), (3, 0), (1, 2), (2, 1)]),
        lax.ppermute(sums_own, "dp", swap),
    ]
    grad_hat, means = pl.pallas_call(
        backward_kernel,
        name="conv_backward",
        out_shape=[
            jax.ShapeDtypeStruct((tiles, rows, LANES), jnp.float32),
            jax.ShapeDtypeStruct((2, rows, LANES), jnp.float32),
        ],
        in_specs=[smem] + [vmem] * 3,
        out_specs=[vmem] * 2,
        scratch_shapes=[pltpu.VMEM((rows, LANES), jnp.float32)] * 2,
        compiler_params=pltpu.CompilerParams(vmem_limit_bytes=32 << 20),
        cost_estimate=pl.CostEstimate(
            flops=2 * TAPS * rows * features,
            bytes_accessed=12 * rows * features,
            transcendentals=0,
        ),
    )(utt_lengths, normed, wide_grad, params)
    pairs, grad_hat = lax.optimization_barrier((pairs, grad_hat))
    across_x, diagonal, sibling = (one.astype(jnp.float32) for one in pairs)
    found = (sums_own.astype(jnp.float32) + sibling) + (across_x + diagonal)
    found = found.astype(jnp.bfloat16)
    arrived = [lax.ppermute(found, "ctx", facing(count, step)) for step in range(1, count)]
    hidden_grad = pl.pallas_call(
        hidden_grad_kernel,
        name="hidden_grad",
        out_shape=jax.ShapeDtypeStruct((rows, features), jnp.bfloat16),
        in_specs=[vmem] * 5,
        out_specs=hbm,
        scratch_shapes=[
            pltpu.VMEM((rows, features), jnp.bfloat16),
            pltpu.SemaphoreType.DMA((tiles,)),
        ],
        compiler_params=pltpu.CompilerParams(vmem_limit_bytes=32 << 20),
        cost_estimate=pl.CostEstimate(
            flops=6 * rows * features, bytes_accessed=12 * rows * features, transcendentals=0
        ),
    )(cotan, normed, inv_rows, grad_hat, means)
    arrived, hidden_grad = lax.optimization_barrier((arrived, hidden_grad))
    factor = 1.0 / math.sqrt(lax.axis_size("fsdp") * lax.axis_size("dp") * rows * count)
    grad_kernel, grad_bias, grad_gain = pl.pallas_call(
        functools.partial(finish_kernel, factor),
        name="finish",
        out_shape=[
            jax.ShapeDtypeStruct((TAPS, half), jnp.float32),
            jax.ShapeDtypeStruct((half,), jnp.float32),
            jax.ShapeDtypeStruct((half,), jnp.float32),
        ],
        in_specs=[vmem] * 5,
        out_specs=[vmem] * 3,
        scratch_shapes=[pltpu.VMEM((count, TAPS + 1, half), jnp.float32)],
        compiler_params=pltpu.CompilerParams(vmem_limit_bytes=32 << 20),
    )(found, *arrived, par_mine)
    return (block_out[None], hidden_grad[None], grad_kernel, grad_bias, grad_gain)


def solution(mesh):
    in_specs = (
        P(("groups", "fsdp", "dp"), "ctx", None),
        P(("groups", "fsdp", "dp"), "ctx", None),
        P(("groups", "fsdp", "dp"), "ctx", None),
        P(("groups", "fsdp", "dp")),
        P(("groups", "fsdp", "dp"), "ctx", None),
        P(None, "fsdp"),
        P(None, "fsdp"),
        P("fsdp"),
        P("fsdp"),
        P(("groups", "fsdp", "dp"), "ctx", None),
    )
    out_specs = (
        P(("groups", "fsdp", "dp"), "ctx", None),
        P(("groups", "fsdp", "dp"), "ctx", None),
        P("groups", "fsdp"),
        P(("groups", "fsdp")),
        P(("groups", "fsdp")),
    )

    def shards(*blocks):
        run = fast_shards if fits_fast(mesh, blocks) else general_shards
        return run(*blocks)

    return jax.shard_map(shards, mesh=mesh, in_specs=in_specs, out_specs=out_specs, check_vma=False)
```
